32 devices in a mesh: runs: 2 (over x), modes: 16 (over z, y, core).
Axes of the slice: x: 2, y: 2, z: 4, core: 2. Of those that a mesh axis runs over, the one named last changes fastest.
Arguments:
- amplitudes: float32 [8192, 2, 5, 512], P(('runs', 'modes')), parts along dimension 0, may hold values from -6 to 6
- mode_table: int32 [4096, 2], replicated, may hold values from 0 to 127, as said below
- slab_map: int32 [8], replicated, may hold values from 0 to 7, each once
- base_flow: float32 [1024], P('runs'), parts along dimension 0, may hold values from 0 to 1.5
- base_coupling: float32 [50, 512], P('runs'), parts along dimension 0, may hold values from -0.36 to 0.36
- slab_inverse: float32 [8, 64, 64], replicated
- wall_operator: float32 [64, 64], replicated, may hold values from -0.75 to 0.75
Outputs:
- marched: float32 [8192, 2, 5, 512], P(('runs', 'modes')), parts along dimension 0
The draws below stay inside these ranges and needn't reach their ends.
There are 2 independent parts, one for each index of `runs`. The reference program is written for one: setup_inputs(seed, part) draws one part's arguments, and reference() takes and returns one part's arrays. A program takes and returns all parts, laid end to end along the dimension named above; an argument that names none is the same for every part. Nothing has to cross between parts.
Inputs may be any that keep to these rules, and one draw needn't show every extreme that they name: `mode_table`: every cell of the 32 x 128 grid is named by exactly one mode; column 0 lies in 0 to 31. `slab_map`: each subdomain has its own slot.
All inputs are finite; a program needn't handle non-finite values.
Results may differ from the reference program's by a relative error of at most 0.0003.
Values sent between devices are 32-bit elements; how exact they have to be, the bound alone decides.
No kernel may reach another device: no remote copies, remote signals or barrier semaphores. Data moves between devices by JAX's collectives and lax.ppermute only.
A program may use at most 192 MiB of HBM per device.

```python
import math
import jax
import jax.numpy as jnp
from jax import lax

M = 4096
NB = 128
NSUB = 8
P_SIZE = 64
SWEEPS = 3
STATIONS = 1
NW = 32
Y = 512


def draw_mode_table(key, part):
    order = jax.random.permutation(key, M).astype(jnp.int32)
    return jnp.stack([order // NB, order % NB], 1).astype(jnp.int32)


def draw_slab_inverse(key, part):
    first_key, second_key = jax.random.split(jax.random.fold_in(key, 7))
    diagonal = jax.random.uniform(first_key, (NSUB, P_SIZE), jnp.float32, 0.5, 0.9)
    spread = jax.random.normal(second_key, (NSUB, P_SIZE, P_SIZE), jnp.float32) * (0.15 / math.sqrt(P_SIZE))
    return spread + diagonal[:, :, None] * jnp.eye(P_SIZE, dtype=jnp.float32)[None]


def block_scale(key, dims, cuts, least, top_value):
    level = 1.0
    for dim, blocks in cuts:
        heights = jax.random.uniform(jax.random.fold_in(jax.random.fold_in(key, 6), dim), (blocks,), jnp.float32, least / len(cuts), top_value / len(cuts))
        level = level * jnp.repeat(jnp.exp(heights), dims[dim] // blocks).reshape((-1,) + (1,) * (len(dims) - 1 - dim))
    return level


def gaussian(stream_key, shape, deviation, reach, shards=(), kind=jnp.bfloat16):
    drawn = deviation * jax.random.normal(stream_key, shape, jnp.float32)
    if shards:
        drawn = drawn * block_scale(stream_key, shape, shards, -0.22, 0.18)
    return jnp.clip(drawn, -reach, reach).astype(kind)


def setup_inputs(seed: int = 0, part: int = 0) -> dict:
    key_list = jax.random.split(jax.random.key(seed), 8)
    own_keys = jax.random.split(jax.random.fold_in(key_list[7], part), 8)
    return {
        "amplitudes": gaussian(own_keys[0], (M, 2, 5, Y), 1.0, 6.0, ((0, 16),), jnp.float32),
        "mode_table": draw_mode_table(jax.random.fold_in(key_list[7], 71), part),
        "slab_map": jax.random.permutation(key_list[2], NSUB).astype(jnp.int32),
        "base_flow": jnp.clip(jax.random.uniform(own_keys[3], (Y,), jnp.float32, 0.0, 1.5), 0.0, 1.5),
        "base_coupling": gaussian(own_keys[4], (25, Y), 0.06, 0.36, (), jnp.float32),
        "slab_inverse": draw_slab_inverse(jax.random.fold_in(key_list[7], 71), part),
        "wall_operator": gaussian(key_list[6], (P_SIZE, P_SIZE), P_SIZE ** -0.5, 0.75, (), jnp.float32),
    }


precise = lax.Precision.HIGHEST
omega_step = 0.01
phase_gain = 0.2
march_step = 0.2
coupling = 0.3

def twiddle(length):
    counter = jnp.arange(length, dtype=jnp.int32)
    product = counter[:, None] * counter[None, :] % length
    angles = product.astype(jnp.float32) * (2.0 * math.pi / length)
    return (jnp.cos(angles), jnp.sin(angles))

def mode_tables(mode_table):
    omega_index = mode_table[:, 0]
    beta_index = mode_table[:, 1]
    signed = jnp.where(beta_index >= NB // 2, beta_index - NB, beta_index)
    wavenum = 2.0 * signed.astype(jnp.float32) / NB
    frequency = omega_step * omega_index.astype(jnp.float32)
    grid_pos = (omega_index * NB + beta_index).astype(jnp.int32)
    mode_at = jnp.zeros((M,), jnp.int32).at[grid_pos].set(jnp.arange(M, dtype=jnp.int32))
    return (wavenum, frequency, grid_pos, mode_at)

def synthesize(real_part, imag_part, tables, factor):
    cos_omega, sin_omega, cos_beta, sin_beta = tables
    mixed_re = jnp.einsum('...wb,bz->...wz', real_part, cos_beta, precision=precise) - jnp.einsum('...wb,bz->...wz', imag_part, sin_beta, precision=precise)
    mixed_im = jnp.einsum('...wb,bz->...wz', real_part, sin_beta, precision=precise) + jnp.einsum('...wb,bz->...wz', imag_part, cos_beta, precision=precise)
    physical = jnp.einsum('...wz,wt->...tz', mixed_re, cos_omega, precision=precise) - jnp.einsum('...wz,wt->...tz', mixed_im, sin_omega, precision=precise)
    return physical * factor

def analyze(physical, tables, factor):
    cos_omega, sin_omega, cos_beta, sin_beta = tables
    half_re = jnp.einsum('...tz,zb->...tb', physical, cos_beta, precision=precise)
    half_im = -jnp.einsum('...tz,zb->...tb', physical, sin_beta, precision=precise)
    coef_re = jnp.einsum('...tb,tw->...wb', half_re, cos_omega, precision=precise) + jnp.einsum('...tb,tw->...wb', half_im, sin_omega, precision=precise)
    coef_im = jnp.einsum('...tb,tw->...wb', half_im, cos_omega, precision=precise) - jnp.einsum('...tb,tw->...wb', half_re, sin_omega, precision=precise)
    return (coef_re * factor, coef_im * factor)

def forcing(normal_vel, spanwise_vel, wall_grad, span_grad, tables, factor):
    vel_v = synthesize(normal_vel[0], normal_vel[1], tables, factor)
    vel_w = synthesize(spanwise_vel[0], spanwise_vel[1], tables, factor)
    grad_y = synthesize(wall_grad[0], wall_grad[1], tables, factor)
    grad_z = synthesize(span_grad[0], span_grad[1], tables, factor)
    product = -(vel_v[None] * grad_y + vel_w[None] * grad_z)
    return analyze(product, tables, factor)

def wall_derivative(values, wall_operator):
    slab_width = wall_operator.shape[0]
    slab_count = values.shape[3] // slab_width
    blocks = values.reshape(values.shape[:3] + (slab_count, slab_width))
    return jnp.einsum('ij,abcsj->abcsi', wall_operator, blocks, precision=precise).reshape(values.shape)

def interface(iterate, slab_map, slab_count, slab_width):
    blocks = iterate.reshape(iterate.shape[:3] + (slab_count, slab_width))
    ordered = jnp.take(blocks, slab_map, axis=3)
    edge_zero = jnp.zeros(blocks.shape[:3] + (1,), jnp.float32)
    lower_rim = jnp.concatenate([edge_zero, ordered[..., :-1, slab_width - 1]], 3)
    upper_rim = jnp.concatenate([ordered[..., 1:, 0], edge_zero], 3)
    middle = jnp.zeros(blocks.shape[:4] + (slab_width - 2,), jnp.float32)
    joined = jnp.concatenate([lower_rim[..., None], middle, upper_rim[..., None]], 4)
    inverse = jnp.zeros((slab_count,), jnp.int32).at[slab_map].set(jnp.arange(slab_count, dtype=jnp.int32))
    return jnp.take(joined, inverse, axis=3).reshape(iterate.shape)

def relaxation(iterate, right_side, wave_local, freq_local, crossflow, base_coupling, slab_inverse, slab_map):
    points = iterate.shape[3]
    slab_count = slab_inverse.shape[0]
    slab_width = slab_inverse.shape[1]
    matrix = base_coupling.reshape(5, 5, points)
    coupled = jnp.einsum('kjy,acjy->acky', matrix, iterate, precision=precise)
    rotation = phase_gain * wave_local[:, None] * crossflow[None, :] - freq_local[:, None]
    applied = jnp.stack([coupled[:, 0] - rotation[:, None, :] * iterate[:, 1], coupled[:, 1] + rotation[:, None, :] * iterate[:, 0]], 1)
    residual_in = right_side - applied + coupling * interface(iterate, slab_map, slab_count, slab_width)
    blocks = residual_in.reshape(iterate.shape[:3] + (slab_count, slab_width))
    return jnp.einsum('sij,acvsj->acvsi', slab_inverse, blocks, precision=precise).reshape(iterate.shape)

def reference(amplitudes, mode_table, slab_map, base_flow, base_coupling, slab_inverse, wall_operator):
    wavenum, frequency, grid_pos, mode_at = mode_tables(mode_table)
    tables = twiddle(NW) + twiddle(NB)
    factor = 1.0 / math.sqrt(M)
    current = amplitudes
    for station in range(STATIONS):
        gradient = wall_derivative(current, wall_operator)
        span = jnp.stack([-wavenum[:, None, None] * current[:, 1], wavenum[:, None, None] * current[:, 0]], 1)
        fields = jnp.concatenate([current[:, :, 2:4], gradient, span], 2)

        def block_forcing(block_index):
            piece = lax.dynamic_slice_in_dim(fields, (block_index * P_SIZE).astype(jnp.int32), P_SIZE, 3)
            gridded = jnp.transpose(piece, (1, 2, 3, 0))[..., mode_at].reshape(2, 12, P_SIZE, NW, NB)
            coef_re, coef_im = forcing(gridded[:, 0], gridded[:, 1], gridded[:, 2:7], gridded[:, 7:12], tables, factor)
            return jnp.stack([coef_re, coef_im], 0).reshape(2, 5, P_SIZE, M)[..., grid_pos]
        pieces = lax.map(block_forcing, jnp.arange(NSUB, dtype=jnp.int32))
        nonlinear = jnp.transpose(pieces, (4, 1, 2, 0, 3)).reshape(M, 2, 5, NSUB * P_SIZE)
        crossflow = base_flow + current[mode_at[0], 0, 3]
        right_side = current + march_step * nonlinear
        iterate = current
        for sweep_index in range(SWEEPS):
            iterate = relaxation(iterate, right_side, wavenum, frequency, crossflow, base_coupling, slab_inverse, slab_map)
        current = iterate
    return current
```

```python
import functools
import math

import jax
import jax.numpy as jnp
import numpy as np
from jax import lax
from jax.experimental import pallas as pl
from jax.experimental.pallas import tpu as pltpu
from jax.sharding import PartitionSpec as P

M = 4096
NB = 128
SWEEPS = 3
NW = 32


precise = lax.Precision.HIGHEST
omega_step = 0.01
phase_gain = 0.2
march_step = 0.2
coupling = 0.3


def twiddle(length):
    counter = jnp.arange(length, dtype=jnp.int32)
    product = counter[:, None] * counter[None, :] % length
    angles = product.astype(jnp.float32) * (2.0 * math.pi / length)
    return (jnp.cos(angles), jnp.sin(angles))


def mode_tables(mode_table):
    omega_index = mode_table[:, 0]
    beta_index = mode_table[:, 1]
    signed = jnp.where(beta_index >= NB // 2, beta_index - NB, beta_index)
    wavenum = 2.0 * signed.astype(jnp.float32) / NB
    frequency = omega_step * omega_index.astype(jnp.float32)
    grid_pos = omega_index * NB + beta_index
    mode_at = jnp.zeros((M,), jnp.int32).at[grid_pos].set(jnp.arange(M, dtype=jnp.int32))
    return (wavenum, frequency, grid_pos, mode_at)


def synthesize(real_part, imag_part, tables, factor):
    cos_omega, sin_omega, cos_beta, sin_beta = tables
    mixed_re = jnp.einsum("...wb,bz->...wz", real_part, cos_beta, precision=precise) - jnp.einsum(
        "...wb,bz->...wz", imag_part, sin_beta, precision=precise
    )
    mixed_im = jnp.einsum("...wb,bz->...wz", real_part, sin_beta, precision=precise) + jnp.einsum(
        "...wb,bz->...wz", imag_part, cos_beta, precision=precise
    )
    physical = jnp.einsum("...wz,wt->...tz", mixed_re, cos_omega, precision=precise) - jnp.einsum(
        "...wz,wt->...tz", mixed_im, sin_omega, precision=precise
    )
    return physical * factor


def analyze(physical, tables, factor):
    cos_omega, sin_omega, cos_beta, sin_beta = tables
    half_re = jnp.einsum("...tz,zb->...tb", physical, cos_beta, precision=precise)
    half_im = -jnp.einsum("...tz,zb->...tb", physical, sin_beta, precision=precise)
    coef_re = jnp.einsum("...tb,tw->...wb", half_re, cos_omega, precision=precise) + jnp.einsum(
        "...tb,tw->...wb", half_im, sin_omega, precision=precise
    )
    coef_im = jnp.einsum("...tb,tw->...wb", half_im, cos_omega, precision=precise) - jnp.einsum(
        "...tb,tw->...wb", half_re, sin_omega, precision=precise
    )
    return (coef_re * factor, coef_im * factor)


def forcing(normal_vel, spanwise_vel, wall_grad, span_grad, tables, factor):
    vel_v = synthesize(normal_vel[0], normal_vel[1], tables, factor)
    vel_w = synthesize(spanwise_vel[0], spanwise_vel[1], tables, factor)
    grad_y = synthesize(wall_grad[0], wall_grad[1], tables, factor)
    grad_z = synthesize(span_grad[0], span_grad[1], tables, factor)
    product = -(vel_v[None] * grad_y + vel_w[None] * grad_z)
    return analyze(product, tables, factor)


def wall_derivative(values, wall_operator):
    slab_width = wall_operator.shape[0]
    slab_count = values.shape[3] // slab_width
    blocks = values.reshape(values.shape[:3] + (slab_count, slab_width))
    return jnp.einsum("ij,abcsj->abcsi", wall_operator, blocks, precision=precise).reshape(
        values.shape
    )


def interface_table(slab_map, slab_count, slab_width):
    inverse = (
        jnp.zeros((slab_count,), jnp.int32)
        .at[slab_map]
        .set(jnp.arange(slab_count, dtype=jnp.int32))
    )
    position = jnp.arange(slab_count * slab_width, dtype=jnp.int32)
    slot_of = position // slab_width
    within = position % slab_width
    domain = inverse[slot_of]
    below = slab_map[jnp.maximum(domain - 1, 0)] * slab_width + (slab_width - 1)
    above = slab_map[jnp.minimum(domain + 1, slab_count - 1)] * slab_width
    lower_ok = (within == 0) & (domain > 0)
    upper_ok = (within == slab_width - 1) & (domain < slab_count - 1)
    source = jnp.where(lower_ok, below, jnp.where(upper_ok, above, 0))
    weight = (lower_ok | upper_ok).astype(jnp.float32)
    return (source, weight)


def relaxation(iterate, right_side, rotation, matrix, slab_inverse, source, weight):
    slab_count = slab_inverse.shape[0]
    slab_width = slab_inverse.shape[1]
    coupled = jnp.einsum("kjy,acjy->acky", matrix, iterate, precision=precise)
    applied = jnp.stack(
        [
            coupled[:, 0] - rotation[:, None, :] * iterate[:, 1],
            coupled[:, 1] + rotation[:, None, :] * iterate[:, 0],
        ],
        1,
    )
    rims = jnp.take(iterate, source, axis=3) * weight
    residual_in = right_side - applied + coupling * rims
    blocks = residual_in.reshape(iterate.shape[:3] + (slab_count, slab_width))
    return jnp.einsum("sij,acvsj->acvsi", slab_inverse, blocks, precision=precise).reshape(
        iterate.shape
    )


def local(amplitudes, mode_table, slab_map, base_flow, base_coupling, slab_inverse, wall_operator):
    local_modes = amplitudes.shape[0]
    wall_points = amplitudes.shape[3]
    groups = lax.axis_size("modes")
    point_share = wall_points // groups
    wavenum, frequency, grid_pos, mode_at = mode_tables(mode_table)
    first_mode = lax.axis_index("modes") * local_modes
    wave_local = lax.dynamic_slice_in_dim(wavenum, first_mode, local_modes)
    freq_local = lax.dynamic_slice_in_dim(frequency, first_mode, local_modes)
    tables = twiddle(NW) + twiddle(NB)
    factor = 1.0 / math.sqrt(M)
    source, weight = interface_table(slab_map, slab_inverse.shape[0], slab_inverse.shape[1])
    matrix = base_coupling.reshape(5, 5, wall_points)
    gradient = wall_derivative(amplitudes, wall_operator)
    span = jnp.stack(
        [
            -wave_local[:, None, None] * amplitudes[:, 1],
            wave_local[:, None, None] * amplitudes[:, 0],
        ],
        1,
    )
    fields = jnp.concatenate([amplitudes[:, :, 2:4], gradient, span], 2)
    field_count = fields.shape[2]
    channels = 2 * field_count
    outgoing = jnp.transpose(
        fields.reshape(local_modes, channels, groups, point_share), (1, 2, 3, 0)
    ).reshape(channels, groups, point_share * local_modes)
    incoming = lax.all_to_all(outgoing, "modes", split_axis=1, concat_axis=1, tiled=True)
    by_mode = jnp.transpose(
        incoming.reshape(channels, groups, point_share, local_modes), (0, 2, 1, 3)
    ).reshape(channels, point_share, M)
    gridded = by_mode[..., mode_at].reshape(2, field_count, point_share, NW, NB)
    normal_vel = gridded[:, 0]
    spanwise_vel = gridded[:, 1]
    wall_grad = gridded[:, 2:7]
    span_grad = gridded[:, 7:12]
    mean_crossflow = lax.all_gather(spanwise_vel[0, :, 0, 0], "modes", axis=0, tiled=True)
    coef_re, coef_im = forcing(normal_vel, spanwise_vel, wall_grad, span_grad, tables, factor)
    packed = jnp.stack([coef_re, coef_im], 0).reshape(10, point_share, M)[..., grid_pos]
    sendback = jnp.transpose(
        packed.reshape(10, point_share, groups, local_modes), (0, 2, 1, 3)
    ).reshape(10, groups, point_share * local_modes)
    returned = lax.all_to_all(sendback, "modes", split_axis=1, concat_axis=1, tiled=True)
    nonlinear = jnp.transpose(
        returned.reshape(10, groups, point_share, local_modes), (3, 0, 1, 2)
    ).reshape(local_modes, 2, 5, wall_points)
    crossflow = base_flow + mean_crossflow
    rotation = phase_gain * wave_local[:, None] * crossflow[None, :] - freq_local[:, None]
    right_side = amplitudes + march_step * nonlinear
    iterate = amplitudes
    for sweep_index in range(SWEEPS):
        iterate = relaxation(iterate, right_side, rotation, matrix, slab_inverse, source, weight)
    return iterate


LANES = 128
SHARE = 32
SLAB = 64
HALF = NW // 2
TIMES = HALF + 1
BLOCKS = LANES // SHARE
STRIPES = 4
PARTS = 10
TILE = 32
VMEM_LIMIT = 60 * 1024 * 1024


def roll(x, shift):
    return pltpu.roll(x, shift % LANES, x.ndim - 1)


def lane_index(shape):
    return lax.broadcasted_iota(jnp.int32, shape, len(shape) - 1)


def lane_masks(shape):
    lane = lane_index(shape)
    return (lane < 64, (lane & 32) == 0)


def real_sign(shape):
    return jnp.where(lane_index(shape) < 64, 1.0, -1.0).astype(jnp.float32)


def block_transpose(rows, low, even):
    r0, r1, r2, r3 = rows
    t0 = jnp.where(low, r0, roll(r2, 64))
    t2 = jnp.where(low, roll(r0, 64), r2)
    t1 = jnp.where(low, r1, roll(r3, 64))
    t3 = jnp.where(low, roll(r1, 64), r3)
    return (
        jnp.where(even, t0, roll(t1, 32)),
        jnp.where(even, roll(t0, 96), t1),
        jnp.where(even, t2, roll(t3, 32)),
        jnp.where(even, roll(t2, 96), t3),
    )


def split(x):
    high = x.astype(jnp.bfloat16)
    return high, (x - high.astype(jnp.float32)).astype(jnp.bfloat16)


def dot(a, b):
    return jnp.dot(a, b, preferred_element_type=jnp.float32)


def cosine_sine(inputs, length, table, sign, real):
    if length == 4:
        first, middle, last = inputs
        middle_re = middle * real
        total = first + last
        return [total + middle_re, (first - last) + (middle - middle_re), total - middle_re]
    step = NW // length
    quarter = length // 4
    even = cosine_sine(inputs[0::2], length // 2, table, sign, real)
    odd_inputs = [(a, inputs[a]) for a in range(1, length // 2, 2)]
    odd = []
    for t in range(quarter + 1):
        if t == 0:
            total = odd_inputs[0][1]
            for _, value in odd_inputs[1:]:
                total = total + value
            odd.append(total * real)
        elif t == quarter:
            total = odd_inputs[0][1]
            for a, value in odd_inputs[1:]:
                total = total + value if a % 4 == 1 else total - value
            odd.append(total - total * real)
        else:
            total = None
            for a, value in odd_inputs:
                term = table(a * t * step % NW) * value
                total = term if total is None else total + term
            odd.append(total)
    out = [None] * (length // 2 + 1)
    for t in range(quarter + 1):
        out[t] = even[t] + odd[t]
        out[length // 2 - t] = sign * (even[t] - odd[t])
    out[quarter] = even[quarter] + odd[quarter]
    return out


def pack_rows(a_ref, o_ref, base, first, second, second_base, count, row, low, even):
    for stripe in range(STRIPES):
        rows = []
        for part in range(2):
            for variable, start in ((first, base), (second, second_base)):
                offset = variable * 2 * STRIPES + stripe * 2 + part
                rows.append(a_ref[pl.ds(start * 2 * STRIPES * 5 + offset, count, stride=2 * STRIPES * 5), :])
        for block, value in enumerate(block_transpose(rows, low, even)):
            o_ref[stripe * BLOCKS + block, pl.ds(row, count), :] = value


def pack_velocity(a_ref, o_ref):
    low, even = lane_masks((TILE, LANES))

    def body(i, carry):
        base = pl.multiple_of(i * TILE, TILE)
        pack_rows(a_ref, o_ref, base, 2, 3, base, TILE, base, low, even)
        return carry

    lax.fori_loop(0, o_ref.shape[1] // TILE, body, 0)


def pack_others(a_ref, o_ref):
    low, even = lane_masks((TILE, LANES))
    modes = o_ref.shape[1] // 3 * 2

    def body(i, carry):
        base = pl.multiple_of(i * TILE, TILE)
        pack_rows(a_ref, o_ref, base, 0, 1, base, TILE, base, low, even)
        return carry

    def last_body(i, carry):
        base = pl.multiple_of(i * TILE, TILE)
        pack_rows(a_ref, o_ref, base, 4, 4, base + modes // 2, TILE, modes + base, low, even)
        return carry

    lax.fori_loop(0, modes // TILE, body, 0)
    lax.fori_loop(0, modes // 2 // TILE, last_body, 0)


UNROLL = 16


def synthesis(with_mean, pos_ref, r_ref, w_ref, tab_ref, *refs):
    if with_mean:
        f_ref, g_ref, mean_ref, grid_ref, spec_ref = refs
        last_ref = None
        modes = r_ref.shape[1]
    else:
        f_ref, g_ref, grid_ref, spec_ref, last_ref = refs
        modes = r_ref.shape[1] // 3 * 2
    groups = r_ref.shape[0]
    sign = real_sign((8, LANES))
    real = jnp.where(lane_index((8, LANES)) < 64, 1.0, 0.0).astype(jnp.float32)
    wide_sign = real_sign((NB, LANES))

    def table(j):
        return tab_ref[j]

    def scatter(source):
        chunks = modes // UNROLL

        def body(i, carry):
            group = i // chunks
            start = (i % chunks) * UNROLL
            for j in range(UNROLL):
                cell = pos_ref[i * UNROLL + j]
                grid_ref[pl.ds(cell, 1), :] = source[group, pl.ds(start + j, 1), :]
            return carry

        lax.fori_loop(0, groups * chunks, body, 0)

    for pair in range(f_ref.shape[0]):
        if pair == 0:
            scatter(r_ref)
        else:

            def unpack(group, carry):
                rows = r_ref[group, pl.ds(modes, modes // 2), :]
                last_ref[group, pl.ds(0, modes // 2), :] = rows
                last_ref[group, pl.ds(modes // 2, modes // 2), :] = roll(rows, 96)
                return carry

            lax.fori_loop(0, groups, unpack, 0)
            scatter(last_ref)
        if with_mean:
            mean_ref[...] = grid_ref[pl.ds(0, 8), :]

        def beta(i, carry):
            columns = []
            for j in range(2):
                x = grid_ref[pl.ds(pl.multiple_of((2 * i + j) * NB, NB), NB), :]
                columns.append(jnp.concatenate([x, -wide_sign * roll(x, 64)], 0))
            high, low_part = split(jnp.concatenate(columns, 1))
            product = dot(w_ref[...], high)
            out = product[: 2 * NB] + product[2 * NB :] + dot(w_ref[pl.ds(0, 2 * NB), :], low_part)
            spec_ref[2 * i] = out[:, :LANES]
            spec_ref[2 * i + 1] = out[:, LANES:]
            return carry

        lax.fori_loop(0, NW // 2, beta, 0)

        def omega(out_ref, shift):
            def body(i, carry):
                rows = pl.ds(pl.multiple_of(i * 8, 8), 8)
                source = pl.ds(pl.multiple_of(shift + i * 8, 8), 8)
                coefs = [spec_ref[a, source, :] for a in range(NW)]
                inputs = [coefs[0] * real]
                for a in range(1, HALF):
                    inputs.append(coefs[a] + sign * coefs[NW - a])
                inputs.append(coefs[HALF] * real)
                for t, value in enumerate(cosine_sine(inputs, NW, table, sign, real)):
                    out_ref[pair, t, rows, :] = value - sign * roll(value, 64)
                return carry

            lax.fori_loop(0, NB // 8, body, 0)

        omega(f_ref, 0)
        omega(g_ref, NB)


def force_analysis(with_mean, pos_ref, vw_ref, f_ref, s_ref, g_ref, d_ref, w_ref, tab_ref, *refs):
    if with_mean:
        mean_ref, o_ref, k_ref, n_ref = refs
        last_ref = None
        modes = o_ref.shape[1] - 8
    else:
        o_ref, k_ref, n_ref, last_ref = refs
        modes = o_ref.shape[1] // 3 * 2
    groups = o_ref.shape[0]
    sign = real_sign((8, LANES))
    real = jnp.where(lane_index((8, LANES)) < 64, 1.0, 0.0).astype(jnp.float32)
    wide_sign = real_sign((NB, LANES))
    wide_real, even = lane_masks((NB, LANES))

    def table(j):
        return tab_ref[j]

    def gather(target):
        chunks = modes // UNROLL

        def body(i, carry):
            group = i // chunks
            start = (i % chunks) * UNROLL
            for j in range(UNROLL):
                cell = pos_ref[i * UNROLL + j]
                target[group, pl.ds(start + j, 1), :] = n_ref[pl.ds(cell, 1), :]
            return carry

        lax.fori_loop(0, groups * chunks, body, 0)

    for pair in range(f_ref.shape[0]):

        def product(t, carry):
            vw = vw_ref[0, t]
            v = jnp.where(even, vw, roll(vw, 32))
            w = jnp.where(even, roll(vw, 96), vw)
            high, low_part = split(jnp.concatenate([f_ref[pair, t], s_ref[pair, t]], 1))
            both = dot(high, d_ref[...])
            grad = both[:, :LANES] + both[:, LANES:] + dot(low_part, d_ref[:, :LANES])
            force = v * grad + w * g_ref[pair, t]
            folded = force + wide_sign * roll(force, 64)
            alone = jnp.logical_or(t == 0, t == HALF)
            k_ref[t] = jnp.where(alone, jnp.where(wide_real, force, 0.0), folded)
            return carry

        lax.fori_loop(0, TIMES, product, 0)

        def omega(i, carry):
            rows = pl.ds(pl.multiple_of(i * 8, 8), 8)
            inputs = [k_ref[t, rows, :] for t in range(TIMES)]
            for a, value in enumerate(cosine_sine(inputs, NW, table, sign, real)):
                k_ref[a, rows, :] = value
            return carry

        lax.fori_loop(0, NB // 8, omega, 0)

        def beta(frequencies, columns):
            high, low_part = split(columns)
            both = dot(w_ref[...], high)
            out = both[: 2 * NB] + both[2 * NB :] + dot(w_ref[pl.ds(0, 2 * NB), :], low_part)
            for j, a in enumerate(frequencies):
                cosine = out[:NB, j * LANES : (j + 1) * LANES]
                sine = roll(out[NB:, j * LANES : (j + 1) * LANES], 64)
                mirror = (NW - a) % NW
                n_ref[pl.ds(pl.multiple_of(mirror * NB, NB), NB), :] = wide_sign * cosine - sine
                n_ref[pl.ds(pl.multiple_of(a * NB, NB), NB), :] = cosine + wide_sign * sine

        def beta_pair(i, carry):
            beta((2 * i, 2 * i + 1), jnp.concatenate([k_ref[2 * i], k_ref[2 * i + 1]], 1))
            return carry

        lax.fori_loop(0, HALF // 2, beta_pair, 0)
        beta((HALF,), k_ref[HALF])

        if pair == 0:
            gather(o_ref)
        else:
            gather(last_ref)

            def join(group, carry):
                first = last_ref[group, pl.ds(0, modes // 2), :]
                second = last_ref[group, pl.ds(modes // 2, modes // 2), :]
                even_half = (lane_index(first.shape) & 32) == 0
                o_ref[group, pl.ds(modes, modes // 2), :] = jnp.where(even_half, first, roll(second, 32))
                return carry

            lax.fori_loop(0, groups, join, 0)

    if with_mean:
        for group in range(groups):
            o_ref[group, pl.ds(modes, 8), :] = mean_ref[...]


def relax_kernel(a_ref, b1_ref, b2_ref, base_ref, coup_ref, kz_ref, om_ref, sw_ref, o_ref, rhs_ref, x_ref, cf_ref, rh_ref, rl_ref, zh_ref, zl_ref):
    modes = kz_ref.shape[0]
    stride = PARTS * STRIPES
    low, even = lane_masks((TILE, LANES))
    lane = lane_index((TILE, LANES))
    edge = ((lane & 63) == 0) | ((lane & 63) == 63)
    block_of = lane_index((1, LANES)) // SHARE

    def load(start, variable, stripe, part):
        return a_ref[pl.ds(start * stride + variable * 2 * STRIPES + stripe * 2 + part, TILE, stride=stride), :]

    for stripe in range(STRIPES):
        total = base_ref[pl.ds(stripe, 1), :]
        for block in range(BLOCKS):
            row = b1_ref[stripe * BLOCKS + block, pl.ds(modes, 1), :]
            total = total + jnp.where(block_of == block, roll(row, SHARE * (block - 1)), 0.0)
        cf_ref[pl.ds(stripe, 1), :] = total

    def unpack(ref, row, targets):
        for stripe in range(STRIPES):
            rows = [ref[stripe * BLOCKS + block, pl.ds(row, TILE), :] for block in range(BLOCKS)]
            values = block_transpose(rows, low, even)
            for value, (variable, part, start) in zip(values, targets):
                rhs_ref[stripe * PARTS + variable * 2 + part, pl.ds(start, TILE), :] = load(start, variable, stripe, part) + march_step * value

    def gather_pairs(i, carry):
        base = pl.multiple_of(i * TILE, TILE)
        unpack(b1_ref, base, [(2, 0, base), (3, 0, base), (2, 1, base), (3, 1, base)])
        unpack(b2_ref, base, [(0, 0, base), (1, 0, base), (0, 1, base), (1, 1, base)])
        return carry

    def gather_last(i, carry):
        base = pl.multiple_of(i * TILE, TILE)
        other = pl.multiple_of(modes // 2 + i * TILE, TILE)
        unpack(b2_ref, pl.multiple_of(modes + i * TILE, TILE), [(4, 0, base), (4, 0, other), (4, 1, base), (4, 1, other)])
        return carry

    lax.fori_loop(0, modes // TILE, gather_pairs, 0)
    lax.fori_loop(0, modes // 2 // TILE, gather_last, 0)

    def tile(i, carry):
        base = pl.multiple_of(i * TILE, TILE)
        rows = pl.ds(base, TILE)
        for stripe in range(STRIPES):
            for part in range(PARTS):
                x_ref[stripe * PARTS + part] = load(base, part // 2, stripe, part % 2)

        def sweep(index, sweep_carry):
            for part in range(PARTS):
                rims = None
                for stripe in range(STRIPES):
                    term = jnp.where(edge, x_ref[stripe * PARTS + part], 0.0)
                    term = roll(term, 2 * stripe) if stripe else term
                    rims = term if rims is None else rims + term
                high, low_part = split(rims)
                zh_ref[pl.ds(part * TILE, TILE), :] = high
                zl_ref[pl.ds(part * TILE, TILE), :] = low_part
            for stripe in range(STRIPES):
                values = [x_ref[stripe * PARTS + part] for part in range(PARTS)]
                rotation = kz_ref[rows, :] * cf_ref[pl.ds(stripe, 1), :] - om_ref[rows, :]
                for k in range(5):
                    out_re = rhs_ref[stripe * PARTS + 2 * k, rows, :] + rotation * values[2 * k + 1]
                    out_im = rhs_ref[stripe * PARTS + 2 * k + 1, rows, :] - rotation * values[2 * k]
                    for j in range(5):
                        weight = coup_ref[pl.ds((k * 5 + j) * STRIPES + stripe, 1), :]
                        out_re = out_re - weight * values[2 * j]
                        out_im = out_im - weight * values[2 * j + 1]
                    for part, out in ((2 * k, out_re), (2 * k + 1, out_im)):
                        high, low_part = split(out)
                        rh_ref[pl.ds(part * TILE, TILE), :] = high
                        rl_ref[pl.ds(part * TILE, TILE), :] = low_part
                high = jnp.concatenate([rh_ref[...], zh_ref[...]], 1)
                low_rows = jnp.concatenate([rl_ref[...], zl_ref[...]], 1)
                both = dot(high, sw_ref[stripe])
                new = both[:, :LANES] + both[:, LANES:] + dot(low_rows, sw_ref[stripe, :, pl.ds(0, LANES)])
                x_ref[pl.ds(stripe * PARTS, PARTS)] = new.reshape(PARTS, TILE, LANES)
            return sweep_carry

        lax.fori_loop(0, SWEEPS, sweep, 0)
        for stripe in range(STRIPES):
            for part in range(PARTS):
                offset = base * stride + (part // 2) * 2 * STRIPES + stripe * 2 + part % 2
                o_ref[pl.ds(offset, TILE, stride=stride), :] = x_ref[stripe * PARTS + part]
        return carry

    lax.fori_loop(0, modes // TILE, tile, 0)


def split_host(x):
    high = x.astype(jnp.bfloat16)
    low_part = (x - high.astype(np.float64)).astype(jnp.bfloat16)
    return high, low_part


def beta_matrices():
    index = np.arange(NB)
    angles = (index[:, None] * index[None, :] % NB) * (2.0 * math.pi / NB)
    cosine = np.cos(angles)
    sine = np.sin(angles)
    wave = 2.0 * np.where(index >= NB // 2, index - NB, index) / NB
    factor = 1.0 / math.sqrt(M)
    forward = factor * np.block([[cosine, sine], [-sine * wave, cosine * wave]])
    backward = -factor * np.concatenate([cosine, sine], 0)
    return tuple(np.concatenate(split_host(matrix), 0) for matrix in (forward, backward))


def omega_table():
    angles = np.arange(NW) * (2.0 * math.pi / NW)
    rows = np.concatenate([np.repeat(np.cos(angles)[:, None], 64, 1), np.repeat(np.sin(angles)[:, None], 64, 1)], 1)
    return np.repeat(rows[:, None, :], 8, 1).astype(np.float32)


def split_device(x):
    high = lax.reduce_precision(x, 8, 7)
    return high.astype(jnp.bfloat16), (x - high).astype(jnp.bfloat16)


def derivative_matrix(wall_operator, half):
    own = lax.dynamic_slice(wall_operator, (half * SHARE, 0), (SHARE, SLAB)).T
    mine = lax.dynamic_slice(own, (half * SHARE, 0), (SHARE, SHARE))
    other = lax.dynamic_slice(own, ((1 - half) * SHARE, 0), (SHARE, SHARE))
    same = jnp.eye(BLOCKS, dtype=jnp.float32)
    stacked = jnp.stack([mine, other], 0)
    full = same[None, :, None, :, None] * stacked[:, None, :, None, :]
    full = full.reshape(2 * LANES, LANES)
    return jnp.concatenate(split_device(full), 1)


def solve_matrices(slab_map, slab_inverse):
    count = slab_inverse.shape[0]
    slots = jnp.arange(count, dtype=jnp.int32)
    holds = slab_map[:, None] == slots[None, :]
    below_of = jnp.concatenate([slab_map[:1] * 0 - 1, slab_map[:-1]])
    above_of = jnp.concatenate([slab_map[1:], slab_map[:1] * 0 - 1])
    below = jnp.sum(jnp.where(holds, below_of[:, None], 0), 0)
    above = jnp.sum(jnp.where(holds, above_of[:, None], 0), 0)
    lane = jnp.arange(LANES, dtype=jnp.int32)

    def one_hot(slot, position):
        where = (slot % 2 * SLAB + position + 2 * (slot // 2)) % LANES
        return ((slot >= 0)[:, None] & (where[:, None] == lane[None, :])).astype(jnp.float32)

    low_rim = one_hot(below, SLAB - 1)
    high_rim = one_hot(above, 0)
    rims = coupling * (
        low_rim[:, :, None] * slab_inverse[:, None, :, 0] + high_rim[:, :, None] * slab_inverse[:, None, :, SLAB - 1]
    )
    rims = rims.reshape(STRIPES, 2, LANES, SLAB).transpose(0, 2, 1, 3).reshape(STRIPES, LANES, LANES)
    same = jnp.eye(2, dtype=jnp.float32)
    turned = slab_inverse.transpose(0, 2, 1).reshape(STRIPES, 2, SLAB, SLAB)
    blocks = same[None, :, None, :, None] * turned[:, :, :, None, :]
    blocks = blocks.reshape(STRIPES, LANES, LANES)
    return jnp.concatenate(split_device(jnp.concatenate([blocks, rims], 1)), 2)


def call(kernel, inputs, outputs, scratch, scalars=0, cost=0):
    specs = [pl.BlockSpec(memory_space=pltpu.SMEM)] * scalars
    specs += [pl.BlockSpec(memory_space=pltpu.VMEM)] * (len(inputs) - scalars)
    single = isinstance(outputs, tuple)
    shapes = [outputs] if single else list(outputs)
    out = pl.pallas_call(
        kernel,
        out_shape=[jax.ShapeDtypeStruct(shape, jnp.float32) for shape in shapes],
        in_specs=specs,
        out_specs=[pl.BlockSpec(memory_space=pltpu.VMEM)] * len(shapes),
        scratch_shapes=scratch,
        compiler_params=pltpu.CompilerParams(vmem_limit_bytes=VMEM_LIMIT),
        cost_estimate=pl.CostEstimate(flops=cost, bytes_accessed=8 << 20, transcendentals=0),
    )(*inputs)
    return out[0] if single else out


def vmem(*shape, dtype=jnp.float32):
    return pltpu.VMEM(shape, dtype)


def local_halves(amplitudes, mode_table, slab_map, base_flow, base_coupling, slab_inverse, wall_operator):
    modes = amplitudes.shape[0]
    points = amplitudes.shape[3]
    groups = lax.axis_size("modes")
    index = lax.axis_index("modes")
    exchange = functools.partial(lax.all_to_all, axis_name="modes", split_axis=0, concat_axis=0, tiled=True)
    neighbours = [(j, j ^ 1) for j in range(groups)]

    rows = amplitudes.transpose(0, 2, 1, 3).reshape(modes, 5, 2, STRIPES, LANES)
    rows = rows.transpose(0, 1, 3, 2, 4).reshape(modes * PARTS * STRIPES, LANES)
    positions = mode_table[:, 0] * NB + mode_table[:, 1]
    forward, backward = (jnp.asarray(matrix) for matrix in beta_matrices())
    table = jnp.asarray(omega_table())
    derivative = derivative_matrix(wall_operator, index % 2)
    solve = solve_matrices(slab_map, slab_inverse)
    beta_index = lax.dynamic_slice_in_dim(mode_table[:, 1], index * modes, modes)
    omega_index = lax.dynamic_slice_in_dim(mode_table[:, 0], index * modes, modes)
    signed = jnp.where(beta_index >= NB // 2, beta_index - NB, beta_index)
    wave = phase_gain * (2.0 * signed.astype(jnp.float32) / NB)
    frequency = omega_step * omega_index.astype(jnp.float32)
    wave = jnp.broadcast_to(wave[:, None], (modes, LANES))
    frequency = jnp.broadcast_to(frequency[:, None], (modes, LANES))

    sent_first = call(pack_velocity, [rows], (groups, modes, LANES), [])
    first = exchange(sent_first)
    sent_second = call(pack_others, [rows], (groups, modes // 2 * 3, LANES), [])
    second = exchange(sent_second)

    grid = vmem(M, LANES)
    spectrum = vmem(NW, 2 * NB, LANES)
    folded = vmem(TIMES, NB, LANES)
    unpacked = vmem(groups, modes, LANES)
    physical = (TIMES, NB, LANES)
    f1, g1, mean = call(
        functools.partial(synthesis, True),
        [positions, first, forward, table],
        [(1,) + physical, (1,) + physical, (8, LANES)],
        [grid, spectrum],
        scalars=1,
        cost=2 * 10**9,
    )
    s1 = lax.ppermute(f1, "modes", neighbours)
    back_first = call(
        functools.partial(force_analysis, True),
        [positions, f1, f1, s1, g1, derivative, backward, table, mean],
        (groups, modes + 8, LANES),
        [folded, grid],
        scalars=1,
        cost=2 * 10**9,
    )
    got_first = exchange(back_first)
    f2, g2 = call(
        functools.partial(synthesis, False),
        [positions, second, forward, table],
        [(2,) + physical, (2,) + physical],
        [grid, spectrum, unpacked],
        scalars=1,
        cost=4 * 10**9,
    )
    s2 = lax.ppermute(f2, "modes", neighbours)
    back_second = call(
        functools.partial(force_analysis, False),
        [positions, f1, f2, s2, g2, derivative, backward, table],
        (groups, modes // 2 * 3, LANES),
        [folded, grid, unpacked],
        scalars=1,
        cost=4 * 10**9,
    )
    got_second = exchange(back_second)

    stacked = TILE * PARTS
    out = call(
        relax_kernel,
        [
            rows,
            got_first,
            got_second,
            base_flow.reshape(STRIPES, LANES),
            base_coupling.reshape(25 * STRIPES, LANES),
            wave,
            frequency,
            solve,
        ],
        (modes * PARTS * STRIPES, LANES),
        [
            vmem(STRIPES * PARTS, modes, LANES),
            vmem(STRIPES * PARTS, TILE, LANES),
            vmem(8, LANES),
            vmem(stacked, LANES, dtype=jnp.bfloat16),
            vmem(stacked, LANES, dtype=jnp.bfloat16),
            vmem(stacked, LANES, dtype=jnp.bfloat16),
            vmem(stacked, LANES, dtype=jnp.bfloat16),
        ],
        cost=4 * 10**9,
    )
    out = out.reshape(modes, 5, STRIPES, 2, LANES).transpose(0, 1, 3, 2, 4).reshape(modes, 5, 2, points)
    return out.transpose(0, 2, 1, 3)


def local_any(amplitudes, mode_table, slab_map, base_flow, base_coupling, slab_inverse, wall_operator):
    points = amplitudes.shape[3]
    fits = points == STRIPES * LANES and points // lax.axis_size("modes") == SHARE
    fits = fits and slab_inverse.shape == (2 * STRIPES, SLAB, SLAB) and amplitudes.shape[0] % (2 * TILE) == 0
    chosen = local_halves if fits else local
    return chosen(amplitudes, mode_table, slab_map, base_flow, base_coupling, slab_inverse, wall_operator)


def solution(mesh):
    return jax.shard_map(
        local_any,
        mesh=mesh,
        in_specs=(
            P(("runs", "modes"), None, None, None),
            P(),
            P(),
            P("runs"),
            P("runs", None),
            P(),
            P(),
        ),
        out_specs=P(("runs", "modes"), None, None, None),
        check_vma=False,
    )
```

```python
import functools
import math

import jax
import jax.numpy as jnp
import numpy as np
from jax import lax
from jax.experimental import pallas as pl
from jax.experimental.pallas import tpu as pltpu
from jax.sharding import PartitionSpec as P

M = 4096
NB = 128
SWEEPS = 3
NW = 32


precise = lax.Precision.HIGHEST
omega_step = 0.01
phase_gain = 0.2
march_step = 0.2
coupling = 0.3


def twiddle(length):
    counter = jnp.arange(length, dtype=jnp.int32)
    product = counter[:, None] * counter[None, :] % length
    angles = product.astype(jnp.float32) * (2.0 * math.pi / length)
    return (jnp.cos(angles), jnp.sin(angles))


def mode_tables(mode_table):
    omega_index = mode_table[:, 0]
    beta_index = mode_table[:, 1]
    signed = jnp.where(beta_index >= NB // 2, beta_index - NB, beta_index)
    wavenum = 2.0 * signed.astype(jnp.float32) / NB
    frequency = omega_step * omega_index.astype(jnp.float32)
    grid_pos = omega_index * NB + beta_index
    mode_at = jnp.zeros((M,), jnp.int32).at[grid_pos].set(jnp.arange(M, dtype=jnp.int32))
    return (wavenum, frequency, grid_pos, mode_at)


def synthesize(real_part, imag_part, tables, factor):
    cos_omega, sin_omega, cos_beta, sin_beta = tables
    mixed_re = jnp.einsum("...wb,bz->...wz", real_part, cos_beta, precision=precise) - jnp.einsum(
        "...wb,bz->...wz", imag_part, sin_beta, precision=precise
    )
    mixed_im = jnp.einsum("...wb,bz->...wz", real_part, sin_beta, precision=precise) + jnp.einsum(
        "...wb,bz->...wz", imag_part, cos_beta, precision=precise
    )
    physical = jnp.einsum("...wz,wt->...tz", mixed_re, cos_omega, precision=precise) - jnp.einsum(
        "...wz,wt->...tz", mixed_im, sin_omega, precision=precise
    )
    return physical * factor


def analyze(physical, tables, factor):
    cos_omega, sin_omega, cos_beta, sin_beta = tables
    half_re = jnp.einsum("...tz,zb->...tb", physical, cos_beta, precision=precise)
    half_im = -jnp.einsum("...tz,zb->...tb", physical, sin_beta, precision=precise)
    coef_re = jnp.einsum("...tb,tw->...wb", half_re, cos_omega, precision=precise) + jnp.einsum(
        "...tb,tw->...wb", half_im, sin_omega, precision=precise
    )
    coef_im = jnp.einsum("...tb,tw->...wb", half_im, cos_omega, precision=precise) - jnp.einsum(
        "...tb,tw->...wb", half_re, sin_omega, precision=precise
    )
    return (coef_re * factor, coef_im * factor)


def forcing(normal_vel, spanwise_vel, wall_grad, span_grad, tables, factor):
    vel_v = synthesize(normal_vel[0], normal_vel[1], tables, factor)
    vel_w = synthesize(spanwise_vel[0], spanwise_vel[1], tables, factor)
    grad_y = synthesize(wall_grad[0], wall_grad[1], tables, factor)
    grad_z = synthesize(span_grad[0], span_grad[1], tables, factor)
    product = -(vel_v[None] * grad_y + vel_w[None] * grad_z)
    return analyze(product, tables, factor)


def wall_derivative(values, wall_operator):
    slab_width = wall_operator.shape[0]
    slab_count = values.shape[3] // slab_width
    blocks = values.reshape(values.shape[:3] + (slab_count, slab_width))
    return jnp.einsum("ij,abcsj->abcsi", wall_operator, blocks, precision=precise).reshape(
        values.shape
    )


def interface_table(slab_map, slab_count, slab_width):
    inverse = (
        jnp.zeros((slab_count,), jnp.int32)
        .at[slab_map]
        .set(jnp.arange(slab_count, dtype=jnp.int32))
    )
    position = jnp.arange(slab_count * slab_width, dtype=jnp.int32)
    slot_of = position // slab_width
    within = position % slab_width
    domain = inverse[slot_of]
    below = slab_map[jnp.maximum(domain - 1, 0)] * slab_width + (slab_width - 1)
    above = slab_map[jnp.minimum(domain + 1, slab_count - 1)] * slab_width
    lower_ok = (within == 0) & (domain > 0)
    upper_ok = (within == slab_width - 1) & (domain < slab_count - 1)
    source = jnp.where(lower_ok, below, jnp.where(upper_ok, above, 0))
    weight = (lower_ok | upper_ok).astype(jnp.float32)
    return (source, weight)


def relaxation(iterate, right_side, rotation, matrix, slab_inverse, source, weight):
    slab_count = slab_inverse.shape[0]
    slab_width = slab_inverse.shape[1]
    coupled = jnp.einsum("kjy,acjy->acky", matrix, iterate, precision=precise)
    applied = jnp.stack(
        [
            coupled[:, 0] - rotation[:, None, :] * iterate[:, 1],
            coupled[:, 1] + rotation[:, None, :] * iterate[:, 0],
        ],
        1,
    )
    rims = jnp.take(iterate, source, axis=3) * weight
    residual_in = right_side - applied + coupling * rims
    blocks = residual_in.reshape(iterate.shape[:3] + (slab_count, slab_width))
    return jnp.einsum("sij,acvsj->acvsi", slab_inverse, blocks, precision=precise).reshape(
        iterate.shape
    )


def local(amplitudes, mode_table, slab_map, base_flow, base_coupling, slab_inverse, wall_operator):
    local_modes = amplitudes.shape[0]
    wall_points = amplitudes.shape[3]
    groups = lax.axis_size("modes")
    point_share = wall_points // groups
    wavenum, frequency, grid_pos, mode_at = mode_tables(mode_table)
    first_mode = lax.axis_index("modes") * local_modes
    wave_local = lax.dynamic_slice_in_dim(wavenum, first_mode, local_modes)
    freq_local = lax.dynamic_slice_in_dim(frequency, first_mode, local_modes)
    tables = twiddle(NW) + twiddle(NB)
    factor = 1.0 / math.sqrt(M)
    source, weight = interface_table(slab_map, slab_inverse.shape[0], slab_inverse.shape[1])
    matrix = base_coupling.reshape(5, 5, wall_points)
    gradient = wall_derivative(amplitudes, wall_operator)
    span = jnp.stack(
        [
            -wave_local[:, None, None] * amplitudes[:, 1],
            wave_local[:, None, None] * amplitudes[:, 0],
        ],
        1,
    )
    fields = jnp.concatenate([amplitudes[:, :, 2:4], gradient, span], 2)
    field_count = fields.shape[2]
    channels = 2 * field_count
    outgoing = jnp.transpose(
        fields.reshape(local_modes, channels, groups, point_share), (1, 2, 3, 0)
    ).reshape(channels, groups, point_share * local_modes)
    incoming = lax.all_to_all(outgoing, "modes", split_axis=1, concat_axis=1, tiled=True)
    by_mode = jnp.transpose(
        incoming.reshape(channels, groups, point_share, local_modes), (0, 2, 1, 3)
    ).reshape(channels, point_share, M)
    gridded = by_mode[..., mode_at].reshape(2, field_count, point_share, NW, NB)
    normal_vel = gridded[:, 0]
    spanwise_vel = gridded[:, 1]
    wall_grad = gridded[:, 2:7]
    span_grad = gridded[:, 7:12]
    mean_crossflow = lax.all_gather(spanwise_vel[0, :, 0, 0], "modes", axis=0, tiled=True)
    coef_re, coef_im = forcing(normal_vel, spanwise_vel, wall_grad, span_grad, tables, factor)
    packed = jnp.stack([coef_re, coef_im], 0).reshape(10, point_share, M)[..., grid_pos]
    sendback = jnp.transpose(
        packed.reshape(10, point_share, groups, local_modes), (0, 2, 1, 3)
    ).reshape(10, groups, point_share * local_modes)
    returned = lax.all_to_all(sendback, "modes", split_axis=1, concat_axis=1, tiled=True)
    nonlinear = jnp.transpose(
        returned.reshape(10, groups, point_share, local_modes), (3, 0, 1, 2)
    ).reshape(local_modes, 2, 5, wall_points)
    crossflow = base_flow + mean_crossflow
    rotation = phase_gain * wave_local[:, None] * crossflow[None, :] - freq_local[:, None]
    right_side = amplitudes + march_step * nonlinear
    iterate = amplitudes
    for sweep_index in range(SWEEPS):
        iterate = relaxation(iterate, right_side, rotation, matrix, slab_inverse, source, weight)
    return iterate


LANES = 128
SHARE = 32
SLAB = 64
HALF = NW // 2
TIMES = HALF + 1
BLOCKS = LANES // SHARE
STRIPES = 4
PARTS = 10
TILE = 32
MIB = 1024 * 1024


def roll(x, shift):
    return pltpu.roll(x, shift % LANES, x.ndim - 1)


def lane_index(shape):
    return lax.broadcasted_iota(jnp.int32, shape, len(shape) - 1)


def lane_masks(shape):
    lane = lane_index(shape)
    return (lane < 64, (lane & 32) == 0)


def real_sign(shape):
    return jnp.where(lane_index(shape) < 64, 1.0, -1.0).astype(jnp.float32)


def block_transpose(rows, low, even):
    r0, r1, r2, r3 = rows
    t0 = jnp.where(low, r0, roll(r2, 64))
    t2 = jnp.where(low, roll(r0, 64), r2)
    t1 = jnp.where(low, r1, roll(r3, 64))
    t3 = jnp.where(low, roll(r1, 64), r3)
    return (
        jnp.where(even, t0, roll(t1, 32)),
        jnp.where(even, roll(t0, 96), t1),
        jnp.where(even, t2, roll(t3, 32)),
        jnp.where(even, roll(t2, 96), t3),
    )


def split(x):
    high = x.astype(jnp.bfloat16)
    return high, (x - high.astype(jnp.float32)).astype(jnp.bfloat16)


def dot(a, b):
    return jnp.dot(a, b, preferred_element_type=jnp.float32)


def cosine_sine(inputs, length, table, sign, real):
    if length == 4:
        first, middle, last = inputs
        middle_re = middle * real
        total = first + last
        return [total + middle_re, (first - last) + (middle - middle_re), total - middle_re]
    step = NW // length
    quarter = length // 4
    even = cosine_sine(inputs[0::2], length // 2, table, sign, real)
    odd_inputs = [(a, inputs[a]) for a in range(1, length // 2, 2)]
    odd = []
    for t in range(quarter + 1):
        if t == 0:
            total = odd_inputs[0][1]
            for _, value in odd_inputs[1:]:
                total = total + value
            odd.append(total * real)
        elif t == quarter:
            total = odd_inputs[0][1]
            for a, value in odd_inputs[1:]:
                total = total + value if a % 4 == 1 else total - value
            odd.append(total - total * real)
        else:
            total = None
            for a, value in odd_inputs:
                term = table(a * t * step % NW) * value
                total = term if total is None else total + term
            odd.append(total)
    out = [None] * (length // 2 + 1)
    for t in range(quarter + 1):
        out[t] = even[t] + odd[t]
        out[length // 2 - t] = sign * (even[t] - odd[t])
    out[quarter] = even[quarter] + odd[quarter]
    return out


def spread(ref, offset):
    flat = ref.reshape(ref.shape[0] * ref.shape[1], LANES)
    return flat[pl.ds(offset, ref.shape[0], stride=ref.shape[1]), :]


def pack_pair(first, first_offset, second, second_offset, low, even):
    out = []
    for stripe in range(STRIPES):
        rows = []
        for part in range(2):
            rows.append(spread(first, first_offset + stripe * 2 + part))
            rows.append(spread(second, second_offset + stripe * 2 + part))
        out.extend(block_transpose(rows, low, even))
    return out


def pack_first(near_ref, far_ref, near_last_ref, far_last_ref, o_ref):
    low, even = lane_masks((TILE, LANES))
    pieces = (
        (near_ref, 0, near_ref, 2 * STRIPES),
        (far_ref, 0, far_ref, 2 * STRIPES),
        (near_last_ref, 0, far_last_ref, 0),
    )
    for place, piece in enumerate(pieces):
        for group, value in enumerate(pack_pair(*piece, low, even)):
            o_ref[group, place] = value


def pack_second(near_ref, o_ref):
    low, even = lane_masks((TILE, LANES))
    for group, value in enumerate(pack_pair(near_ref, 0, near_ref, 2 * STRIPES, low, even)):
        o_ref[group] = value


ROWS = 128


def loop(count, unroll, body):
    def step(i, carry):
        for j in range(unroll):
            body(i * unroll + j)
        return carry

    lax.fori_loop(0, count // unroll, step, 0)
    for i in range(count // unroll * unroll, count):
        body(i)


def lanes_constants():
    sign = real_sign((8, LANES))
    real = jnp.where(lane_index((8, LANES)) < 64, 1.0, 0.0).astype(jnp.float32)
    even = (lane_index((8, LANES)) & 32) == 0
    return sign, real, even


def pair_left(even, near, far):
    return jnp.where(even, near, roll(far, 32))


def pair_right(even, near, far):
    return jnp.where(even, roll(near, 96), far)


def synthesis(with_last, pos_ref, r_ref, w_ref, tab_ref, *refs):
    if with_last:
        f_ref, g_ref, f_last_ref, g_last_ref, mean_ref, grid_ref, spec_ref, turned_ref = refs
    else:
        f_ref, g_ref, grid_ref, spec_ref = refs
    groups = r_ref.shape[0]
    modes = M // groups
    sign, real, even = lanes_constants()
    wide_sign = real_sign((NB, LANES))
    wide_even = (lane_index((NB, LANES)) & 32) == 0

    def table(j):
        return tab_ref[j]

    def scatter(group, mode, source, row):
        for j in range(ROWS):
            cell = pos_ref[group * modes + mode + j]
            grid_ref[pl.ds(cell, 1), :] = source[group, pl.ds(row + j, 1), :]

    def beta(first, second):
        columns = [jnp.concatenate([x, -wide_sign * roll(x, 64)], 0) for x in (first, second)]
        high, low_part = split(jnp.concatenate(columns, 1))
        product = dot(w_ref[...], high)
        out = product[: 2 * NB] + product[2 * NB :] + dot(w_ref[pl.ds(0, 2 * NB), :], low_part)
        return out[:, :LANES], out[:, LANES:]

    def grid(a):
        return grid_ref[pl.ds(pl.multiple_of(a * NB, NB), NB), :]

    def both_halves(i):
        group = i // (modes // ROWS)
        start = pl.multiple_of(i % (modes // ROWS) * ROWS, ROWS)
        scatter(group, start, r_ref, start)

    loop(groups * (modes // ROWS), 1, both_halves)
    if with_last:
        mean_ref[...] = grid_ref[pl.ds(0, 8), :]

    def full_beta(i):
        spec_ref[2 * i], spec_ref[2 * i + 1] = beta(grid(2 * i), grid(2 * i + 1))

    loop(NW // 2, 2, full_beta)

    def full_omega(out_ref, shift):
        def body(i):
            rows = pl.ds(pl.multiple_of(i * 8, 8), 8)
            source = pl.ds(pl.multiple_of(shift + i * 8, 8), 8)
            inputs = [spec_ref[0, source, :] * real]
            for a in range(1, HALF):
                inputs.append(spec_ref[a, source, :] + sign * spec_ref[NW - a, source, :])
            inputs.append(spec_ref[HALF, source, :] * real)
            for t, value in enumerate(cosine_sine(inputs, NW, table, sign, real)):
                out_ref[t, rows, :] = value - sign * roll(value, 64)

        loop(NB // 8, 2, body)

    full_omega(f_ref, 0)
    full_omega(g_ref, NB)
    if not with_last:
        return

    def turn(group):
        turned_ref[group] = roll(r_ref[group, pl.ds(modes, modes // 2), :], 96)
        for block in range(modes // 2 // ROWS):
            scatter(group, block * ROWS, r_ref, modes + block * ROWS)
            scatter(group, modes // 2 + block * ROWS, turned_ref, block * ROWS)

    loop(groups, 1, turn)

    def half_beta(i):
        columns = [pair_left(wide_even, grid(a), grid(a + HALF)) for a in (2 * i, 2 * i + 1)]
        spec_ref[2 * i], spec_ref[2 * i + 1] = beta(*columns)

    loop(HALF // 2, 2, half_beta)

    def half_omega(out_ref, shift):
        def body(i):
            rows = pl.ds(pl.multiple_of(i * 8, 8), 8)
            near = pl.ds(pl.multiple_of(shift + i * 8, 8), 8)
            far = pl.ds(pl.multiple_of(shift + NB // 2 + i * 8, 8), 8)
            firsts = []
            seconds = []
            for a in range(HALF):
                pieces = (even, spec_ref[a, near, :], spec_ref[a, far, :])
                firsts.append(pair_left(*pieces))
                seconds.append(pair_right(*pieces))
            inputs = [firsts[0] * real]
            for a in range(1, HALF):
                inputs.append(firsts[a] + sign * seconds[HALF - a])
            inputs.append(seconds[0] * real)
            for t, value in enumerate(cosine_sine(inputs, NW, table, sign, real)):
                out_ref[t, rows, :] = value - sign * roll(value, 64)

        loop(NB // 16, 2, body)

    half_omega(f_last_ref, 0)
    half_omega(g_last_ref, NB)


def force_analysis(with_last, pos_ref, vw_ref, f_ref, s_ref, g_ref, d_ref, w_ref, tab_ref, *refs):
    if with_last:
        f_last_ref, s_last_ref, g_last_ref, mean_ref, o_ref, k_ref, r_ref, n_ref, turned_ref = refs
    else:
        o_ref, k_ref, r_ref, n_ref = refs
    groups = o_ref.shape[0]
    modes = M // groups
    sign, real, _ = lanes_constants()
    wide_sign = real_sign((NB, LANES))
    wide_real, wide_even = lane_masks((NB, LANES))
    half_rows = NB // 2

    def table(j):
        return tab_ref[j]

    def gather(group, mode, target, row):
        for j in range(ROWS):
            cell = pos_ref[group * modes + mode + j]
            target[group, pl.ds(row + j, 1), :] = n_ref[pl.ds(cell, 1), :]

    def force_of(t, rows, v, w, f, s, g):
        high, low_part = split(jnp.concatenate([f, s], 1))
        both = dot(high, d_ref[...])
        grad = both[:, :LANES] + both[:, LANES:] + dot(low_part, d_ref[:, :LANES])
        force = v * grad + w * g
        if t is None:
            return jnp.where(wide_real[:rows], force, 0.0)
        return force + wide_sign[:rows] * roll(force, 64)

    def full_product(t, alone=False):
        vw = vw_ref[t]
        v = pair_left(wide_even, vw, vw)
        w = pair_right(wide_even, vw, vw)
        k_ref[t] = force_of(None if alone else t, NB, v, w, f_ref[t], s_ref[t], g_ref[t])

    def products(product):
        product(0, True)
        product(HALF, True)
        loop(HALF - 1, 3, lambda i: product(i + 1))

    def omegas(tiles):
        def body(i):
            rows = pl.ds(pl.multiple_of(i * 8, 8), 8)
            inputs = [k_ref[t, rows, :] for t in range(TIMES)]
            for a, value in enumerate(cosine_sine(inputs, NW, table, sign, real)):
                r_ref[a, rows, :] = value

        loop(tiles, 2, body)

    def beta(columns):
        high, low_part = split(jnp.concatenate(columns, 1) if len(columns) > 1 else columns[0])
        both = dot(w_ref[...], high)
        out = both[: 2 * NB] + both[2 * NB :] + dot(w_ref[pl.ds(0, 2 * NB), :], low_part)
        result = []
        for j in range(len(columns)):
            cosine = out[:NB, j * LANES : (j + 1) * LANES]
            sine = roll(out[NB:, j * LANES : (j + 1) * LANES], 64)
            result.append((cosine + wide_sign * sine, wide_sign * cosine - sine))
        return result

    def store(a, plus, minus):
        mirror = (NW - a) % NW
        n_ref[pl.ds(pl.multiple_of(mirror * NB, NB), NB), :] = minus
        n_ref[pl.ds(pl.multiple_of(a * NB, NB), NB), :] = plus

    products(full_product)
    omegas(NB // 8)

    def full_beta(i):
        for j, (plus, minus) in enumerate(beta([r_ref[2 * i], r_ref[2 * i + 1]])):
            store(2 * i + j, plus, minus)

    loop(HALF // 2, 2, full_beta)
    store(HALF, *beta([r_ref[HALF]])[0])

    def both_halves(i):
        group = i // (modes // ROWS)
        start = pl.multiple_of(i % (modes // ROWS) * ROWS, ROWS)
        gather(group, start, o_ref, start)

    loop(groups * (modes // ROWS), 1, both_halves)
    if not with_last:
        return

    def half_product(t, alone=False):
        vw = vw_ref[t]
        near = vw[:half_rows]
        far = vw[half_rows:]
        v = pair_left(wide_even[:half_rows], near, far)
        w = pair_right(wide_even[:half_rows], near, far)
        k_ref[t, pl.ds(0, half_rows), :] = force_of(
            None if alone else t, half_rows, v, w, f_last_ref[t], s_last_ref[t], g_last_ref[t]
        )

    products(half_product)
    omegas(NB // 16)

    def half_columns(a):
        even = wide_even[:half_rows]
        pieces = (even, r_ref[a, pl.ds(0, half_rows), :], r_ref[a + 1, pl.ds(0, half_rows), :])
        return jnp.concatenate([pair_left(*pieces), pair_right(*pieces)], 0)

    def half_beta(i):
        for j, (plus, minus) in enumerate(beta([half_columns(4 * i), half_columns(4 * i + 2)])):
            a = 4 * i + 2 * j
            store(a, plus, minus)
            store(a + 1, roll(plus, 96), roll(minus, 96))

    loop(HALF // 4, 1, half_beta)
    last = r_ref[HALF, pl.ds(0, half_rows), :]
    store(HALF, *beta([jnp.concatenate([last, roll(last, 96)], 0)])[0])

    def turn(group):
        for block in range(modes // 2 // ROWS):
            gather(group, block * ROWS, o_ref, modes + block * ROWS)
            gather(group, modes // 2 + block * ROWS, turned_ref, block * ROWS)
        here = pl.ds(modes, modes // 2)
        near = o_ref[group, here, :]
        o_ref[group, here, :] = pair_left((lane_index(near.shape) & 32) == 0, near, turned_ref[group])
        o_ref[group, pl.ds(modes // 2 * 3, 8), :] = mean_ref[...]

    loop(groups, 1, turn)


def find_rims(x_of, zh_ref, zl_ref):
    lane = lane_index((TILE, LANES))
    edge = ((lane & 63) == 0) | ((lane & 63) == 63)
    for part in range(PARTS):
        rims = None
        for stripe in range(STRIPES):
            term = jnp.where(edge, x_of(stripe, part), 0.0)
            term = roll(term, 2 * stripe) if stripe else term
            rims = term if rims is None else rims + term
        rows = pl.ds(part * TILE, TILE)
        zh_ref[rows, :], zl_ref[rows, :] = split(rims)


def three_pass(high, low_part, weights):
    both = dot(high, weights)
    return both[:, :LANES] + both[:, LANES:] + dot(low_part, weights[:, :LANES])


def relax(stripe, x_of, cross, kz_ref, om_ref, coup_ref, sw_ref, rh_ref, rl_ref, zh_ref, zl_ref):
    values = [x_of(stripe, part) for part in range(PARTS)]
    rotation = kz_ref[...] * cross - om_ref[...]
    for k in range(5):
        out_re = rotation * values[2 * k + 1]
        out_im = -(rotation * values[2 * k])
        for j in range(5):
            weight = coup_ref[pl.ds((k * 5 + j) * STRIPES + stripe, 1), :]
            out_re = out_re - weight * values[2 * j]
            out_im = out_im - weight * values[2 * j + 1]
        for part, out in ((2 * k, out_re), (2 * k + 1, out_im)):
            rows = pl.ds(part * TILE, TILE)
            rh_ref[stripe, rows, :], rl_ref[stripe, rows, :] = split(out)
    high = jnp.concatenate([rh_ref[stripe], zh_ref[...]], 1)
    low_rows = jnp.concatenate([rl_ref[stripe], zl_ref[...]], 1)
    return three_pass(high, low_rows, sw_ref[stripe])


def relax_first(a_ref, b_ref, t_ref, mean_ref, base_ref, coup_ref, kz_ref, om_ref, sw_ref, start_ref, x_ref, cf_ref, rh_ref, rl_ref, zh_ref, zl_ref):
    low, even = lane_masks((TILE, LANES))
    block_of = lane_index((1, LANES)) // SHARE
    far = pl.program_id(0) >= pl.num_programs(0) // 2
    for stripe in range(STRIPES):
        total = base_ref[pl.ds(stripe, 1), :]
        for block in range(BLOCKS):
            row = mean_ref[stripe * BLOCKS + block, pl.ds(0, 1), :]
            total = total + jnp.where(block_of == block, roll(row, SHARE * (block - 1)), 0.0)
        cf_ref[pl.ds(stripe, 1), :] = total

    def x_of(stripe, part):
        return spread(a_ref, part // 2 * 2 * STRIPES + stripe * 2 + part % 2)

    for stripe in range(STRIPES):
        groups = [stripe * BLOCKS + block for block in range(BLOCKS)]
        velocity = block_transpose([b_ref[group] for group in groups], low, even)
        last = block_transpose([t_ref[group] for group in groups], low, even)
        gained = {
            4: velocity[0],
            6: velocity[1],
            5: velocity[2],
            7: velocity[3],
            8: jnp.where(far, last[1], last[0]),
            9: jnp.where(far, last[3], last[2]),
        }
        for part in range(PARTS):
            right = x_of(stripe, part)
            if part in gained:
                right = right + march_step * gained[part]
            rows = pl.ds(part * TILE, TILE)
            rh_ref[stripe, rows, :], rl_ref[stripe, rows, :] = split(right)
        solved = three_pass(rh_ref[stripe], rl_ref[stripe], sw_ref[stripe, pl.ds(0, LANES), :])
        start_ref[pl.ds(stripe * PARTS, PARTS)] = solved.reshape(PARTS, TILE, LANES)
    find_rims(x_of, zh_ref, zl_ref)
    for stripe in range(STRIPES):
        here = pl.ds(stripe * PARTS, PARTS)
        cross = cf_ref[pl.ds(stripe, 1), :]
        new = relax(stripe, x_of, cross, kz_ref, om_ref, coup_ref, sw_ref, rh_ref, rl_ref, zh_ref, zl_ref)
        x_ref[here] = start_ref[here] + new.reshape(PARTS, TILE, LANES)


def relax_last(start_ref, first_ref, b_ref, cf_ref, coup_ref, kz_ref, om_ref, sw_ref, o_ref, right_ref, x_ref, rh_ref, rl_ref, zh_ref, zl_ref):
    low, even = lane_masks((TILE, LANES))
    gained = 4
    for stripe in range(STRIPES):
        here = pl.ds(stripe * PARTS, PARTS)
        rows = [b_ref[stripe * BLOCKS + block] for block in range(BLOCKS)]
        first_re, second_re, first_im, second_im = block_transpose(rows, low, even)
        for part, value in enumerate((first_re, first_im, second_re, second_im)):
            place = pl.ds(part * TILE, TILE)
            rh_ref[stripe, place, :], rl_ref[stripe, place, :] = split(march_step * value)
        place = pl.ds(0, gained * TILE)
        weights = sw_ref[stripe, pl.ds(0, LANES), :]
        added = three_pass(rh_ref[stripe, place, :], rl_ref[stripe, place, :], weights).reshape(gained, TILE, LANES)
        with_added = pl.ds(stripe * PARTS, gained)
        others = pl.ds(stripe * PARTS + gained, PARTS - gained)
        right_ref[with_added] = start_ref[with_added] + added
        x_ref[with_added] = first_ref[with_added] + added
        right_ref[others] = start_ref[others]
        x_ref[others] = first_ref[others]

    def x_of(stripe, part):
        return x_ref[stripe * PARTS + part]

    flat = o_ref.reshape(TILE * PARTS * STRIPES, LANES)
    for sweep in range(1, SWEEPS):
        find_rims(x_of, zh_ref, zl_ref)
        for stripe in range(STRIPES):
            here = pl.ds(stripe * PARTS, PARTS)
            cross = cf_ref[pl.ds(stripe, 1), :]
            new = relax(stripe, x_of, cross, kz_ref, om_ref, coup_ref, sw_ref, rh_ref, rl_ref, zh_ref, zl_ref)
            new = right_ref[here] + new.reshape(PARTS, TILE, LANES)
            if sweep < SWEEPS - 1:
                x_ref[here] = new
                continue
            for part in range(PARTS):
                offset = part // 2 * 2 * STRIPES + stripe * 2 + part % 2
                flat[pl.ds(offset, TILE, stride=PARTS * STRIPES), :] = new[part]


def split_host(x):
    high = x.astype(jnp.bfloat16)
    low_part = (x - high.astype(np.float64)).astype(jnp.bfloat16)
    return high, low_part


def beta_matrices():
    index = np.arange(NB)
    angles = (index[:, None] * index[None, :] % NB) * (2.0 * math.pi / NB)
    cosine = np.cos(angles)
    sine = np.sin(angles)
    wave = 2.0 * np.where(index >= NB // 2, index - NB, index) / NB
    factor = 1.0 / math.sqrt(M)
    forward = factor * np.block([[cosine, sine], [-sine * wave, cosine * wave]])
    backward = -factor * np.concatenate([cosine, sine], 0)
    return tuple(np.concatenate(split_host(matrix), 0) for matrix in (forward, backward))


def omega_table():
    angles = np.arange(NW) * (2.0 * math.pi / NW)
    rows = np.concatenate([np.repeat(np.cos(angles)[:, None], 64, 1), np.repeat(np.sin(angles)[:, None], 64, 1)], 1)
    return np.repeat(rows[:, None, :], 8, 1).astype(np.float32)


def split_device(x):
    high = lax.reduce_precision(x, 8, 7)
    return high.astype(jnp.bfloat16), (x - high).astype(jnp.bfloat16)


def derivative_matrix(wall_operator, half):
    own = lax.dynamic_slice(wall_operator, (half * SHARE, 0), (SHARE, SLAB)).T
    mine = lax.dynamic_slice(own, (half * SHARE, 0), (SHARE, SHARE))
    other = lax.dynamic_slice(own, ((1 - half) * SHARE, 0), (SHARE, SHARE))
    same = jnp.eye(BLOCKS, dtype=jnp.float32)
    stacked = jnp.stack([mine, other], 0)
    full = same[None, :, None, :, None] * stacked[:, None, :, None, :]
    full = full.reshape(2 * LANES, LANES)
    return jnp.concatenate(split_device(full), 1)


def solve_matrices(slab_map, slab_inverse):
    count = slab_inverse.shape[0]
    slots = jnp.arange(count, dtype=jnp.int32)
    holds = slab_map[:, None] == slots[None, :]
    below_of = jnp.concatenate([slab_map[:1] * 0 - 1, slab_map[:-1]])
    above_of = jnp.concatenate([slab_map[1:], slab_map[:1] * 0 - 1])
    below = jnp.sum(jnp.where(holds, below_of[:, None], 0), 0)
    above = jnp.sum(jnp.where(holds, above_of[:, None], 0), 0)
    lane = jnp.arange(LANES, dtype=jnp.int32)

    def one_hot(slot, position):
        where = (slot % 2 * SLAB + position + 2 * (slot // 2)) % LANES
        return ((slot >= 0)[:, None] & (where[:, None] == lane[None, :])).astype(jnp.float32)

    low_rim = one_hot(below, SLAB - 1)
    high_rim = one_hot(above, 0)
    rims = coupling * (
        low_rim[:, :, None] * slab_inverse[:, None, :, 0] + high_rim[:, :, None] * slab_inverse[:, None, :, SLAB - 1]
    )
    rims = rims.reshape(STRIPES, 2, LANES, SLAB).transpose(0, 2, 1, 3).reshape(STRIPES, LANES, LANES)
    same = jnp.eye(2, dtype=jnp.float32)
    turned = slab_inverse.transpose(0, 2, 1).reshape(STRIPES, 2, SLAB, SLAB)
    blocks = same[None, :, None, :, None] * turned[:, :, :, None, :]
    blocks = blocks.reshape(STRIPES, LANES, LANES)
    return jnp.concatenate(split_device(jnp.concatenate([blocks, rims], 1)), 2)


def call(kernel, inputs, outputs, scratch, scalars=0, cost=0, limit=60, grid=None, in_specs=None, out_specs=None):
    whole = pl.BlockSpec(memory_space=pltpu.VMEM)
    if in_specs is None:
        in_specs = [pl.BlockSpec(memory_space=pltpu.SMEM)] * scalars + [whole] * (len(inputs) - scalars)
    if out_specs is None:
        out_specs = [whole] * len(outputs)
    extra = {} if grid is None else {"grid": grid}
    return pl.pallas_call(
        kernel,
        out_shape=[jax.ShapeDtypeStruct(shape, jnp.float32) for shape in outputs],
        in_specs=in_specs,
        out_specs=out_specs,
        scratch_shapes=scratch,
        compiler_params=pltpu.CompilerParams(vmem_limit_bytes=limit * MIB),
        cost_estimate=pl.CostEstimate(flops=cost, bytes_accessed=8 << 20, transcendentals=0),
        **extra,
    )(*inputs)


def vmem(*shape, dtype=jnp.float32):
    return pltpu.VMEM(shape, dtype)


def fixed(*shape):
    return pl.BlockSpec(shape, lambda i: (0,) * len(shape))


def local_halves(amplitudes, mode_table, slab_map, base_flow, base_coupling, slab_inverse, wall_operator):
    modes = amplitudes.shape[0]
    points = amplitudes.shape[3]
    groups = lax.axis_size("modes")
    index = lax.axis_index("modes")
    exchange = functools.partial(lax.all_to_all, axis_name="modes", split_axis=0, concat_axis=0, tiled=True)
    neighbours = [(j, j ^ 1) for j in range(groups)]
    stride = PARTS * STRIPES
    tiles = modes // TILE
    first_rows = modes // 2 * 3

    rows = amplitudes.transpose(0, 2, 1, 3).reshape(modes, 5, 2, STRIPES, LANES)
    rows = rows.transpose(0, 1, 3, 2, 4).reshape(modes, stride, LANES)
    positions = mode_table[:, 0] * NB + mode_table[:, 1]
    forward, backward = (jnp.asarray(matrix) for matrix in beta_matrices())
    table = jnp.asarray(omega_table())
    derivative = derivative_matrix(wall_operator, index % 2)
    solve = solve_matrices(slab_map, slab_inverse)
    beta_index = lax.dynamic_slice_in_dim(mode_table[:, 1], index * modes, modes)
    omega_index = lax.dynamic_slice_in_dim(mode_table[:, 0], index * modes, modes)
    signed = jnp.where(beta_index >= NB // 2, beta_index - NB, beta_index)
    wave = phase_gain * (2.0 * signed.astype(jnp.float32) / NB)
    frequency = omega_step * omega_index.astype(jnp.float32)
    wave = jnp.broadcast_to(wave[:, None], (modes, LANES))
    frequency = jnp.broadcast_to(frequency[:, None], (modes, LANES))
    couple = base_coupling.reshape(25 * STRIPES, LANES)

    def variables(count, place, shift):
        return pl.BlockSpec((TILE, count * 2 * STRIPES, LANES), lambda i: (i + shift, place, 0))

    half = tiles // 2
    (sent_first,) = call(
        pack_first,
        [rows] * 4,
        [(groups, 3, modes // 2, LANES)],
        [],
        cost=10**8,
        grid=(half,),
        in_specs=[variables(2, 1, 0), variables(2, 1, half), variables(1, 4, 0), variables(1, 4, half)],
        out_specs=[pl.BlockSpec((groups, 3, TILE, LANES), lambda i: (0, 0, i, 0))],
    )
    first = exchange(sent_first.reshape(groups, first_rows, LANES))
    (sent_second,) = call(
        pack_second,
        [rows],
        [(groups, modes, LANES)],
        [],
        cost=10**8,
        grid=(tiles,),
        in_specs=[variables(2, 0, 0)],
        out_specs=[pl.BlockSpec((groups, TILE, LANES), lambda i: (0, i, 0))],
    )
    second = exchange(sent_second)
    first, derivative, solve, wave, frequency, couple, positions = lax.optimization_barrier(
        (first, derivative, solve, wave, frequency, couple, positions)
    )

    grid = vmem(M, LANES)
    spectrum = vmem(NW, 2 * NB, LANES)
    folded = vmem(TIMES, NB, LANES)
    turned = vmem(groups, modes // 2, LANES)
    physical = (TIMES, NB, LANES)
    half_physical = (TIMES, NB // 2, LANES)
    f1, g1, f_last, g_last, mean = call(
        functools.partial(synthesis, True),
        [positions, first, forward, table],
        [physical, physical, half_physical, half_physical, (8, LANES)],
        [grid, spectrum, turned],
        scalars=1,
        cost=3 * 10**9,
    )
    s1 = lax.ppermute(f1, "modes", neighbours)
    s_last = lax.ppermute(f_last, "modes", neighbours)
    (back_first,) = call(
        functools.partial(force_analysis, True),
        [positions, f1, f1, s1, g1, derivative, backward, table, f_last, s_last, g_last, mean],
        [(groups, first_rows + 8, LANES)],
        [folded, folded, grid, turned],
        scalars=1,
        cost=3 * 10**9,
    )
    got_first = exchange(back_first)
    f2, g2 = call(
        functools.partial(synthesis, False),
        [positions, second, forward, table],
        [physical, physical],
        [grid, spectrum],
        scalars=1,
        cost=2 * 10**9,
    )
    s2 = lax.ppermute(f2, "modes", neighbours)
    (back_second,) = call(
        functools.partial(force_analysis, False),
        [positions, f1, f2, s2, g2, derivative, backward, table],
        [(groups, modes, LANES)],
        [folded, folded, grid],
        scalars=1,
        cost=2 * 10**9,
    )
    got_second = exchange(back_second)

    stacked = TILE * PARTS
    state = (STRIPES * PARTS, modes, LANES)
    state_spec = pl.BlockSpec((STRIPES * PARTS, TILE, LANES), lambda i: (0, i, 0))
    returned_spec = pl.BlockSpec((groups, TILE, LANES), lambda i: (0, i, 0))
    last_spec = pl.BlockSpec((groups, TILE, LANES), lambda i: (0, tiles + i % half, 0))
    mean_spec = pl.BlockSpec((groups, 8, LANES), lambda i: (0, first_rows // 8, 0))
    mode_spec = pl.BlockSpec((TILE, LANES), lambda i: (i, 0))
    all_spec = pl.BlockSpec((TILE, stride, LANES), lambda i: (i, 0, 0))
    halves = [vmem(STRIPES, stacked, LANES, dtype=jnp.bfloat16)] * 2 + [vmem(stacked, LANES, dtype=jnp.bfloat16)] * 2
    solve_spec = fixed(*solve.shape)
    start, iterate, cross = call(
        relax_first,
        [rows, got_first, got_first, got_first, base_flow.reshape(STRIPES, LANES), couple, wave, frequency, solve],
        [state, state, (8, LANES)],
        halves,
        cost=2 * 10**9,
        grid=(tiles,),
        in_specs=[
            all_spec,
            returned_spec,
            last_spec,
            mean_spec,
            fixed(STRIPES, LANES),
            fixed(*couple.shape),
            mode_spec,
            mode_spec,
            solve_spec,
        ],
        out_specs=[state_spec, state_spec, fixed(8, LANES)],
    )
    (out,) = call(
        relax_last,
        [start, iterate, got_second, cross, couple, wave, frequency, solve],
        [(modes, stride, LANES)],
        [vmem(STRIPES * PARTS, TILE, LANES)] * 2 + halves,
        cost=2 * 10**9,
        grid=(tiles,),
        in_specs=[
            state_spec,
            state_spec,
            returned_spec,
            fixed(8, LANES),
            fixed(*couple.shape),
            mode_spec,
            mode_spec,
            solve_spec,
        ],
        out_specs=[all_spec],
    )
    out = out.reshape(modes, 5, STRIPES, 2, LANES).transpose(0, 1, 3, 2, 4).reshape(modes, 5, 2, points)
    return out.transpose(0, 2, 1, 3)


def local_any(amplitudes, mode_table, slab_map, base_flow, base_coupling, slab_inverse, wall_operator):
    points = amplitudes.shape[3]
    fits = points == STRIPES * LANES and points // lax.axis_size("modes") == SHARE
    fits = fits and slab_inverse.shape == (2 * STRIPES, SLAB, SLAB) and amplitudes.shape[0] % (2 * ROWS) == 0
    chosen = local_halves if fits else local
    return chosen(amplitudes, mode_table, slab_map, base_flow, base_coupling, slab_inverse, wall_operator)


def solution(mesh):
    return jax.shard_map(
        local_any,
        mesh=mesh,
        in_specs=(
            P(("runs", "modes"), None, None, None),
            P(),
            P(),
            P("runs"),
            P("runs", None),
            P(),
            P(),
        ),
        out_specs=P(("runs", "modes"), None, None, None),
        check_vma=False,
    )
```

```python
import functools
import math

import jax
import jax.numpy as jnp
import numpy as np
from jax import lax
from jax.experimental import pallas as pl
from jax.experimental.pallas import tpu as pltpu
from jax.sharding import PartitionSpec as P

M = 4096
NB = 128
SWEEPS = 3
NW = 32


precise = lax.Precision.HIGHEST
omega_step = 0.01
phase_gain = 0.2
march_step = 0.2
coupling = 0.3


def twiddle(length):
    counter = jnp.arange(length, dtype=jnp.int32)
    product = counter[:, None] * counter[None, :] % length
    angles = product.astype(jnp.float32) * (2.0 * math.pi / length)
    return (jnp.cos(angles), jnp.sin(angles))


def mode_tables(mode_table):
    omega_index = mode_table[:, 0]
    beta_index = mode_table[:, 1]
    signed = jnp.where(beta_index >= NB // 2, beta_index - NB, beta_index)
    wavenum = 2.0 * signed.astype(jnp.float32) / NB
    frequency = omega_step * omega_index.astype(jnp.float32)
    grid_pos = omega_index * NB + beta_index
    mode_at = jnp.zeros((M,), jnp.int32).at[grid_pos].set(jnp.arange(M, dtype=jnp.int32))
    return (wavenum, frequency, grid_pos, mode_at)


def synthesize(real_part, imag_part, tables, factor):
    cos_omega, sin_omega, cos_beta, sin_beta = tables
    mixed_re = jnp.einsum("...wb,bz->...wz", real_part, cos_beta, precision=precise) - jnp.einsum(
        "...wb,bz->...wz", imag_part, sin_beta, precision=precise
    )
    mixed_im = jnp.einsum("...wb,bz->...wz", real_part, sin_beta, precision=precise) + jnp.einsum(
        "...wb,bz->...wz", imag_part, cos_beta, precision=precise
    )
    physical = jnp.einsum("...wz,wt->...tz", mixed_re, cos_omega, precision=precise) - jnp.einsum(
        "...wz,wt->...tz", mixed_im, sin_omega, precision=precise
    )
    return physical * factor


def analyze(physical, tables, factor):
    cos_omega, sin_omega, cos_beta, sin_beta = tables
    half_re = jnp.einsum("...tz,zb->...tb", physical, cos_beta, precision=precise)
    half_im = -jnp.einsum("...tz,zb->...tb", physical, sin_beta, precision=precise)
    coef_re = jnp.einsum("...tb,tw->...wb", half_re, cos_omega, precision=precise) + jnp.einsum(
        "...tb,tw->...wb", half_im, sin_omega, precision=precise
    )
    coef_im = jnp.einsum("...tb,tw->...wb", half_im, cos_omega, precision=precise) - jnp.einsum(
        "...tb,tw->...wb", half_re, sin_omega, precision=precise
    )
    return (coef_re * factor, coef_im * factor)


def forcing(normal_vel, spanwise_vel, wall_grad, span_grad, tables, factor):
    vel_v = synthesize(normal_vel[0], normal_vel[1], tables, factor)
    vel_w = synthesize(spanwise_vel[0], spanwise_vel[1], tables, factor)
    grad_y = synthesize(wall_grad[0], wall_grad[1], tables, factor)
    grad_z = synthesize(span_grad[0], span_grad[1], tables, factor)
    product = -(vel_v[None] * grad_y + vel_w[None] * grad_z)
    return analyze(product, tables, factor)


def wall_derivative(values, wall_operator):
    slab_width = wall_operator.shape[0]
    slab_count = values.shape[3] // slab_width
    blocks = values.reshape(values.shape[:3] + (slab_count, slab_width))
    return jnp.einsum("ij,abcsj->abcsi", wall_operator, blocks, precision=precise).reshape(
        values.shape
    )


def interface_table(slab_map, slab_count, slab_width):
    inverse = (
        jnp.zeros((slab_count,), jnp.int32)
        .at[slab_map]
        .set(jnp.arange(slab_count, dtype=jnp.int32))
    )
    position = jnp.arange(slab_count * slab_width, dtype=jnp.int32)
    slot_of = position // slab_width
    within = position % slab_width
    domain = inverse[slot_of]
    below = slab_map[jnp.maximum(domain - 1, 0)] * slab_width + (slab_width - 1)
    above = slab_map[jnp.minimum(domain + 1, slab_count - 1)] * slab_width
    lower_ok = (within == 0) & (domain > 0)
    upper_ok = (within == slab_width - 1) & (domain < slab_count - 1)
    source = jnp.where(lower_ok, below, jnp.where(upper_ok, above, 0))
    weight = (lower_ok | upper_ok).astype(jnp.float32)
    return (source, weight)


def relaxation(iterate, right_side, rotation, matrix, slab_inverse, source, weight):
    slab_count = slab_inverse.shape[0]
    slab_width = slab_inverse.shape[1]
    coupled = jnp.einsum("kjy,acjy->acky", matrix, iterate, precision=precise)
    applied = jnp.stack(
        [
            coupled[:, 0] - rotation[:, None, :] * iterate[:, 1],
            coupled[:, 1] + rotation[:, None, :] * iterate[:, 0],
        ],
        1,
    )
    rims = jnp.take(iterate, source, axis=3) * weight
    residual_in = right_side - applied + coupling * rims
    blocks = residual_in.reshape(iterate.shape[:3] + (slab_count, slab_width))
    return jnp.einsum("sij,acvsj->acvsi", slab_inverse, blocks, precision=precise).reshape(
        iterate.shape
    )


def local(amplitudes, mode_table, slab_map, base_flow, base_coupling, slab_inverse, wall_operator):
    local_modes = amplitudes.shape[0]
    wall_points = amplitudes.shape[3]
    groups = lax.axis_size("modes")
    point_share = wall_points // groups
    wavenum, frequency, grid_pos, mode_at = mode_tables(mode_table)
    first_mode = lax.axis_index("modes") * local_modes
    wave_local = lax.dynamic_slice_in_dim(wavenum, first_mode, local_modes)
    freq_local = lax.dynamic_slice_in_dim(frequency, first_mode, local_modes)
    tables = twiddle(NW) + twiddle(NB)
    factor = 1.0 / math.sqrt(M)
    source, weight = interface_table(slab_map, slab_inverse.shape[0], slab_inverse.shape[1])
    matrix = base_coupling.reshape(5, 5, wall_points)
    gradient = wall_derivative(amplitudes, wall_operator)
    span = jnp.stack(
        [
            -wave_local[:, None, None] * amplitudes[:, 1],
            wave_local[:, None, None] * amplitudes[:, 0],
        ],
        1,
    )
    fields = jnp.concatenate([amplitudes[:, :, 2:4], gradient, span], 2)
    field_count = fields.shape[2]
    channels = 2 * field_count
    outgoing = jnp.transpose(
        fields.reshape(local_modes, channels, groups, point_share), (1, 2, 3, 0)
    ).reshape(channels, groups, point_share * local_modes)
    incoming = lax.all_to_all(outgoing, "modes", split_axis=1, concat_axis=1, tiled=True)
    by_mode = jnp.transpose(
        incoming.reshape(channels, groups, point_share, local_modes), (0, 2, 1, 3)
    ).reshape(channels, point_share, M)
    gridded = by_mode[..., mode_at].reshape(2, field_count, point_share, NW, NB)
    normal_vel = gridded[:, 0]
    spanwise_vel = gridded[:, 1]
    wall_grad = gridded[:, 2:7]
    span_grad = gridded[:, 7:12]
    mean_crossflow = lax.all_gather(spanwise_vel[0, :, 0, 0], "modes", axis=0, tiled=True)
    coef_re, coef_im = forcing(normal_vel, spanwise_vel, wall_grad, span_grad, tables, factor)
    packed = jnp.stack([coef_re, coef_im], 0).reshape(10, point_share, M)[..., grid_pos]
    sendback = jnp.transpose(
        packed.reshape(10, point_share, groups, local_modes), (0, 2, 1, 3)
    ).reshape(10, groups, point_share * local_modes)
    returned = lax.all_to_all(sendback, "modes", split_axis=1, concat_axis=1, tiled=True)
    nonlinear = jnp.transpose(
        returned.reshape(10, groups, point_share, local_modes), (3, 0, 1, 2)
    ).reshape(local_modes, 2, 5, wall_points)
    crossflow = base_flow + mean_crossflow
    rotation = phase_gain * wave_local[:, None] * crossflow[None, :] - freq_local[:, None]
    right_side = amplitudes + march_step * nonlinear
    iterate = amplitudes
    for sweep_index in range(SWEEPS):
        iterate = relaxation(iterate, right_side, rotation, matrix, slab_inverse, source, weight)
    return iterate


LANES = 128
SHARE = 32
SLAB = 64
HALF = NW // 2
TIMES = HALF + 1
BLOCKS = LANES // SHARE
STRIPES = 4
PARTS = 10
TILE = 32
PACK_TILE = 64
MIB = 1024 * 1024


def roll(x, shift):
    return pltpu.roll(x, shift % LANES, x.ndim - 1)


def lane_index(shape):
    return lax.broadcasted_iota(jnp.int32, shape, len(shape) - 1)


def lane_masks(shape):
    lane = lane_index(shape)
    return (lane < 64, (lane & 32) == 0)


def real_sign(shape):
    return jnp.where(lane_index(shape) < 64, 1.0, -1.0).astype(jnp.float32)


def block_transpose(rows, low, even):
    r0, r1, r2, r3 = rows
    crossed = roll(jnp.where(low, r2, r0), 64)
    t0 = jnp.where(low, r0, crossed)
    t2 = jnp.where(low, crossed, r2)
    crossed = roll(jnp.where(low, r3, r1), 64)
    t1 = jnp.where(low, r1, crossed)
    t3 = jnp.where(low, crossed, r3)
    return (
        jnp.where(even, t0, roll(t1, 32)),
        jnp.where(even, roll(t0, 96), t1),
        jnp.where(even, t2, roll(t3, 32)),
        jnp.where(even, roll(t2, 96), t3),
    )


def split(x):
    high = x.astype(jnp.bfloat16)
    return high, (x - high.astype(jnp.float32)).astype(jnp.bfloat16)


def dot(a, b):
    return jnp.dot(a, b, preferred_element_type=jnp.float32)


def cosine_sine(inputs, length, table, sign, real):
    if length == 4:
        first, middle, last = inputs
        middle_re = middle * real
        total = first + last
        return [total + middle_re, (first - last) + (middle - middle_re), total - middle_re]
    step = NW // length
    quarter = length // 4
    even = cosine_sine(inputs[0::2], length // 2, table, sign, real)
    odd_inputs = [(a, inputs[a]) for a in range(1, length // 2, 2)]
    odd = []
    for t in range(quarter + 1):
        if t == 0:
            total = odd_inputs[0][1]
            for _, value in odd_inputs[1:]:
                total = total + value
            odd.append(total * real)
        elif t == quarter:
            total = odd_inputs[0][1]
            for a, value in odd_inputs[1:]:
                total = total + value if a % 4 == 1 else total - value
            odd.append(total - total * real)
        else:
            total = None
            for a, value in odd_inputs:
                term = table(a * t * step % NW) * value
                total = term if total is None else total + term
            odd.append(total)
    out = [None] * (length // 2 + 1)
    for t in range(quarter + 1):
        out[t] = even[t] + odd[t]
        out[length // 2 - t] = sign * (even[t] - odd[t])
    out[quarter] = even[quarter] + odd[quarter]
    return out


def spread(ref, offset):
    flat = ref.reshape(ref.shape[0] * ref.shape[1], LANES)
    return flat[pl.ds(offset, ref.shape[0], stride=ref.shape[1]), :]


def pack_pair(first, first_offset, second, second_offset, low, even):
    out = []
    for stripe in range(STRIPES):
        rows = []
        for part in range(2):
            rows.append(spread(first, first_offset + stripe * 2 + part))
            rows.append(spread(second, second_offset + stripe * 2 + part))
        out.extend(block_transpose(rows, low, even))
    return out


def pack_first(near_ref, far_ref, near_last_ref, far_last_ref, o_ref):
    low, even = lane_masks((PACK_TILE, LANES))
    pieces = (
        (near_ref, 0, near_ref, 2 * STRIPES),
        (far_ref, 0, far_ref, 2 * STRIPES),
        (near_last_ref, 0, far_last_ref, 0),
    )
    for place, piece in enumerate(pieces):
        for group, value in enumerate(pack_pair(*piece, low, even)):
            o_ref[group, place] = value


def pack_second(near_ref, o_ref):
    low, even = lane_masks((PACK_TILE, LANES))
    for group, value in enumerate(pack_pair(near_ref, 0, near_ref, 2 * STRIPES, low, even)):
        o_ref[group] = value


ROWS = 128


def loop(count, unroll, body):
    def step(i, carry):
        for j in range(unroll):
            body(i * unroll + j)
        return carry

    lax.fori_loop(0, count // unroll, step, 0)
    for i in range(count // unroll * unroll, count):
        body(i)


def lanes_constants():
    sign = real_sign((8, LANES))
    real = jnp.where(lane_index((8, LANES)) < 64, 1.0, 0.0).astype(jnp.float32)
    even = (lane_index((8, LANES)) & 32) == 0
    return sign, real, even


def pair_left(even, near, far):
    return jnp.where(even, near, roll(far, 32))


def pair_right(even, near, far):
    return jnp.where(even, roll(near, 96), far)


def scatter(pos_ref, grid_ref, cell, source, group, row):
    for j in range(ROWS):
        grid_ref[pl.ds(pos_ref[cell + j], 1), :] = source[group, pl.ds(row + j, 1), :]


def synthesis_beta(w_ref, first, second):
    wide_sign = real_sign((NB, LANES))
    columns = [jnp.concatenate([x, -wide_sign * roll(x, 64)], 0) for x in (first, second)]
    high, low_part = split(jnp.concatenate(columns, 1))
    product = dot(w_ref[...], high)
    out = product[: 2 * NB] + product[2 * NB :] + dot(w_ref[pl.ds(0, 2 * NB), :], low_part)
    return out[:, :LANES], out[:, LANES:]


def synthesis(with_mean, pos_ref, r_ref, w_ref, tab_ref, *refs):
    if with_mean:
        f_ref, g_ref, mean_ref, grid_ref, spec_ref = refs
    else:
        f_ref, g_ref, grid_ref, spec_ref = refs
    groups = r_ref.shape[0]
    modes = M // groups
    sign, real, _ = lanes_constants()

    def table(j):
        return tab_ref[j]

    def grid(a):
        return grid_ref[pl.ds(pl.multiple_of(a * NB, NB), NB), :]

    def both_halves(i):
        group = i // (modes // ROWS)
        start = pl.multiple_of(i % (modes // ROWS) * ROWS, ROWS)
        scatter(pos_ref, grid_ref, i * ROWS, r_ref, group, start)

    loop(groups * (modes // ROWS), 1, both_halves)
    if with_mean:
        mean_ref[...] = grid_ref[pl.ds(0, 8), :]

    def beta(i):
        spec_ref[2 * i], spec_ref[2 * i + 1] = synthesis_beta(w_ref, grid(2 * i), grid(2 * i + 1))

    loop(NW // 2, 2, beta)

    def omega(out_ref, shift):
        def body(i):
            rows = pl.ds(pl.multiple_of(i * 8, 8), 8)
            source = pl.ds(pl.multiple_of(shift + i * 8, 8), 8)
            inputs = [spec_ref[0, source, :] * real]
            for a in range(1, HALF):
                inputs.append(spec_ref[a, source, :] + sign * spec_ref[NW - a, source, :])
            inputs.append(spec_ref[HALF, source, :] * real)
            for t, value in enumerate(cosine_sine(inputs, NW, table, sign, real)):
                out_ref[t, rows, :] = value - sign * roll(value, 64)

        loop(NB // 8, 2, body)

    omega(f_ref, 0)
    omega(g_ref, NB)


def synthesis_half(pos_ref, r_ref, w_ref, tab_ref, f_ref, g_ref, grid_ref, spec_ref, turned_ref):
    groups = r_ref.shape[0]
    modes = M // groups
    sign, real, even = lanes_constants()
    wide_even = (lane_index((NB, LANES)) & 32) == 0

    def table(j):
        return tab_ref[j]

    def grid(a):
        return grid_ref[pl.ds(pl.multiple_of(a * NB, NB), NB), :]

    def turn(group):
        turned_ref[group] = roll(r_ref[group], 96)
        for block in range(modes // 2 // ROWS):
            cell = group * modes + block * ROWS
            scatter(pos_ref, grid_ref, cell, r_ref, group, block * ROWS)
            scatter(pos_ref, grid_ref, cell + modes // 2, turned_ref, group, block * ROWS)

    loop(groups, 1, turn)

    def beta(i):
        columns = [pair_left(wide_even, grid(a), grid(a + HALF)) for a in (2 * i, 2 * i + 1)]
        spec_ref[2 * i], spec_ref[2 * i + 1] = synthesis_beta(w_ref, *columns)

    loop(HALF // 2, 2, beta)

    def omega(out_ref, shift):
        def body(i):
            rows = pl.ds(pl.multiple_of(i * 8, 8), 8)
            near = pl.ds(pl.multiple_of(shift + i * 8, 8), 8)
            far = pl.ds(pl.multiple_of(shift + NB // 2 + i * 8, 8), 8)
            firsts = []
            seconds = []
            for a in range(HALF):
                pieces = (even, spec_ref[a, near, :], spec_ref[a, far, :])
                firsts.append(pair_left(*pieces))
                seconds.append(pair_right(*pieces))
            inputs = [firsts[0] * real]
            for a in range(1, HALF):
                inputs.append(firsts[a] + sign * seconds[HALF - a])
            inputs.append(seconds[0] * real)
            for t, value in enumerate(cosine_sine(inputs, NW, table, sign, real)):
                out_ref[t, rows, :] = value - sign * roll(value, 64)

        loop(NB // 16, 2, body)

    omega(f_ref, 0)
    omega(g_ref, NB)


def force_analysis(with_last, pos_ref, vw_ref, f_ref, s_ref, g_ref, d_ref, w_ref, tab_ref, *refs):
    if with_last:
        f_last_ref, s_last_ref, g_last_ref, o_ref, k_ref, r_ref, n_ref, turned_ref = refs
    else:
        mean_ref, o_ref, k_ref, r_ref, n_ref = refs
    groups = o_ref.shape[0]
    modes = M // groups
    sign, real, _ = lanes_constants()
    wide_sign = real_sign((NB, LANES))
    wide_real, wide_even = lane_masks((NB, LANES))
    half_rows = NB // 2

    def table(j):
        return tab_ref[j]

    def gather(group, mode, target, row):
        for j in range(ROWS):
            cell = pos_ref[group * modes + mode + j]
            target[group, pl.ds(row + j, 1), :] = n_ref[pl.ds(cell, 1), :]

    def force_of(t, rows, v, w, f, s, g):
        high, low_part = split(jnp.concatenate([f, s], 1))
        both = dot(high, d_ref[...])
        grad = both[:, :LANES] + both[:, LANES:] + dot(low_part, d_ref[:, :LANES])
        force = v * grad + w * g
        if t is None:
            return jnp.where(wide_real[:rows], force, 0.0)
        return force + wide_sign[:rows] * roll(force, 64)

    def full_product(t, alone=False):
        vw = vw_ref[t]
        v = pair_left(wide_even, vw, vw)
        w = pair_right(wide_even, vw, vw)
        k_ref[t] = force_of(None if alone else t, NB, v, w, f_ref[t], s_ref[t], g_ref[t])

    def products(product):
        product(0, True)
        product(HALF, True)
        loop(HALF - 1, 3, lambda i: product(i + 1))

    def omegas(tiles):
        def body(i):
            rows = pl.ds(pl.multiple_of(i * 8, 8), 8)
            inputs = [k_ref[t, rows, :] for t in range(TIMES)]
            for a, value in enumerate(cosine_sine(inputs, NW, table, sign, real)):
                r_ref[a, rows, :] = value

        loop(tiles, 2, body)

    def beta(columns):
        high, low_part = split(jnp.concatenate(columns, 1) if len(columns) > 1 else columns[0])
        both = dot(w_ref[...], high)
        out = both[: 2 * NB] + both[2 * NB :] + dot(w_ref[pl.ds(0, 2 * NB), :], low_part)
        result = []
        for j in range(len(columns)):
            cosine = out[:NB, j * LANES : (j + 1) * LANES]
            sine = roll(out[NB:, j * LANES : (j + 1) * LANES], 64)
            result.append((cosine + wide_sign * sine, wide_sign * cosine - sine))
        return result

    def store(a, plus, minus):
        mirror = (NW - a) % NW
        n_ref[pl.ds(pl.multiple_of(mirror * NB, NB), NB), :] = minus
        n_ref[pl.ds(pl.multiple_of(a * NB, NB), NB), :] = plus

    products(full_product)
    omegas(NB // 8)

    def full_beta(i):
        for j, (plus, minus) in enumerate(beta([r_ref[2 * i], r_ref[2 * i + 1]])):
            store(2 * i + j, plus, minus)

    loop(HALF // 2, 2, full_beta)
    store(HALF, *beta([r_ref[HALF]])[0])

    def both_halves(i):
        group = i // (modes // ROWS)
        start = pl.multiple_of(i % (modes // ROWS) * ROWS, ROWS)
        gather(group, start, o_ref, start)

    loop(groups * (modes // ROWS), 1, both_halves)
    if not with_last:
        for group in range(groups):
            o_ref[group, pl.ds(modes, 8), :] = mean_ref[...]
        return

    def half_product(t, alone=False):
        vw = vw_ref[t]
        near = vw[:half_rows]
        far = vw[half_rows:]
        v = pair_left(wide_even[:half_rows], near, far)
        w = pair_right(wide_even[:half_rows], near, far)
        k_ref[t, pl.ds(0, half_rows), :] = force_of(
            None if alone else t, half_rows, v, w, f_last_ref[t], s_last_ref[t], g_last_ref[t]
        )

    products(half_product)
    omegas(NB // 16)

    def half_columns(a):
        even = wide_even[:half_rows]
        pieces = (even, r_ref[a, pl.ds(0, half_rows), :], r_ref[a + 1, pl.ds(0, half_rows), :])
        return jnp.concatenate([pair_left(*pieces), pair_right(*pieces)], 0)

    def half_beta(i):
        for j, (plus, minus) in enumerate(beta([half_columns(4 * i), half_columns(4 * i + 2)])):
            a = 4 * i + 2 * j
            store(a, plus, minus)
            store(a + 1, roll(plus, 96), roll(minus, 96))

    loop(HALF // 4, 1, half_beta)
    last = r_ref[HALF, pl.ds(0, half_rows), :]
    store(HALF, *beta([jnp.concatenate([last, roll(last, 96)], 0)])[0])

    def turn(group):
        for block in range(modes // 2 // ROWS):
            gather(group, block * ROWS, o_ref, modes + block * ROWS)
            gather(group, modes // 2 + block * ROWS, turned_ref, block * ROWS)
        here = pl.ds(modes, modes // 2)
        near = o_ref[group, here, :]
        o_ref[group, here, :] = pair_left((lane_index(near.shape) & 32) == 0, near, turned_ref[group])

    loop(groups, 1, turn)


def find_rims(x_of, parts, zh_ref, zl_ref):
    lane = lane_index((TILE, LANES))
    edge = ((lane & 63) == 0) | ((lane & 63) == 63)
    for part in range(PARTS):
        rows = pl.ds(part * TILE, TILE)
        if part not in parts:
            zh_ref[rows, :] = zl_ref[rows, :] = jnp.zeros((TILE, LANES), jnp.bfloat16)
            continue
        rims = None
        for stripe in range(STRIPES):
            term = jnp.where(edge, x_of(stripe, part), 0.0)
            term = roll(term, 2 * stripe) if stripe else term
            rims = term if rims is None else rims + term
        zh_ref[rows, :], zl_ref[rows, :] = split(rims)


def three_pass(high, low_part, weights):
    both = dot(high, weights)
    return both[:, :LANES] + both[:, LANES:] + dot(low_part, weights[:, :LANES])


def relax(stripe, x_of, parts, cross, kz_ref, om_ref, coup_ref, sw_ref, rh_ref, rl_ref, zh_ref, zl_ref):
    values = {part: x_of(stripe, part) for part in parts}
    rotation = kz_ref[...] * cross - om_ref[...]
    for k in range(5):
        out_re = jnp.zeros((TILE, LANES), jnp.float32)
        out_im = out_re
        if 2 * k in values:
            out_re = rotation * values[2 * k + 1]
            out_im = -(rotation * values[2 * k])
        for j in range(5):
            if 2 * j not in values:
                continue
            weight = coup_ref[pl.ds((k * 5 + j) * STRIPES + stripe, 1), :]
            out_re = out_re - weight * values[2 * j]
            out_im = out_im - weight * values[2 * j + 1]
        for part, out in ((2 * k, out_re), (2 * k + 1, out_im)):
            rows = pl.ds(part * TILE, TILE)
            rh_ref[stripe, rows, :], rl_ref[stripe, rows, :] = split(out)
    high = jnp.concatenate([rh_ref[stripe], zh_ref[...]], 1)
    low_rows = jnp.concatenate([rl_ref[stripe], zl_ref[...]], 1)
    return three_pass(high, low_rows, sw_ref[stripe]).reshape(PARTS, TILE, LANES)


def relax_first(a_ref, b_ref, mean_ref, base_ref, coup_ref, kz_ref, om_ref, sw_ref, out_ref, cf_ref, right_ref, x_ref, *halves):
    rh_ref, rl_ref, zh_ref, zl_ref = halves
    low, even = lane_masks((TILE, LANES))
    block_of = lane_index((1, LANES)) // SHARE
    for stripe in range(STRIPES):
        total = base_ref[pl.ds(stripe, 1), :]
        for block in range(BLOCKS):
            row = mean_ref[stripe * BLOCKS + block, pl.ds(0, 1), :]
            total = total + jnp.where(block_of == block, roll(row, SHARE * (block - 1)), 0.0)
        cf_ref[pl.ds(stripe, 1), :] = total

    for stripe in range(STRIPES):
        groups = [stripe * BLOCKS + block for block in range(BLOCKS)]
        velocity = block_transpose([b_ref[group] for group in groups], low, even)
        gained = {4: velocity[0], 6: velocity[1], 5: velocity[2], 7: velocity[3]}
        for part in range(PARTS):
            value = spread(a_ref, part // 2 * 2 * STRIPES + stripe * 2 + part % 2)
            x_ref[stripe * PARTS + part] = value
            if part in gained:
                value = value + march_step * gained[part]
            rows = pl.ds(part * TILE, TILE)
            rh_ref[stripe, rows, :], rl_ref[stripe, rows, :] = split(value)
        solved = three_pass(rh_ref[stripe], rl_ref[stripe], sw_ref[stripe, pl.ds(0, LANES), :])
        right_ref[pl.ds(stripe * PARTS, PARTS)] = solved.reshape(PARTS, TILE, LANES)

    def x_of(stripe, part):
        return x_ref[stripe * PARTS + part]

    for sweep in range(SWEEPS):
        target = x_ref if sweep < SWEEPS - 1 else out_ref
        find_rims(x_of, range(PARTS), zh_ref, zl_ref)
        for stripe in range(STRIPES):
            here = pl.ds(stripe * PARTS, PARTS)
            cross = cf_ref[pl.ds(stripe, 1), :]
            new = relax(stripe, x_of, range(PARTS), cross, kz_ref, om_ref, coup_ref, sw_ref, *halves)
            target[here] = right_ref[here] + new


LATE = (0, 1, 2, 3, 8, 9)


def relax_last(first_ref, b_ref, t_ref, cf_ref, coup_ref, kz_ref, om_ref, sw_ref, o_ref, right_ref, x_ref, *halves):
    rh_ref, rl_ref, zh_ref, zl_ref = halves
    low, even = lane_masks((TILE, LANES))
    far = pl.program_id(0) >= pl.num_programs(0) // 2
    count = len(LATE)
    for stripe in range(STRIPES):
        groups = [stripe * BLOCKS + block for block in range(BLOCKS)]
        pair = block_transpose([b_ref[group] for group in groups], low, even)
        last = block_transpose([t_ref[group] for group in groups], low, even)
        last = (jnp.where(far, last[1], last[0]), jnp.where(far, last[3], last[2]))
        for place, value in enumerate((pair[0], pair[2], pair[1], pair[3]) + last):
            rows = pl.ds(place * TILE, TILE)
            rh_ref[stripe, rows, :], rl_ref[stripe, rows, :] = split(march_step * value)
        rows = pl.ds(0, count * TILE)
        weights = sw_ref[stripe, pl.ds(0, LANES), :]
        added = three_pass(rh_ref[stripe, rows, :], rl_ref[stripe, rows, :], weights)
        right_ref[stripe] = added.reshape(count, TILE, LANES)

    def right_of(stripe, part):
        return right_ref[stripe, LATE.index(part)]

    def x_of(stripe, part):
        return x_ref[stripe * PARTS + part]

    flat = o_ref.reshape(TILE * PARTS * STRIPES, LANES)
    for sweep in range(1, SWEEPS):
        source, parts = (right_of, LATE) if sweep == 1 else (x_of, range(PARTS))
        find_rims(source, parts, zh_ref, zl_ref)
        for stripe in range(STRIPES):
            cross = cf_ref[pl.ds(stripe, 1), :]
            new = relax(stripe, source, parts, cross, kz_ref, om_ref, coup_ref, sw_ref, *halves)
            for part in range(PARTS):
                value = new[part] + right_of(stripe, part) if part in LATE else new[part]
                if sweep < SWEEPS - 1:
                    x_ref[stripe * PARTS + part] = value
                    continue
                offset = part // 2 * 2 * STRIPES + stripe * 2 + part % 2
                value = value + first_ref[stripe * PARTS + part]
                flat[pl.ds(offset, TILE, stride=PARTS * STRIPES), :] = value


def split_host(x):
    high = x.astype(jnp.bfloat16)
    low_part = (x - high.astype(np.float64)).astype(jnp.bfloat16)
    return high, low_part


def beta_matrices():
    index = np.arange(NB)
    angles = (index[:, None] * index[None, :] % NB) * (2.0 * math.pi / NB)
    cosine = np.cos(angles)
    sine = np.sin(angles)
    wave = 2.0 * np.where(index >= NB // 2, index - NB, index) / NB
    factor = 1.0 / math.sqrt(M)
    forward = factor * np.block([[cosine, sine], [-sine * wave, cosine * wave]])
    backward = -factor * np.concatenate([cosine, sine], 0)
    return tuple(np.concatenate(split_host(matrix), 0) for matrix in (forward, backward))


def omega_table():
    angles = np.arange(NW) * (2.0 * math.pi / NW)
    rows = np.concatenate([np.repeat(np.cos(angles)[:, None], 64, 1), np.repeat(np.sin(angles)[:, None], 64, 1)], 1)
    return np.repeat(rows[:, None, :], 8, 1).astype(np.float32)


def split_device(x):
    high = lax.reduce_precision(x, 8, 7)
    return high.astype(jnp.bfloat16), (x - high).astype(jnp.bfloat16)


def derivative_matrix(wall_operator, half):
    own = lax.dynamic_slice(wall_operator, (half * SHARE, 0), (SHARE, SLAB)).T
    mine = lax.dynamic_slice(own, (half * SHARE, 0), (SHARE, SHARE))
    other = lax.dynamic_slice(own, ((1 - half) * SHARE, 0), (SHARE, SHARE))
    same = jnp.eye(BLOCKS, dtype=jnp.float32)
    stacked = jnp.stack([mine, other], 0)
    full = same[None, :, None, :, None] * stacked[:, None, :, None, :]
    full = full.reshape(2 * LANES, LANES)
    return jnp.concatenate(split_device(full), 1)


def solve_matrices(slab_map, slab_inverse):
    count = slab_inverse.shape[0]
    slots = jnp.arange(count, dtype=jnp.int32)
    holds = slab_map[:, None] == slots[None, :]
    below_of = jnp.concatenate([slab_map[:1] * 0 - 1, slab_map[:-1]])
    above_of = jnp.concatenate([slab_map[1:], slab_map[:1] * 0 - 1])
    below = jnp.sum(jnp.where(holds, below_of[:, None], 0), 0)
    above = jnp.sum(jnp.where(holds, above_of[:, None], 0), 0)
    lane = jnp.arange(LANES, dtype=jnp.int32)

    def one_hot(slot, position):
        where = (slot % 2 * SLAB + position + 2 * (slot // 2)) % LANES
        return ((slot >= 0)[:, None] & (where[:, None] == lane[None, :])).astype(jnp.float32)

    low_rim = one_hot(below, SLAB - 1)
    high_rim = one_hot(above, 0)
    rims = coupling * (
        low_rim[:, :, None] * slab_inverse[:, None, :, 0] + high_rim[:, :, None] * slab_inverse[:, None, :, SLAB - 1]
    )
    rims = rims.reshape(STRIPES, 2, LANES, SLAB).transpose(0, 2, 1, 3).reshape(STRIPES, LANES, LANES)
    same = jnp.eye(2, dtype=jnp.float32)
    turned = slab_inverse.transpose(0, 2, 1).reshape(STRIPES, 2, SLAB, SLAB)
    blocks = same[None, :, None, :, None] * turned[:, :, :, None, :]
    blocks = blocks.reshape(STRIPES, LANES, LANES)
    return jnp.concatenate(split_device(jnp.concatenate([blocks, rims], 1)), 2)


def call(kernel, inputs, outputs, scratch, scalars=0, cost=0, limit=60, grid=None, in_specs=None, out_specs=None):
    whole = pl.BlockSpec(memory_space=pltpu.VMEM)
    if in_specs is None:
        in_specs = [pl.BlockSpec(memory_space=pltpu.SMEM)] * scalars + [whole] * (len(inputs) - scalars)
    if out_specs is None:
        out_specs = [whole] * len(outputs)
    extra = {} if grid is None else {"grid": grid}
    return pl.pallas_call(
        kernel,
        out_shape=[jax.ShapeDtypeStruct(shape, jnp.float32) for shape in outputs],
        in_specs=in_specs,
        out_specs=out_specs,
        scratch_shapes=scratch,
        compiler_params=pltpu.CompilerParams(vmem_limit_bytes=limit * MIB),
        cost_estimate=pl.CostEstimate(flops=cost, bytes_accessed=8 << 20, transcendentals=0),
        **extra,
    )(*inputs)


def vmem(*shape, dtype=jnp.float32):
    return pltpu.VMEM(shape, dtype)


def fixed(*shape):
    return pl.BlockSpec(shape, lambda i: (0,) * len(shape))


def local_halves(amplitudes, mode_table, slab_map, base_flow, base_coupling, slab_inverse, wall_operator):
    modes = amplitudes.shape[0]
    points = amplitudes.shape[3]
    groups = lax.axis_size("modes")
    index = lax.axis_index("modes")
    exchange = functools.partial(lax.all_to_all, axis_name="modes", split_axis=0, concat_axis=0, tiled=True)
    neighbours = [(j, j ^ 1) for j in range(groups)]
    stride = PARTS * STRIPES
    tiles = modes // TILE
    first_rows = modes // 2 * 3

    rows = amplitudes.transpose(0, 2, 1, 3).reshape(modes, 5, 2, STRIPES, LANES)
    rows = rows.transpose(0, 1, 3, 2, 4).reshape(modes, stride, LANES)
    positions = mode_table[:, 0] * NB + mode_table[:, 1]
    forward, backward = (jnp.asarray(matrix) for matrix in beta_matrices())
    table = jnp.asarray(omega_table())
    derivative = derivative_matrix(wall_operator, index % 2)
    solve = solve_matrices(slab_map, slab_inverse)
    beta_index = lax.dynamic_slice_in_dim(mode_table[:, 1], index * modes, modes)
    omega_index = lax.dynamic_slice_in_dim(mode_table[:, 0], index * modes, modes)
    signed = jnp.where(beta_index >= NB // 2, beta_index - NB, beta_index)
    wave = phase_gain * (2.0 * signed.astype(jnp.float32) / NB)
    frequency = omega_step * omega_index.astype(jnp.float32)
    wave = jnp.broadcast_to(wave[:, None], (modes, LANES))
    frequency = jnp.broadcast_to(frequency[:, None], (modes, LANES))
    couple = base_coupling.reshape(25 * STRIPES, LANES)

    def variables(count, place, shift):
        return pl.BlockSpec((PACK_TILE, count * 2 * STRIPES, LANES), lambda i: (i + shift, place, 0))

    half = modes // PACK_TILE // 2
    (sent_first,) = call(
        pack_first,
        [rows] * 4,
        [(groups, 3, modes // 2, LANES)],
        [],
        cost=10**8,
        grid=(half,),
        in_specs=[variables(2, 1, 0), variables(2, 1, half), variables(1, 4, 0), variables(1, 4, half)],
        out_specs=[pl.BlockSpec((groups, 3, PACK_TILE, LANES), lambda i: (0, 0, i, 0))],
    )
    first = exchange(sent_first.reshape(groups, first_rows, LANES))
    (sent_second,) = call(
        pack_second,
        [rows],
        [(groups, modes, LANES)],
        [],
        cost=10**8,
        grid=(modes // PACK_TILE,),
        in_specs=[variables(2, 0, 0)],
        out_specs=[pl.BlockSpec((groups, PACK_TILE, LANES), lambda i: (0, i, 0))],
    )
    sent_second, derivative, solve, wave, frequency, couple, positions = lax.optimization_barrier(
        (sent_second, derivative, solve, wave, frequency, couple, positions)
    )
    second = exchange(sent_second)

    grid = vmem(M, LANES)
    spectrum = vmem(NW, 2 * NB, LANES)
    folded = vmem(TIMES, NB, LANES)
    turned = vmem(groups, modes // 2, LANES)
    physical = (TIMES, NB, LANES)
    half_physical = (TIMES, NB // 2, LANES)
    scalars = pl.BlockSpec(memory_space=pltpu.SMEM)

    def spectral(kernel, received, count, place, outputs, scratch, cost):
        block = pl.BlockSpec((groups, count, LANES), lambda i: (0, place, 0))
        return call(
            kernel,
            [positions, received, forward, table],
            outputs,
            scratch,
            cost=cost,
            grid=(1,),
            in_specs=[scalars, block, fixed(*forward.shape), fixed(*table.shape)],
            out_specs=[fixed(*shape) for shape in outputs],
        )

    f1, g1, mean = spectral(
        functools.partial(synthesis, True), first, modes, 0, [physical, physical, (8, LANES)], [grid, spectrum], 2 * 10**9
    )
    s1 = lax.ppermute(f1, "modes", neighbours)
    f_last, g_last = spectral(
        synthesis_half, first, modes // 2, 2, [half_physical] * 2, [grid, spectrum, turned], 10**9
    )
    s1, f_last, g_last = lax.optimization_barrier((s1, f_last, g_last))
    s_last = lax.ppermute(f_last, "modes", neighbours)
    (back_first,) = call(
        functools.partial(force_analysis, False),
        [positions, f1, f1, s1, g1, derivative, backward, table, mean],
        [(groups, modes + 8, LANES)],
        [folded, folded, grid],
        scalars=1,
        cost=2 * 10**9,
    )
    got_first = exchange(back_first)
    f2, g2 = spectral(
        functools.partial(synthesis, False), second, modes, 0, [physical, physical], [grid, spectrum], 2 * 10**9
    )
    s2 = lax.ppermute(f2, "modes", neighbours)
    (back_second,) = call(
        functools.partial(force_analysis, True),
        [positions, f1, f2, s2, g2, derivative, backward, table, f_last, s_last, g_last],
        [(groups, first_rows, LANES)],
        [folded, folded, grid, turned],
        scalars=1,
        cost=3 * 10**9,
    )
    got_second = exchange(back_second)

    stacked = TILE * PARTS
    state = (STRIPES * PARTS, modes, LANES)
    state_spec = pl.BlockSpec((STRIPES * PARTS, TILE, LANES), lambda i: (0, i, 0))
    returned_spec = pl.BlockSpec((groups, TILE, LANES), lambda i: (0, i, 0))
    last_spec = pl.BlockSpec((groups, TILE, LANES), lambda i: (0, tiles + i % (tiles // 2), 0))
    mean_spec = pl.BlockSpec((groups, 8, LANES), lambda i: (0, modes // 8, 0))
    mode_spec = pl.BlockSpec((TILE, LANES), lambda i: (i, 0))
    all_spec = pl.BlockSpec((TILE, stride, LANES), lambda i: (i, 0, 0))
    halves = [vmem(STRIPES, stacked, LANES, dtype=jnp.bfloat16)] * 2 + [vmem(stacked, LANES, dtype=jnp.bfloat16)] * 2
    shared_specs = [fixed(*couple.shape), mode_spec, mode_spec, fixed(*solve.shape)]
    shared = [couple, wave, frequency, solve]
    iterate, cross = call(
        relax_first,
        [rows, got_first, got_first, base_flow.reshape(STRIPES, LANES)] + shared,
        [state, (8, LANES)],
        [vmem(STRIPES * PARTS, TILE, LANES)] * 2 + halves,
        cost=3 * 10**9,
        grid=(tiles,),
        in_specs=[all_spec, returned_spec, mean_spec, fixed(STRIPES, LANES)] + shared_specs,
        out_specs=[state_spec, fixed(8, LANES)],
    )
    (out,) = call(
        relax_last,
        [iterate, got_second, got_second, cross] + shared,
        [(modes, stride, LANES)],
        [vmem(STRIPES, len(LATE), TILE, LANES), vmem(STRIPES * PARTS, TILE, LANES)] + halves,
        cost=2 * 10**9,
        grid=(tiles,),
        in_specs=[state_spec, returned_spec, last_spec, fixed(8, LANES)] + shared_specs,
        out_specs=[all_spec],
    )
    out = out.reshape(modes, 5, STRIPES, 2, LANES).transpose(0, 1, 3, 2, 4).reshape(modes, 5, 2, points)
    return out.transpose(0, 2, 1, 3)


def local_any(amplitudes, mode_table, slab_map, base_flow, base_coupling, slab_inverse, wall_operator):
    points = amplitudes.shape[3]
    fits = points == STRIPES * LANES and points // lax.axis_size("modes") == SHARE
    fits = fits and slab_inverse.shape == (2 * STRIPES, SLAB, SLAB) and amplitudes.shape[0] % (2 * ROWS) == 0
    chosen = local_halves if fits else local
    return chosen(amplitudes, mode_table, slab_map, base_flow, base_coupling, slab_inverse, wall_operator)


def solution(mesh):
    return jax.shard_map(
        local_any,
        mesh=mesh,
        in_specs=(
            P(("runs", "modes"), None, None, None),
            P(),
            P(),
            P("runs"),
            P("runs", None),
            P(),
            P(),
        ),
        out_specs=P(("runs", "modes"), None, None, None),
        check_vma=False,
    )
```

```python
import functools
import math

import jax
import jax.numpy as jnp
import numpy as np
from jax import lax
from jax.experimental import pallas as pl
from jax.experimental.pallas import tpu as pltpu
from jax.sharding import PartitionSpec as P

M = 4096
NB = 128
SWEEPS = 3
NW = 32


precise = lax.Precision.HIGHEST
omega_step = 0.01
phase_gain = 0.2
march_step = 0.2
coupling = 0.3


def twiddle(length):
    counter = jnp.arange(length, dtype=jnp.int32)
    product = counter[:, None] * counter[None, :] % length
    angles = product.astype(jnp.float32) * (2.0 * math.pi / length)
    return (jnp.cos(angles), jnp.sin(angles))


def mode_tables(mode_table):
    omega_index = mode_table[:, 0]
    beta_index = mode_table[:, 1]
    signed = jnp.where(beta_index >= NB // 2, beta_index - NB, beta_index)
    wavenum = 2.0 * signed.astype(jnp.float32) / NB
    frequency = omega_step * omega_index.astype(jnp.float32)
    grid_pos = omega_index * NB + beta_index
    mode_at = jnp.zeros((M,), jnp.int32).at[grid_pos].set(jnp.arange(M, dtype=jnp.int32))
    return (wavenum, frequency, grid_pos, mode_at)


def synthesize(real_part, imag_part, tables, factor):
    cos_omega, sin_omega, cos_beta, sin_beta = tables
    mixed_re = jnp.einsum("...wb,bz->...wz", real_part, cos_beta, precision=precise) - jnp.einsum(
        "...wb,bz->...wz", imag_part, sin_beta, precision=precise
    )
    mixed_im = jnp.einsum("...wb,bz->...wz", real_part, sin_beta, precision=precise) + jnp.einsum(
        "...wb,bz->...wz", imag_part, cos_beta, precision=precise
    )
    physical = jnp.einsum("...wz,wt->...tz", mixed_re, cos_omega, precision=precise) - jnp.einsum(
        "...wz,wt->...tz", mixed_im, sin_omega, precision=precise
    )
    return physical * factor


def analyze(physical, tables, factor):
    cos_omega, sin_omega, cos_beta, sin_beta = tables
    half_re = jnp.einsum("...tz,zb->...tb", physical, cos_beta, precision=precise)
    half_im = -jnp.einsum("...tz,zb->...tb", physical, sin_beta, precision=precise)
    coef_re = jnp.einsum("...tb,tw->...wb", half_re, cos_omega, precision=precise) + jnp.einsum(
        "...tb,tw->...wb", half_im, sin_omega, precision=precise
    )
    coef_im = jnp.einsum("...tb,tw->...wb", half_im, cos_omega, precision=precise) - jnp.einsum(
        "...tb,tw->...wb", half_re, sin_omega, precision=precise
    )
    return (coef_re * factor, coef_im * factor)


def forcing(normal_vel, spanwise_vel, wall_grad, span_grad, tables, factor):
    vel_v = synthesize(normal_vel[0], normal_vel[1], tables, factor)
    vel_w = synthesize(spanwise_vel[0], spanwise_vel[1], tables, factor)
    grad_y = synthesize(wall_grad[0], wall_grad[1], tables, factor)
    grad_z = synthesize(span_grad[0], span_grad[1], tables, factor)
    product = -(vel_v[None] * grad_y + vel_w[None] * grad_z)
    return analyze(product, tables, factor)


def wall_derivative(values, wall_operator):
    slab_width = wall_operator.shape[0]
    slab_count = values.shape[3] // slab_width
    blocks = values.reshape(values.shape[:3] + (slab_count, slab_width))
    return jnp.einsum("ij,abcsj->abcsi", wall_operator, blocks, precision=precise).reshape(
        values.shape
    )


def interface_table(slab_map, slab_count, slab_width):
    inverse = (
        jnp.zeros((slab_count,), jnp.int32)
        .at[slab_map]
        .set(jnp.arange(slab_count, dtype=jnp.int32))
    )
    position = jnp.arange(slab_count * slab_width, dtype=jnp.int32)
    slot_of = position // slab_width
    within = position % slab_width
    domain = inverse[slot_of]
    below = slab_map[jnp.maximum(domain - 1, 0)] * slab_width + (slab_width - 1)
    above = slab_map[jnp.minimum(domain + 1, slab_count - 1)] * slab_width
    lower_ok = (within == 0) & (domain > 0)
    upper_ok = (within == slab_width - 1) & (domain < slab_count - 1)
    source = jnp.where(lower_ok, below, jnp.where(upper_ok, above, 0))
    weight = (lower_ok | upper_ok).astype(jnp.float32)
    return (source, weight)


def relaxation(iterate, right_side, rotation, matrix, slab_inverse, source, weight):
    slab_count = slab_inverse.shape[0]
    slab_width = slab_inverse.shape[1]
    coupled = jnp.einsum("kjy,acjy->acky", matrix, iterate, precision=precise)
    applied = jnp.stack(
        [
            coupled[:, 0] - rotation[:, None, :] * iterate[:, 1],
            coupled[:, 1] + rotation[:, None, :] * iterate[:, 0],
        ],
        1,
    )
    rims = jnp.take(iterate, source, axis=3) * weight
    residual_in = right_side - applied + coupling * rims
    blocks = residual_in.reshape(iterate.shape[:3] + (slab_count, slab_width))
    return jnp.einsum("sij,acvsj->acvsi", slab_inverse, blocks, precision=precise).reshape(
        iterate.shape
    )


def local(amplitudes, mode_table, slab_map, base_flow, base_coupling, slab_inverse, wall_operator):
    local_modes = amplitudes.shape[0]
    wall_points = amplitudes.shape[3]
    groups = lax.axis_size("modes")
    point_share = wall_points // groups
    wavenum, frequency, grid_pos, mode_at = mode_tables(mode_table)
    first_mode = lax.axis_index("modes") * local_modes
    wave_local = lax.dynamic_slice_in_dim(wavenum, first_mode, local_modes)
    freq_local = lax.dynamic_slice_in_dim(frequency, first_mode, local_modes)
    tables = twiddle(NW) + twiddle(NB)
    factor = 1.0 / math.sqrt(M)
    source, weight = interface_table(slab_map, slab_inverse.shape[0], slab_inverse.shape[1])
    matrix = base_coupling.reshape(5, 5, wall_points)
    gradient = wall_derivative(amplitudes, wall_operator)
    span = jnp.stack(
        [
            -wave_local[:, None, None] * amplitudes[:, 1],
            wave_local[:, None, None] * amplitudes[:, 0],
        ],
        1,
    )
    fields = jnp.concatenate([amplitudes[:, :, 2:4], gradient, span], 2)
    field_count = fields.shape[2]
    channels = 2 * field_count
    outgoing = jnp.transpose(
        fields.reshape(local_modes, channels, groups, point_share), (1, 2, 3, 0)
    ).reshape(channels, groups, point_share * local_modes)
    incoming = lax.all_to_all(outgoing, "modes", split_axis=1, concat_axis=1, tiled=True)
    by_mode = jnp.transpose(
        incoming.reshape(channels, groups, point_share, local_modes), (0, 2, 1, 3)
    ).reshape(channels, point_share, M)
    gridded = by_mode[..., mode_at].reshape(2, field_count, point_share, NW, NB)
    normal_vel = gridded[:, 0]
    spanwise_vel = gridded[:, 1]
    wall_grad = gridded[:, 2:7]
    span_grad = gridded[:, 7:12]
    mean_crossflow = lax.all_gather(spanwise_vel[0, :, 0, 0], "modes", axis=0, tiled=True)
    coef_re, coef_im = forcing(normal_vel, spanwise_vel, wall_grad, span_grad, tables, factor)
    packed = jnp.stack([coef_re, coef_im], 0).reshape(10, point_share, M)[..., grid_pos]
    sendback = jnp.transpose(
        packed.reshape(10, point_share, groups, local_modes), (0, 2, 1, 3)
    ).reshape(10, groups, point_share * local_modes)
    returned = lax.all_to_all(sendback, "modes", split_axis=1, concat_axis=1, tiled=True)
    nonlinear = jnp.transpose(
        returned.reshape(10, groups, point_share, local_modes), (3, 0, 1, 2)
    ).reshape(local_modes, 2, 5, wall_points)
    crossflow = base_flow + mean_crossflow
    rotation = phase_gain * wave_local[:, None] * crossflow[None, :] - freq_local[:, None]
    right_side = amplitudes + march_step * nonlinear
    iterate = amplitudes
    for sweep_index in range(SWEEPS):
        iterate = relaxation(iterate, right_side, rotation, matrix, slab_inverse, source, weight)
    return iterate


LANES = 128
SHARE = 32
SLAB = 64
HALF = NW // 2
TIMES = HALF + 1
BLOCKS = LANES // SHARE
STRIPES = 4
PARTS = 10
TILE = 64
PACK_TILE = 64
FIRST_TILE = 32
MIB = 1024 * 1024
LAST_LIMIT = 53


def roll(x, shift):
    return pltpu.roll(x, shift % LANES, x.ndim - 1)


def lane_index(shape):
    return lax.broadcasted_iota(jnp.int32, shape, len(shape) - 1)


def lane_masks(shape):
    lane = lane_index(shape)
    return (lane < 64, (lane & 32) == 0)


def real_sign(shape):
    return jnp.where(lane_index(shape) < 64, 1.0, -1.0).astype(jnp.float32)


def block_transpose(rows, low, even):
    r0, r1, r2, r3 = rows
    crossed = roll(jnp.where(low, r2, r0), 64)
    t0 = jnp.where(low, r0, crossed)
    t2 = jnp.where(low, crossed, r2)
    crossed = roll(jnp.where(low, r3, r1), 64)
    t1 = jnp.where(low, r1, crossed)
    t3 = jnp.where(low, crossed, r3)
    return (
        jnp.where(even, t0, roll(t1, 32)),
        jnp.where(even, roll(t0, 96), t1),
        jnp.where(even, t2, roll(t3, 32)),
        jnp.where(even, roll(t2, 96), t3),
    )


def split(x):
    high = x.astype(jnp.bfloat16)
    return high, (x - high.astype(jnp.float32)).astype(jnp.bfloat16)


def dot(a, b):
    return jnp.dot(a, b, preferred_element_type=jnp.float32)


def cosine_sine(inputs, length, table, sign, real):
    if length == 4:
        first, middle, last = inputs
        middle_re = middle * real
        total = first + last
        return [total + middle_re, (first - last) + (middle - middle_re), total - middle_re]
    step = NW // length
    quarter = length // 4
    even = cosine_sine(inputs[0::2], length // 2, table, sign, real)
    odd_inputs = [(a, inputs[a]) for a in range(1, length // 2, 2)]
    odd = []
    for t in range(quarter + 1):
        if t == 0:
            total = odd_inputs[0][1]
            for _, value in odd_inputs[1:]:
                total = total + value
            odd.append(total * real)
        elif t == quarter:
            total = odd_inputs[0][1]
            for a, value in odd_inputs[1:]:
                total = total + value if a % 4 == 1 else total - value
            odd.append(total - total * real)
        else:
            total = None
            for a, value in odd_inputs:
                term = table(a * t * step % NW) * value
                total = term if total is None else total + term
            odd.append(total)
    out = [None] * (length // 2 + 1)
    for t in range(quarter + 1):
        out[t] = even[t] + odd[t]
        out[length // 2 - t] = sign * (even[t] - odd[t])
    out[quarter] = even[quarter] + odd[quarter]
    return out


def spread(ref, offset):
    flat = ref.reshape(ref.shape[0] * ref.shape[1], LANES)
    return flat[pl.ds(offset, ref.shape[0], stride=ref.shape[1]), :]


def pack_pair(first, first_offset, second, second_offset, low, even):
    out = []
    for stripe in range(STRIPES):
        rows = []
        for part in range(2):
            rows.append(spread(first, first_offset + stripe * 2 + part))
            rows.append(spread(second, second_offset + stripe * 2 + part))
        out.extend(block_transpose(rows, low, even))
    return out


def pack_first(rows_ref, o_ref, in_ref, out_ref, in_sem, out_sem):
    tiles = in_ref.shape[0]
    count = in_ref.shape[1]
    wanted = pl.ds(2 * 2 * STRIPES, 3 * 2 * STRIPES)
    low, even = lane_masks((count, LANES))
    loads = []
    for tile in range(tiles):
        source = rows_ref.at[pl.ds(tile * count, count), wanted, :]
        loads.append(pltpu.make_async_copy(source, in_ref.at[tile], in_sem.at[tile]))
    half = tiles // 2
    for tile in range(half):
        loads[tile].start()
        loads[tile + half].start()
    stores = []
    for tile in range(half):
        loads[tile].wait()
        loads[tile + half].wait()
        near = in_ref.at[tile]
        far = in_ref.at[tile + half]
        pieces = (
            (near, 0, near, 2 * STRIPES),
            (far, 0, far, 2 * STRIPES),
            (near, 4 * STRIPES, far, 4 * STRIPES),
        )
        for place, piece in enumerate(pieces):
            for group, value in enumerate(pack_pair(*piece, low, even)):
                out_ref[tile, place, group] = value
            target = o_ref.at[:, pl.ds((place * half + tile) * count, count), :]
            store = pltpu.make_async_copy(out_ref.at[tile, place], target, out_sem.at[tile, place])
            store.start()
            stores.append(store)
    for store in stores:
        store.wait()


def pack_second(near_ref, o_ref):
    low, even = lane_masks((PACK_TILE, LANES))
    for group, value in enumerate(pack_pair(near_ref, 0, near_ref, 2 * STRIPES, low, even)):
        o_ref[group] = value


ROWS = 128


def loop(count, unroll, body):
    def step(i, carry):
        for j in range(unroll):
            body(i * unroll + j)
        return carry

    lax.fori_loop(0, count // unroll, step, 0)
    for i in range(count // unroll * unroll, count):
        body(i)


def lanes_constants():
    sign = real_sign((8, LANES))
    real = jnp.where(lane_index((8, LANES)) < 64, 1.0, 0.0).astype(jnp.float32)
    even = (lane_index((8, LANES)) & 32) == 0
    return sign, real, even


def pair_left(even, near, far):
    return jnp.where(even, near, roll(far, 32))


def pair_right(even, near, far):
    return jnp.where(even, roll(near, 96), far)


def scatter(pos_ref, grid_ref, cell, source, group, row):
    for j in range(ROWS):
        grid_ref[pl.ds(pos_ref[cell + j], 1), :] = source[group, pl.ds(row + j, 1), :]


def synthesis_beta(w_ref, first, second):
    wide_sign = real_sign((NB, LANES))
    columns = [jnp.concatenate([x, -wide_sign * roll(x, 64)], 0) for x in (first, second)]
    high, low_part = split(jnp.concatenate(columns, 1))
    product = dot(w_ref[...], high)
    out = product[: 2 * NB] + product[2 * NB :] + dot(w_ref[pl.ds(0, 2 * NB), :], low_part)
    return out[:, :LANES], out[:, LANES:]


def synthesis(with_mean, pos_ref, r_ref, w_ref, tab_ref, *refs):
    if with_mean:
        f_ref, g_ref, mean_ref, grid_ref, spec_ref = refs
    else:
        f_ref, g_ref, grid_ref, spec_ref = refs
    groups = r_ref.shape[0]
    modes = M // groups
    sign, real, _ = lanes_constants()

    def table(j):
        return tab_ref[j]

    def grid(a):
        return grid_ref[pl.ds(pl.multiple_of(a * NB, NB), NB), :]

    def both_halves(i):
        group = i // (modes // ROWS)
        start = pl.multiple_of(i % (modes // ROWS) * ROWS, ROWS)
        scatter(pos_ref, grid_ref, i * ROWS, r_ref, group, start)

    loop(groups * (modes // ROWS), 1, both_halves)
    if with_mean:
        mean_ref[...] = grid_ref[pl.ds(0, 8), :]

    def beta(i):
        spec_ref[2 * i], spec_ref[2 * i + 1] = synthesis_beta(w_ref, grid(2 * i), grid(2 * i + 1))

    loop(NW // 2, 2, beta)

    def omega(out_ref, shift):
        def body(i):
            rows = pl.ds(pl.multiple_of(i * 8, 8), 8)
            source = pl.ds(pl.multiple_of(shift + i * 8, 8), 8)
            inputs = [spec_ref[0, source, :] * real]
            for a in range(1, HALF):
                inputs.append(spec_ref[a, source, :] + sign * spec_ref[NW - a, source, :])
            inputs.append(spec_ref[HALF, source, :] * real)
            for t, value in enumerate(cosine_sine(inputs, NW, table, sign, real)):
                out_ref[t, rows, :] = value - sign * roll(value, 64)

        loop(NB // 8, 2, body)

    omega(f_ref, 0)
    omega(g_ref, NB)


def synthesis_half(pos_ref, r_ref, w_ref, tab_ref, f_ref, g_ref, grid_ref, spec_ref, turned_ref):
    groups = r_ref.shape[0]
    modes = M // groups
    sign, real, even = lanes_constants()
    wide_even = (lane_index((NB, LANES)) & 32) == 0

    def table(j):
        return tab_ref[j]

    def grid(a):
        return grid_ref[pl.ds(pl.multiple_of(a * NB, NB), NB), :]

    def turn(group):
        turned_ref[group] = roll(r_ref[group], 96)
        for block in range(modes // 2 // ROWS):
            cell = group * modes + block * ROWS
            scatter(pos_ref, grid_ref, cell, r_ref, group, block * ROWS)
            scatter(pos_ref, grid_ref, cell + modes // 2, turned_ref, group, block * ROWS)

    loop(groups, 1, turn)

    def beta(i):
        columns = [pair_left(wide_even, grid(a), grid(a + HALF)) for a in (2 * i, 2 * i + 1)]
        spec_ref[2 * i], spec_ref[2 * i + 1] = synthesis_beta(w_ref, *columns)

    loop(HALF // 2, 2, beta)

    def omega(out_ref, shift):
        def body(i):
            rows = pl.ds(pl.multiple_of(i * 8, 8), 8)
            near = pl.ds(pl.multiple_of(shift + i * 8, 8), 8)
            far = pl.ds(pl.multiple_of(shift + NB // 2 + i * 8, 8), 8)
            firsts = []
            seconds = []
            for a in range(HALF):
                pieces = (even, spec_ref[a, near, :], spec_ref[a, far, :])
                firsts.append(pair_left(*pieces))
                seconds.append(pair_right(*pieces))
            inputs = [firsts[0] * real]
            for a in range(1, HALF):
                inputs.append(firsts[a] + sign * seconds[HALF - a])
            inputs.append(seconds[0] * real)
            for t, value in enumerate(cosine_sine(inputs, NW, table, sign, real)):
                out_ref[t, rows, :] = value - sign * roll(value, 64)

        loop(NB // 16, 2, body)

    omega(f_ref, 0)
    omega(g_ref, NB)


def force_analysis(with_last, pos_ref, vw_ref, f_ref, s_ref, g_ref, d_ref, w_ref, tab_ref, *refs):
    if with_last:
        f_last_ref, s_last_ref, g_last_ref, o_ref, k_ref, r_ref, n_ref, turned_ref = refs
    else:
        mean_ref, o_ref, k_ref, r_ref, n_ref = refs
    groups = o_ref.shape[0]
    modes = M // groups
    sign, real, _ = lanes_constants()
    wide_sign = real_sign((NB, LANES))
    wide_real, wide_even = lane_masks((NB, LANES))
    half_rows = NB // 2

    def table(j):
        return tab_ref[j]

    def gather(group, mode, target, row):
        for j in range(ROWS):
            cell = pos_ref[group * modes + mode + j]
            target[group, pl.ds(row + j, 1), :] = n_ref[pl.ds(cell, 1), :]

    def force_of(t, rows, v, w, f, s, g):
        high, low_part = split(jnp.concatenate([f, s], 1))
        both = dot(high, d_ref[...])
        grad = both[:, :LANES] + both[:, LANES:] + dot(low_part, d_ref[:, :LANES])
        force = v * grad + w * g
        if t is None:
            return jnp.where(wide_real[:rows], force, 0.0)
        return force + wide_sign[:rows] * roll(force, 64)

    def full_product(t, alone=False):
        vw = vw_ref[t]
        v = pair_left(wide_even, vw, vw)
        w = pair_right(wide_even, vw, vw)
        k_ref[t] = force_of(None if alone else t, NB, v, w, f_ref[t], s_ref[t], g_ref[t])

    def products(product):
        product(0, True)
        product(HALF, True)
        loop(HALF - 1, 3, lambda i: product(i + 1))

    def omegas(tiles):
        def body(i):
            rows = pl.ds(pl.multiple_of(i * 8, 8), 8)
            inputs = [k_ref[t, rows, :] for t in range(TIMES)]
            for a, value in enumerate(cosine_sine(inputs, NW, table, sign, real)):
                r_ref[a, rows, :] = value

        loop(tiles, 2, body)

    def beta(columns):
        high, low_part = split(jnp.concatenate(columns, 1) if len(columns) > 1 else columns[0])
        both = dot(w_ref[...], high)
        out = both[: 2 * NB] + both[2 * NB :] + dot(w_ref[pl.ds(0, 2 * NB), :], low_part)
        result = []
        for j in range(len(columns)):
            cosine = out[:NB, j * LANES : (j + 1) * LANES]
            sine = roll(out[NB:, j * LANES : (j + 1) * LANES], 64)
            result.append((cosine + wide_sign * sine, wide_sign * cosine - sine))
        return result

    def store(a, plus, minus):
        mirror = (NW - a) % NW
        n_ref[pl.ds(pl.multiple_of(mirror * NB, NB), NB), :] = minus
        n_ref[pl.ds(pl.multiple_of(a * NB, NB), NB), :] = plus

    products(full_product)
    omegas(NB // 8)

    def full_beta(i):
        for j, (plus, minus) in enumerate(beta([r_ref[2 * i], r_ref[2 * i + 1]])):
            store(2 * i + j, plus, minus)

    loop(HALF // 2, 2, full_beta)
    store(HALF, *beta([r_ref[HALF]])[0])

    def both_halves(i):
        group = i // (modes // ROWS)
        start = pl.multiple_of(i % (modes // ROWS) * ROWS, ROWS)
        gather(group, start, o_ref, start)

    loop(groups * (modes // ROWS), 1, both_halves)
    if not with_last:
        for group in range(groups):
            o_ref[group, pl.ds(modes, 8), :] = mean_ref[...]
        return

    def half_product(t, alone=False):
        vw = vw_ref[t]
        near = vw[:half_rows]
        far = vw[half_rows:]
        v = pair_left(wide_even[:half_rows], near, far)
        w = pair_right(wide_even[:half_rows], near, far)
        k_ref[t, pl.ds(0, half_rows), :] = force_of(
            None if alone else t, half_rows, v, w, f_last_ref[t], s_last_ref[t], g_last_ref[t]
        )

    products(half_product)
    omegas(NB // 16)

    def half_columns(a):
        even = wide_even[:half_rows]
        pieces = (even, r_ref[a, pl.ds(0, half_rows), :], r_ref[a + 1, pl.ds(0, half_rows), :])
        return jnp.concatenate([pair_left(*pieces), pair_right(*pieces)], 0)

    def half_beta(i):
        for j, (plus, minus) in enumerate(beta([half_columns(4 * i), half_columns(4 * i + 2)])):
            a = 4 * i + 2 * j
            store(a, plus, minus)
            store(a + 1, roll(plus, 96), roll(minus, 96))

    loop(HALF // 4, 1, half_beta)
    last = r_ref[HALF, pl.ds(0, half_rows), :]
    store(HALF, *beta([jnp.concatenate([last, roll(last, 96)], 0)])[0])

    def turn(group):
        for block in range(modes // 2 // ROWS):
            gather(group, block * ROWS, o_ref, modes + block * ROWS)
            gather(group, modes // 2 + block * ROWS, turned_ref, block * ROWS)
        here = pl.ds(modes, modes // 2)
        near = o_ref[group, here, :]
        o_ref[group, here, :] = pair_left((lane_index(near.shape) & 32) == 0, near, turned_ref[group])

    loop(groups, 1, turn)


def find_rims(x_of, parts, zh_ref, zl_ref):
    lane = lane_index((TILE, LANES))
    edge = ((lane & 63) == 0) | ((lane & 63) == 63)
    for part in range(PARTS):
        rows = pl.ds(part * TILE, TILE)
        if part not in parts:
            zh_ref[rows, :] = zl_ref[rows, :] = jnp.zeros((TILE, LANES), jnp.bfloat16)
            continue
        rims = None
        for stripe in range(STRIPES):
            term = jnp.where(edge, x_of(stripe, part), 0.0)
            term = roll(term, 2 * stripe) if stripe else term
            rims = term if rims is None else rims + term
        zh_ref[rows, :], zl_ref[rows, :] = split(rims)


def three_pass(high, low_part, weights):
    both = dot(high, weights)
    return both[:, :LANES] + both[:, LANES:] + dot(low_part, weights[:, :LANES])


def relax(stripe, x_of, parts, cross, kz_ref, om_ref, coup_ref, sw_ref, rh_ref, rl_ref, zh_ref, zl_ref):
    values = {part: x_of(stripe, part) for part in parts}
    rotation = kz_ref[...] * cross - om_ref[...]
    for k in range(5):
        out_re = jnp.zeros((TILE, LANES), jnp.float32)
        out_im = out_re
        if 2 * k in values:
            out_re = rotation * values[2 * k + 1]
            out_im = -(rotation * values[2 * k])
        for j in range(5):
            if 2 * j not in values:
                continue
            weight = coup_ref[pl.ds((k * 5 + j) * STRIPES + stripe, 1), :]
            out_re = out_re - weight * values[2 * j]
            out_im = out_im - weight * values[2 * j + 1]
        for part, out in ((2 * k, out_re), (2 * k + 1, out_im)):
            rows = pl.ds(part * TILE, TILE)
            rh_ref[stripe, rows, :], rl_ref[stripe, rows, :] = split(out)
    high = jnp.concatenate([rh_ref[stripe], zh_ref[...]], 1)
    low_rows = jnp.concatenate([rl_ref[stripe], zl_ref[...]], 1)
    return three_pass(high, low_rows, sw_ref[stripe]).reshape(PARTS, TILE, LANES)


def relax_first(a_ref, b_ref, mean_ref, base_ref, coup_ref, kz_ref, om_ref, sw_ref, out_ref, right_ref, x_ref, cf_ref, *halves):
    rh_ref, rl_ref, zh_ref, zl_ref = halves
    low, even = lane_masks((TILE, LANES))
    block_of = lane_index((1, LANES)) // SHARE
    for stripe in range(STRIPES):
        total = base_ref[pl.ds(stripe, 1), :]
        for block in range(BLOCKS):
            row = mean_ref[stripe * BLOCKS + block, pl.ds(0, 1), :]
            total = total + jnp.where(block_of == block, roll(row, SHARE * (block - 1)), 0.0)
        cf_ref[pl.ds(stripe, 1), :] = total
    out_ref[0, STRIPES * PARTS, pl.ds(0, 8), :] = cf_ref[...]

    for stripe in range(STRIPES):
        groups = [stripe * BLOCKS + block for block in range(BLOCKS)]
        velocity = block_transpose([b_ref[group] for group in groups], low, even)
        gained = {4: velocity[0], 6: velocity[1], 5: velocity[2], 7: velocity[3]}
        for part in range(PARTS):
            value = spread(a_ref, part // 2 * 2 * STRIPES + stripe * 2 + part % 2)
            x_ref[stripe * PARTS + part] = value
            if part in gained:
                value = value + march_step * gained[part]
            rows = pl.ds(part * TILE, TILE)
            rh_ref[stripe, rows, :], rl_ref[stripe, rows, :] = split(value)
        solved = three_pass(rh_ref[stripe], rl_ref[stripe], sw_ref[stripe, pl.ds(0, LANES), :])
        right_ref[pl.ds(stripe * PARTS, PARTS)] = solved.reshape(PARTS, TILE, LANES)

    def x_of(stripe, part):
        return x_ref[stripe * PARTS + part]

    for sweep in range(SWEEPS):
        find_rims(x_of, range(PARTS), zh_ref, zl_ref)
        for stripe in range(STRIPES):
            here = pl.ds(stripe * PARTS, PARTS)
            cross = cf_ref[pl.ds(stripe, 1), :]
            new = relax(stripe, x_of, range(PARTS), cross, kz_ref, om_ref, coup_ref, sw_ref, *halves)
            if sweep < SWEEPS - 1:
                x_ref[here] = right_ref[here] + new
            else:
                out_ref[0, here] = right_ref[here] + new


LATE = (0, 1, 2, 3, 8, 9)


def relax_last(first_hbm, b_any, *refs):
    shared_hbm, o_hbm, (first_buf, b_buf, t_buf, o_buf), shared = refs[:4], refs[4], refs[5:9], refs[9:13]
    (in_sem, out_sem, shared_sem), scratch = refs[13:16], refs[16:]
    coup_ref, kz_ref, om_ref, sw_ref = shared
    tiles = first_buf.shape[0]
    modes = tiles * TILE

    def loads(i):
        pair = b_any.at[:, pl.ds(i * TILE, TILE), :]
        last = b_any.at[:, pl.ds(modes + i % (tiles // 2) * TILE, TILE), :]
        return (
            pltpu.make_async_copy(pair, b_buf.at[i], in_sem.at[0, i]),
            pltpu.make_async_copy(last, t_buf.at[i], in_sem.at[1, i]),
            pltpu.make_async_copy(first_hbm.at[i], first_buf.at[i], in_sem.at[2, i]),
        )

    def store(i):
        target = o_hbm.at[pl.ds(i * TILE, TILE), :, :]
        return pltpu.make_async_copy(o_buf.at[i], target, out_sem.at[i])

    ahead = 2
    fixed_loads = [
        pltpu.make_async_copy(source, target, shared_sem.at[place])
        for place, (source, target) in enumerate(zip(shared_hbm, shared))
    ]
    for load in fixed_loads:
        load.start()
    for i in range(ahead):
        for load in loads(i):
            load.start()
    for load in fixed_loads:
        load.wait()

    def body(i, carry):
        for load in loads(i):
            load.wait()

        @pl.when(i + ahead < tiles)
        def _():
            for load in loads(i + ahead):
                load.start()

        modes_here = pl.ds(pl.multiple_of(i * TILE, TILE), TILE)
        relax_tile(
            i >= tiles // 2,
            first_buf.at[i],
            b_buf.at[i],
            t_buf.at[i],
            first_buf.at[i, STRIPES * PARTS],
            coup_ref,
            kz_ref.at[modes_here, :],
            om_ref.at[modes_here, :],
            sw_ref,
            o_buf.at[i],
            *scratch,
        )
        store(i).start()
        return carry

    lax.fori_loop(0, tiles, body, 0)
    for i in range(tiles):
        store(i).wait()


def relax_tile(far, first_ref, b_ref, t_ref, cf_ref, coup_ref, kz_ref, om_ref, sw_ref, o_ref, right_ref, x_ref, *halves):
    rh_ref, rl_ref, zh_ref, zl_ref = halves
    low, even = lane_masks((TILE, LANES))
    count = len(LATE)
    for stripe in range(STRIPES):
        groups = [stripe * BLOCKS + block for block in range(BLOCKS)]
        pair = block_transpose([b_ref[group] for group in groups], low, even)
        last = block_transpose([t_ref[group] for group in groups], low, even)
        last = (jnp.where(far, last[1], last[0]), jnp.where(far, last[3], last[2]))
        for place, value in enumerate((pair[0], pair[2], pair[1], pair[3]) + last):
            rows = pl.ds(place * TILE, TILE)
            rh_ref[stripe, rows, :], rl_ref[stripe, rows, :] = split(march_step * value)
        rows = pl.ds(0, count * TILE)
        weights = sw_ref[stripe, pl.ds(0, LANES), :]
        added = three_pass(rh_ref[stripe, rows, :], rl_ref[stripe, rows, :], weights)
        right_ref[stripe] = added.reshape(count, TILE, LANES)

    def right_of(stripe, part):
        return right_ref[stripe, LATE.index(part)]

    def x_of(stripe, part):
        return x_ref[stripe * PARTS + part]

    flat = o_ref.reshape(TILE * PARTS * STRIPES, LANES)
    for sweep in range(1, SWEEPS):
        source, parts = (right_of, LATE) if sweep == 1 else (x_of, range(PARTS))
        find_rims(source, parts, zh_ref, zl_ref)
        for stripe in range(STRIPES):
            cross = cf_ref[pl.ds(stripe, 1), :]
            new = relax(stripe, source, parts, cross, kz_ref, om_ref, coup_ref, sw_ref, *halves)
            for part in range(PARTS):
                value = new[part] + right_of(stripe, part) if part in LATE else new[part]
                if sweep < SWEEPS - 1:
                    x_ref[stripe * PARTS + part] = value
                    continue
                offset = part // 2 * 2 * STRIPES + stripe * 2 + part % 2
                value = value + first_ref[stripe * PARTS + part]
                flat[pl.ds(offset, TILE, stride=PARTS * STRIPES), :] = value


def split_host(x):
    high = x.astype(jnp.bfloat16)
    low_part = (x - high.astype(np.float64)).astype(jnp.bfloat16)
    return high, low_part


def beta_matrices():
    index = np.arange(NB)
    angles = (index[:, None] * index[None, :] % NB) * (2.0 * math.pi / NB)
    cosine = np.cos(angles)
    sine = np.sin(angles)
    wave = 2.0 * np.where(index >= NB // 2, index - NB, index) / NB
    factor = 1.0 / math.sqrt(M)
    forward = factor * np.block([[cosine, sine], [-sine * wave, cosine * wave]])
    backward = -factor * np.concatenate([cosine, sine], 0)
    return tuple(np.concatenate(split_host(matrix), 0) for matrix in (forward, backward))


def omega_table():
    angles = np.arange(NW) * (2.0 * math.pi / NW)
    rows = np.concatenate([np.repeat(np.cos(angles)[:, None], 64, 1), np.repeat(np.sin(angles)[:, None], 64, 1)], 1)
    return np.repeat(rows[:, None, :], 8, 1).astype(np.float32)


def split_device(x):
    high = lax.reduce_precision(x, 8, 7)
    return high.astype(jnp.bfloat16), (x - high).astype(jnp.bfloat16)


def derivative_matrix(wall_operator, half):
    own = lax.dynamic_slice(wall_operator, (half * SHARE, 0), (SHARE, SLAB)).T
    mine = lax.dynamic_slice(own, (half * SHARE, 0), (SHARE, SHARE))
    other = lax.dynamic_slice(own, ((1 - half) * SHARE, 0), (SHARE, SHARE))
    same = jnp.eye(BLOCKS, dtype=jnp.float32)
    stacked = jnp.stack([mine, other], 0)
    full = same[None, :, None, :, None] * stacked[:, None, :, None, :]
    full = full.reshape(2 * LANES, LANES)
    return jnp.concatenate(split_device(full), 1)


def solve_matrices(slab_map, slab_inverse):
    count = slab_inverse.shape[0]
    slots = jnp.arange(count, dtype=jnp.int32)
    holds = slab_map[:, None] == slots[None, :]
    below_of = jnp.concatenate([slab_map[:1] * 0 - 1, slab_map[:-1]])
    above_of = jnp.concatenate([slab_map[1:], slab_map[:1] * 0 - 1])
    below = jnp.sum(jnp.where(holds, below_of[:, None], 0), 0)
    above = jnp.sum(jnp.where(holds, above_of[:, None], 0), 0)
    lane = jnp.arange(LANES, dtype=jnp.int32)

    def one_hot(slot, position):
        where = (slot % 2 * SLAB + position + 2 * (slot // 2)) % LANES
        return ((slot >= 0)[:, None] & (where[:, None] == lane[None, :])).astype(jnp.float32)

    low_rim = one_hot(below, SLAB - 1)
    high_rim = one_hot(above, 0)
    rims = coupling * (
        low_rim[:, :, None] * slab_inverse[:, None, :, 0] + high_rim[:, :, None] * slab_inverse[:, None, :, SLAB - 1]
    )
    rims = rims.reshape(STRIPES, 2, LANES, SLAB).transpose(0, 2, 1, 3).reshape(STRIPES, LANES, LANES)
    same = jnp.eye(2, dtype=jnp.float32)
    turned = slab_inverse.transpose(0, 2, 1).reshape(STRIPES, 2, SLAB, SLAB)
    blocks = same[None, :, None, :, None] * turned[:, :, :, None, :]
    blocks = blocks.reshape(STRIPES, LANES, LANES)
    return jnp.concatenate(split_device(jnp.concatenate([blocks, rims], 1)), 2)


def call(kernel, inputs, outputs, scratch, scalars=0, cost=0, limit=60, grid=None, in_specs=None, out_specs=None):
    whole = pl.BlockSpec(memory_space=pltpu.VMEM)
    if in_specs is None:
        in_specs = [pl.BlockSpec(memory_space=pltpu.SMEM)] * scalars + [whole] * (len(inputs) - scalars)
    if out_specs is None:
        out_specs = [whole] * len(outputs)
    extra = {} if grid is None else {"grid": grid}
    return pl.pallas_call(
        kernel,
        out_shape=[jax.ShapeDtypeStruct(shape, jnp.float32) for shape in outputs],
        in_specs=in_specs,
        out_specs=out_specs,
        scratch_shapes=scratch,
        compiler_params=pltpu.CompilerParams(vmem_limit_bytes=limit * MIB),
        cost_estimate=pl.CostEstimate(flops=cost, bytes_accessed=8 << 20, transcendentals=0),
        **extra,
    )(*inputs)


def vmem(*shape, dtype=jnp.float32):
    return pltpu.VMEM(shape, dtype)


def fixed(*shape):
    return pl.BlockSpec(shape, lambda i: (0,) * len(shape))


def local_halves(amplitudes, mode_table, slab_map, base_flow, base_coupling, slab_inverse, wall_operator):
    modes = amplitudes.shape[0]
    points = amplitudes.shape[3]
    groups = lax.axis_size("modes")
    index = lax.axis_index("modes")
    exchange = functools.partial(lax.all_to_all, axis_name="modes", split_axis=0, concat_axis=0, tiled=True)
    neighbours = [(j, j ^ 1) for j in range(groups)]
    stride = PARTS * STRIPES
    tiles = modes // TILE
    first_rows = modes // 2 * 3

    rows = amplitudes.transpose(0, 2, 1, 3).reshape(modes, 5, 2, STRIPES, LANES)
    rows = rows.transpose(0, 1, 3, 2, 4).reshape(modes, stride, LANES)
    positions = mode_table[:, 0] * NB + mode_table[:, 1]
    forward, backward = (jnp.asarray(matrix) for matrix in beta_matrices())
    table = jnp.asarray(omega_table())
    derivative = derivative_matrix(wall_operator, index % 2)
    solve = solve_matrices(slab_map, slab_inverse)
    beta_index = lax.dynamic_slice_in_dim(mode_table[:, 1], index * modes, modes)
    omega_index = lax.dynamic_slice_in_dim(mode_table[:, 0], index * modes, modes)
    signed = jnp.where(beta_index >= NB // 2, beta_index - NB, beta_index)
    wave = phase_gain * (2.0 * signed.astype(jnp.float32) / NB)
    frequency = omega_step * omega_index.astype(jnp.float32)
    wave = jnp.broadcast_to(wave[:, None], (modes, LANES))
    frequency = jnp.broadcast_to(frequency[:, None], (modes, LANES))
    couple = base_coupling.reshape(25 * STRIPES, LANES)

    in_hbm = pl.BlockSpec(memory_space=pltpu.HBM)
    anywhere = pl.BlockSpec(memory_space=pl.ANY)

    def variables(count, place, shift):
        return pl.BlockSpec((PACK_TILE, count * 2 * STRIPES, LANES), lambda i: (i + shift, place, 0))

    packs = modes // FIRST_TILE
    (sent_first,) = call(
        pack_first,
        [rows],
        [(groups, first_rows, LANES)],
        [
            vmem(packs, FIRST_TILE, 3 * 2 * STRIPES, LANES),
            vmem(packs // 2, 3, groups, FIRST_TILE, LANES),
            pltpu.SemaphoreType.DMA((packs,)),
            pltpu.SemaphoreType.DMA((packs // 2, 3)),
        ],
        cost=10**8,
        in_specs=[in_hbm],
        out_specs=[in_hbm],
    )
    first = exchange(sent_first)
    (sent_second,) = call(
        pack_second,
        [rows],
        [(groups, modes, LANES)],
        [],
        cost=10**8,
        grid=(modes // PACK_TILE,),
        in_specs=[variables(2, 0, 0)],
        out_specs=[pl.BlockSpec((groups, PACK_TILE, LANES), lambda i: (0, i, 0))],
    )
    sent_second, derivative, solve, wave, frequency, couple, positions = lax.optimization_barrier(
        (sent_second, derivative, solve, wave, frequency, couple, positions)
    )
    second = exchange(sent_second)

    grid = vmem(M, LANES)
    spectrum = vmem(NW, 2 * NB, LANES)
    folded = vmem(TIMES, NB, LANES)
    turned = vmem(groups, modes // 2, LANES)
    physical = (TIMES, NB, LANES)
    half_physical = (TIMES, NB // 2, LANES)
    scalars = pl.BlockSpec(memory_space=pltpu.SMEM)

    def spectral(kernel, received, count, place, outputs, scratch, cost):
        block = pl.BlockSpec((groups, count, LANES), lambda i: (0, place, 0))
        return call(
            kernel,
            [positions, received, forward, table],
            outputs,
            scratch,
            cost=cost,
            grid=(1,),
            in_specs=[scalars, block, fixed(*forward.shape), fixed(*table.shape)],
            out_specs=[fixed(*shape) for shape in outputs],
        )

    f1, g1, mean = spectral(
        functools.partial(synthesis, True), first, modes, 0, [physical, physical, (8, LANES)], [grid, spectrum], 2 * 10**9
    )
    s1 = lax.ppermute(f1, "modes", neighbours)
    f_last, g_last = spectral(
        synthesis_half, first, modes // 2, 2, [half_physical] * 2, [grid, spectrum, turned], 10**9
    )
    s1, f_last, g_last = lax.optimization_barrier((s1, f_last, g_last))
    s_last = lax.ppermute(f_last, "modes", neighbours)
    (back_first,) = call(
        functools.partial(force_analysis, False),
        [positions, f1, f1, s1, g1, derivative, backward, table, mean],
        [(groups, modes + 8, LANES)],
        [folded, folded, grid],
        scalars=1,
        cost=2 * 10**9,
    )
    got_first = exchange(back_first)
    f2, g2 = spectral(
        functools.partial(synthesis, False), second, modes, 0, [physical, physical], [grid, spectrum], 2 * 10**9
    )
    s2 = lax.ppermute(f2, "modes", neighbours)
    (back_second,) = call(
        functools.partial(force_analysis, True),
        [positions, f1, f2, s2, g2, derivative, backward, table, f_last, s_last, g_last],
        [(groups, first_rows, LANES)],
        [folded, folded, grid, turned],
        scalars=1,
        cost=3 * 10**9,
    )
    got_second = exchange(back_second)

    stacked = TILE * PARTS
    state = (tiles, STRIPES * PARTS + 1, TILE, LANES)
    state_spec = pl.BlockSpec((1,) + state[1:], lambda i: (i, 0, 0, 0))
    returned_spec = pl.BlockSpec((groups, TILE, LANES), lambda i: (0, i, 0))
    mean_spec = pl.BlockSpec((groups, 8, LANES), lambda i: (0, modes // 8, 0))
    mode_spec = pl.BlockSpec((TILE, LANES), lambda i: (i, 0))
    all_spec = pl.BlockSpec((TILE, stride, LANES), lambda i: (i, 0, 0))
    halves = [vmem(STRIPES, stacked, LANES, dtype=jnp.bfloat16)] * 2 + [vmem(stacked, LANES, dtype=jnp.bfloat16)] * 2
    shared_specs = [fixed(*couple.shape), mode_spec, mode_spec, fixed(*solve.shape)]
    shared = [couple, wave, frequency, solve]
    (iterate,) = call(
        relax_first,
        [rows, got_first, got_first, base_flow.reshape(STRIPES, LANES)] + shared,
        [state],
        [vmem(STRIPES * PARTS, TILE, LANES)] * 2 + [vmem(8, LANES)] + halves,
        cost=3 * 10**9,
        grid=(tiles,),
        in_specs=[all_spec, returned_spec, mean_spec, fixed(STRIPES, LANES)] + shared_specs,
        out_specs=[state_spec],
    )
    (out,) = call(
        relax_last,
        [iterate, got_second] + shared,
        [(modes, stride, LANES)],
        [
            vmem(*state),
            vmem(tiles, groups, TILE, LANES),
            vmem(tiles, groups, TILE, LANES),
            vmem(tiles, TILE, stride, LANES),
            vmem(*couple.shape),
            vmem(*wave.shape),
            vmem(*frequency.shape),
            vmem(*solve.shape, dtype=jnp.bfloat16),
            pltpu.SemaphoreType.DMA((3, tiles)),
            pltpu.SemaphoreType.DMA((tiles,)),
            pltpu.SemaphoreType.DMA((4,)),
            vmem(STRIPES, len(LATE), TILE, LANES),
            vmem(STRIPES * PARTS, TILE, LANES),
        ]
        + halves,
        cost=2 * 10**9,
        limit=LAST_LIMIT,
        in_specs=[in_hbm, anywhere] + [in_hbm] * 4,
        out_specs=[in_hbm],
    )
    out = out.reshape(modes, 5, STRIPES, 2, LANES).transpose(0, 1, 3, 2, 4).reshape(modes, 5, 2, points)
    return out.transpose(0, 2, 1, 3)


def local_any(amplitudes, mode_table, slab_map, base_flow, base_coupling, slab_inverse, wall_operator):
    points = amplitudes.shape[3]
    fits = points == STRIPES * LANES and points // lax.axis_size("modes") == SHARE
    fits = fits and slab_inverse.shape == (2 * STRIPES, SLAB, SLAB) and amplitudes.shape[0] % (2 * ROWS) == 0
    chosen = local_halves if fits else local
    return chosen(amplitudes, mode_table, slab_map, base_flow, base_coupling, slab_inverse, wall_operator)


def solution(mesh):
    return jax.shard_map(
        local_any,
        mesh=mesh,
        in_specs=(
            P(("runs", "modes"), None, None, None),
            P(),
            P(),
            P("runs"),
            P("runs", None),
            P(),
            P(),
        ),
        out_specs=P(("runs", "modes"), None, None, None),
        check_vma=False,
    )
```

```python
import functools
import math

import jax
import jax.numpy as jnp
import numpy as np
from jax import lax
from jax.experimental import pallas as pl
from jax.experimental.pallas import tpu as pltpu
from jax.sharding import PartitionSpec as P

M = 4096
NB = 128
SWEEPS = 3
NW = 32


precise = lax.Precision.HIGHEST
omega_step = 0.01
phase_gain = 0.2
march_step = 0.2
coupling = 0.3


def twiddle(length):
    counter = jnp.arange(length, dtype=jnp.int32)
    product = counter[:, None] * counter[None, :] % length
    angles = product.astype(jnp.float32) * (2.0 * math.pi / length)
    return (jnp.cos(angles), jnp.sin(angles))


def mode_tables(mode_table):
    omega_index = mode_table[:, 0]
    beta_index = mode_table[:, 1]
    signed = jnp.where(beta_index >= NB // 2, beta_index - NB, beta_index)
    wavenum = 2.0 * signed.astype(jnp.float32) / NB
    frequency = omega_step * omega_index.astype(jnp.float32)
    grid_pos = omega_index * NB + beta_index
    mode_at = jnp.zeros((M,), jnp.int32).at[grid_pos].set(jnp.arange(M, dtype=jnp.int32))
    return (wavenum, frequency, grid_pos, mode_at)


def synthesize(real_part, imag_part, tables, factor):
    cos_omega, sin_omega, cos_beta, sin_beta = tables
    mixed_re = jnp.einsum("...wb,bz->...wz", real_part, cos_beta, precision=precise) - jnp.einsum(
        "...wb,bz->...wz", imag_part, sin_beta, precision=precise
    )
    mixed_im = jnp.einsum("...wb,bz->...wz", real_part, sin_beta, precision=precise) + jnp.einsum(
        "...wb,bz->...wz", imag_part, cos_beta, precision=precise
    )
    physical = jnp.einsum("...wz,wt->...tz", mixed_re, cos_omega, precision=precise) - jnp.einsum(
        "...wz,wt->...tz", mixed_im, sin_omega, precision=precise
    )
    return physical * factor


def analyze(physical, tables, factor):
    cos_omega, sin_omega, cos_beta, sin_beta = tables
    half_re = jnp.einsum("...tz,zb->...tb", physical, cos_beta, precision=precise)
    half_im = -jnp.einsum("...tz,zb->...tb", physical, sin_beta, precision=precise)
    coef_re = jnp.einsum("...tb,tw->...wb", half_re, cos_omega, precision=precise) + jnp.einsum(
        "...tb,tw->...wb", half_im, sin_omega, precision=precise
    )
    coef_im = jnp.einsum("...tb,tw->...wb", half_im, cos_omega, precision=precise) - jnp.einsum(
        "...tb,tw->...wb", half_re, sin_omega, precision=precise
    )
    return (coef_re * factor, coef_im * factor)


def forcing(normal_vel, spanwise_vel, wall_grad, span_grad, tables, factor):
    vel_v = synthesize(normal_vel[0], normal_vel[1], tables, factor)
    vel_w = synthesize(spanwise_vel[0], spanwise_vel[1], tables, factor)
    grad_y = synthesize(wall_grad[0], wall_grad[1], tables, factor)
    grad_z = synthesize(span_grad[0], span_grad[1], tables, factor)
    product = -(vel_v[None] * grad_y + vel_w[None] * grad_z)
    return analyze(product, tables, factor)


def wall_derivative(values, wall_operator):
    slab_width = wall_operator.shape[0]
    slab_count = values.shape[3] // slab_width
    blocks = values.reshape(values.shape[:3] + (slab_count, slab_width))
    return jnp.einsum("ij,abcsj->abcsi", wall_operator, blocks, precision=precise).reshape(
        values.shape
    )


def interface_table(slab_map, slab_count, slab_width):
    inverse = (
        jnp.zeros((slab_count,), jnp.int32)
        .at[slab_map]
        .set(jnp.arange(slab_count, dtype=jnp.int32))
    )
    position = jnp.arange(slab_count * slab_width, dtype=jnp.int32)
    slot_of = position // slab_width
    within = position % slab_width
    domain = inverse[slot_of]
    below = slab_map[jnp.maximum(domain - 1, 0)] * slab_width + (slab_width - 1)
    above = slab_map[jnp.minimum(domain + 1, slab_count - 1)] * slab_width
    lower_ok = (within == 0) & (domain > 0)
    upper_ok = (within == slab_width - 1) & (domain < slab_count - 1)
    source = jnp.where(lower_ok, below, jnp.where(upper_ok, above, 0))
    weight = (lower_ok | upper_ok).astype(jnp.float32)
    return (source, weight)


def relaxation(iterate, right_side, rotation, matrix, slab_inverse, source, weight):
    slab_count = slab_inverse.shape[0]
    slab_width = slab_inverse.shape[1]
    coupled = jnp.einsum("kjy,acjy->acky", matrix, iterate, precision=precise)
    applied = jnp.stack(
        [
            coupled[:, 0] - rotation[:, None, :] * iterate[:, 1],
            coupled[:, 1] + rotation[:, None, :] * iterate[:, 0],
        ],
        1,
    )
    rims = jnp.take(iterate, source, axis=3) * weight
    residual_in = right_side - applied + coupling * rims
    blocks = residual_in.reshape(iterate.shape[:3] + (slab_count, slab_width))
    return jnp.einsum("sij,acvsj->acvsi", slab_inverse, blocks, precision=precise).reshape(
        iterate.shape
    )


def local(amplitudes, mode_table, slab_map, base_flow, base_coupling, slab_inverse, wall_operator):
    local_modes = amplitudes.shape[0]
    wall_points = amplitudes.shape[3]
    groups = lax.axis_size("modes")
    point_share = wall_points // groups
    wavenum, frequency, grid_pos, mode_at = mode_tables(mode_table)
    first_mode = lax.axis_index("modes") * local_modes
    wave_local = lax.dynamic_slice_in_dim(wavenum, first_mode, local_modes)
    freq_local = lax.dynamic_slice_in_dim(frequency, first_mode, local_modes)
    tables = twiddle(NW) + twiddle(NB)
    factor = 1.0 / math.sqrt(M)
    source, weight = interface_table(slab_map, slab_inverse.shape[0], slab_inverse.shape[1])
    matrix = base_coupling.reshape(5, 5, wall_points)
    gradient = wall_derivative(amplitudes, wall_operator)
    span = jnp.stack(
        [
            -wave_local[:, None, None] * amplitudes[:, 1],
            wave_local[:, None, None] * amplitudes[:, 0],
        ],
        1,
    )
    fields = jnp.concatenate([amplitudes[:, :, 2:4], gradient, span], 2)
    field_count = fields.shape[2]
    channels = 2 * field_count
    outgoing = jnp.transpose(
        fields.reshape(local_modes, channels, groups, point_share), (1, 2, 3, 0)
    ).reshape(channels, groups, point_share * local_modes)
    incoming = lax.all_to_all(outgoing, "modes", split_axis=1, concat_axis=1, tiled=True)
    by_mode = jnp.transpose(
        incoming.reshape(channels, groups, point_share, local_modes), (0, 2, 1, 3)
    ).reshape(channels, point_share, M)
    gridded = by_mode[..., mode_at].reshape(2, field_count, point_share, NW, NB)
    normal_vel = gridded[:, 0]
    spanwise_vel = gridded[:, 1]
    wall_grad = gridded[:, 2:7]
    span_grad = gridded[:, 7:12]
    mean_crossflow = lax.all_gather(spanwise_vel[0, :, 0, 0], "modes", axis=0, tiled=True)
    coef_re, coef_im = forcing(normal_vel, spanwise_vel, wall_grad, span_grad, tables, factor)
    packed = jnp.stack([coef_re, coef_im], 0).reshape(10, point_share, M)[..., grid_pos]
    sendback = jnp.transpose(
        packed.reshape(10, point_share, groups, local_modes), (0, 2, 1, 3)
    ).reshape(10, groups, point_share * local_modes)
    returned = lax.all_to_all(sendback, "modes", split_axis=1, concat_axis=1, tiled=True)
    nonlinear = jnp.transpose(
        returned.reshape(10, groups, point_share, local_modes), (3, 0, 1, 2)
    ).reshape(local_modes, 2, 5, wall_points)
    crossflow = base_flow + mean_crossflow
    rotation = phase_gain * wave_local[:, None] * crossflow[None, :] - freq_local[:, None]
    right_side = amplitudes + march_step * nonlinear
    iterate = amplitudes
    for sweep_index in range(SWEEPS):
        iterate = relaxation(iterate, right_side, rotation, matrix, slab_inverse, source, weight)
    return iterate


LANES = 128
SHARE = 32
SLAB = 64
HALF = NW // 2
TIMES = HALF + 1
BLOCKS = LANES // SHARE
STRIPES = 4
PARTS = 10
TILE = 64
PACK_TILE = 32
MIB = 1024 * 1024
VMEM_LIMIT = 53


def roll(x, shift):
    return pltpu.roll(x, shift % LANES, x.ndim - 1)


def lane_index(shape):
    return lax.broadcasted_iota(jnp.int32, shape, len(shape) - 1)


def lane_masks(shape):
    lane = lane_index(shape)
    return (lane < 64, (lane & 32) == 0)


def real_sign(shape):
    return jnp.where(lane_index(shape) < 64, 1.0, -1.0).astype(jnp.float32)


def block_transpose(rows, low, even):
    r0, r1, r2, r3 = rows
    crossed = roll(jnp.where(low, r2, r0), 64)
    t0 = jnp.where(low, r0, crossed)
    t2 = jnp.where(low, crossed, r2)
    crossed = roll(jnp.where(low, r3, r1), 64)
    t1 = jnp.where(low, r1, crossed)
    t3 = jnp.where(low, crossed, r3)
    return (
        jnp.where(even, t0, roll(t1, 32)),
        jnp.where(even, roll(t0, 96), t1),
        jnp.where(even, t2, roll(t3, 32)),
        jnp.where(even, roll(t2, 96), t3),
    )


def split(x):
    high = x.astype(jnp.bfloat16)
    return high, (x - high.astype(jnp.float32)).astype(jnp.bfloat16)


def dot(a, b):
    return jnp.dot(a, b, preferred_element_type=jnp.float32)


def cosine_sine(inputs, length, table, sign, real):
    if length == 4:
        first, middle, last = inputs
        middle_re = middle * real
        total = first + last
        return [total + middle_re, (first - last) + (middle - middle_re), total - middle_re]
    step = NW // length
    quarter = length // 4
    even = cosine_sine(inputs[0::2], length // 2, table, sign, real)
    odd_inputs = [(a, inputs[a]) for a in range(1, length // 2, 2)]
    odd = []
    for t in range(quarter + 1):
        if t == 0:
            total = odd_inputs[0][1]
            for _, value in odd_inputs[1:]:
                total = total + value
            odd.append(total * real)
        elif t == quarter:
            total = odd_inputs[0][1]
            for a, value in odd_inputs[1:]:
                total = total + value if a % 4 == 1 else total - value
            odd.append(total - total * real)
        else:
            total = None
            for a, value in odd_inputs:
                term = table(a * t * step % NW) * value
                total = term if total is None else total + term
            odd.append(total)
    out = [None] * (length // 2 + 1)
    for t in range(quarter + 1):
        out[t] = even[t] + odd[t]
        out[length // 2 - t] = sign * (even[t] - odd[t])
    out[quarter] = even[quarter] + odd[quarter]
    return out


def spread(ref, offset):
    flat = ref.reshape(ref.shape[0] * ref.shape[1], LANES)
    return flat[pl.ds(offset, ref.shape[0], stride=ref.shape[1]), :]


def pack_pair(first, first_offset, second, second_offset, low, even):
    out = []
    for stripe in range(STRIPES):
        rows = []
        for part in range(2):
            rows.append(spread(first, first_offset + stripe * 2 + part))
            rows.append(spread(second, second_offset + stripe * 2 + part))
        out.extend(block_transpose(rows, low, even))
    return out


def pack(first, with_last, rows_ref, o_ref, in_ref, out_ref, in_sem, out_sem):
    tiles = in_ref.shape[0]
    count = in_ref.shape[1]
    wanted = pl.ds(first * 2 * STRIPES, in_ref.shape[2])
    low, even = lane_masks((count, LANES))
    loads = []
    for tile in range(tiles):
        source = rows_ref.at[pl.ds(tile * count, count), wanted, :]
        loads.append(pltpu.make_async_copy(source, in_ref.at[tile], in_sem.at[tile]))
    half = tiles // 2
    for tile in range(half):
        loads[tile].start()
        loads[tile + half].start()
    stores = []
    for tile in range(half):
        loads[tile].wait()
        loads[tile + half].wait()
        near = in_ref.at[tile]
        far = in_ref.at[tile + half]
        pieces = [(near, 0, near, 2 * STRIPES), (far, 0, far, 2 * STRIPES)]
        if with_last:
            pieces.append((near, 8 * STRIPES, far, 8 * STRIPES))
        for place, piece in enumerate(pieces):
            for group, value in enumerate(pack_pair(*piece, low, even)):
                out_ref[tile, place, group] = value
            target = o_ref.at[:, pl.ds((place * half + tile) * count, count), :]
            store = pltpu.make_async_copy(out_ref.at[tile, place], target, out_sem.at[tile, place])
            store.start()
            stores.append(store)
    for store in stores:
        store.wait()


ROWS = 128


def loop(count, unroll, body):
    def step(i, carry):
        for j in range(unroll):
            body(i * unroll + j)
        return carry

    lax.fori_loop(0, count // unroll, step, 0)
    for i in range(count // unroll * unroll, count):
        body(i)


def lanes_constants():
    sign = real_sign((8, LANES))
    real = jnp.where(lane_index((8, LANES)) < 64, 1.0, 0.0).astype(jnp.float32)
    even = (lane_index((8, LANES)) & 32) == 0
    return sign, real, even


def pair_left(even, near, far):
    return jnp.where(even, near, roll(far, 32))


def pair_right(even, near, far):
    return jnp.where(even, roll(near, 96), far)


def scatter(pos_ref, grid_ref, cell, source, group, row):
    for j in range(ROWS):
        grid_ref[pl.ds(pos_ref[cell + j], 1), :] = source[group, pl.ds(row + j, 1), :]


def synthesis_beta(w_ref, first, second):
    wide_sign = real_sign((NB, LANES))
    columns = [jnp.concatenate([x, -wide_sign * roll(x, 64)], 0) for x in (first, second)]
    high, low_part = split(jnp.concatenate(columns, 1))
    product = dot(w_ref[...], high)
    out = product[: 2 * NB] + product[2 * NB :] + dot(w_ref[pl.ds(0, 2 * NB), :], low_part)
    return out[:, :LANES], out[:, LANES:]


def synthesis(with_mean, pos_ref, r_ref, w_ref, tab_ref, *refs):
    if with_mean:
        f_ref, g_ref, mean_ref, grid_ref, spec_ref = refs
    else:
        f_ref, g_ref, grid_ref, spec_ref = refs
    groups = r_ref.shape[0]
    modes = M // groups
    sign, real, _ = lanes_constants()

    def table(j):
        return tab_ref[j]

    def grid(a):
        return grid_ref[pl.ds(pl.multiple_of(a * NB, NB), NB), :]

    def both_halves(i):
        group = i // (modes // ROWS)
        start = pl.multiple_of(i % (modes // ROWS) * ROWS, ROWS)
        scatter(pos_ref, grid_ref, i * ROWS, r_ref, group, start)

    loop(groups * (modes // ROWS), 1, both_halves)
    if with_mean:
        mean_ref[...] = grid_ref[pl.ds(0, 8), :]

    def beta(i):
        spec_ref[2 * i], spec_ref[2 * i + 1] = synthesis_beta(w_ref, grid(2 * i), grid(2 * i + 1))

    loop(NW // 2, 2, beta)

    def omega(out_ref, shift):
        def body(i):
            rows = pl.ds(pl.multiple_of(i * 8, 8), 8)
            source = pl.ds(pl.multiple_of(shift + i * 8, 8), 8)
            inputs = [spec_ref[0, source, :] * real]
            for a in range(1, HALF):
                inputs.append(spec_ref[a, source, :] + sign * spec_ref[NW - a, source, :])
            inputs.append(spec_ref[HALF, source, :] * real)
            for t, value in enumerate(cosine_sine(inputs, NW, table, sign, real)):
                out_ref[t, rows, :] = value - sign * roll(value, 64)

        loop(NB // 8, 2, body)

    omega(f_ref, 0)
    omega(g_ref, NB)


def synthesis_half(pos_ref, r_ref, w_ref, tab_ref, f_ref, g_ref, grid_ref, spec_ref, turned_ref):
    groups = r_ref.shape[0]
    modes = M // groups
    sign, real, even = lanes_constants()
    wide_even = (lane_index((NB, LANES)) & 32) == 0

    def table(j):
        return tab_ref[j]

    def grid(a):
        return grid_ref[pl.ds(pl.multiple_of(a * NB, NB), NB), :]

    def turn(group):
        turned_ref[group] = roll(r_ref[group], 96)
        for block in range(modes // 2 // ROWS):
            cell = group * modes + block * ROWS
            scatter(pos_ref, grid_ref, cell, r_ref, group, block * ROWS)
            scatter(pos_ref, grid_ref, cell + modes // 2, turned_ref, group, block * ROWS)

    loop(groups, 1, turn)

    def beta(i):
        columns = [pair_left(wide_even, grid(a), grid(a + HALF)) for a in (2 * i, 2 * i + 1)]
        spec_ref[2 * i], spec_ref[2 * i + 1] = synthesis_beta(w_ref, *columns)

    loop(HALF // 2, 2, beta)

    def omega(out_ref, shift):
        def body(i):
            rows = pl.ds(pl.multiple_of(i * 8, 8), 8)
            near = pl.ds(pl.multiple_of(shift + i * 8, 8), 8)
            far = pl.ds(pl.multiple_of(shift + NB // 2 + i * 8, 8), 8)
            firsts = []
            seconds = []
            for a in range(HALF):
                pieces = (even, spec_ref[a, near, :], spec_ref[a, far, :])
                firsts.append(pair_left(*pieces))
                seconds.append(pair_right(*pieces))
            inputs = [firsts[0] * real]
            for a in range(1, HALF):
                inputs.append(firsts[a] + sign * seconds[HALF - a])
            inputs.append(seconds[0] * real)
            for t, value in enumerate(cosine_sine(inputs, NW, table, sign, real)):
                out_ref[t, rows, :] = value - sign * roll(value, 64)

        loop(NB // 16, 2, body)

    omega(f_ref, 0)
    omega(g_ref, NB)


def force_analysis(with_last, pos_ref, vw_ref, f_ref, s_ref, g_ref, d_ref, w_ref, tab_ref, *refs):
    if with_last:
        f_last_ref, s_last_ref, g_last_ref, o_ref, k_ref, r_ref, n_ref, turned_ref = refs
    else:
        mean_ref, o_ref, k_ref, r_ref, n_ref = refs
    groups = o_ref.shape[0]
    modes = M // groups
    sign, real, _ = lanes_constants()
    wide_sign = real_sign((NB, LANES))
    wide_real, wide_even = lane_masks((NB, LANES))
    half_rows = NB // 2

    def table(j):
        return tab_ref[j]

    def gather(group, mode, target, row):
        for j in range(ROWS):
            cell = pos_ref[group * modes + mode + j]
            target[group, pl.ds(row + j, 1), :] = n_ref[pl.ds(cell, 1), :]

    def force_of(t, rows, v, w, f, s, g):
        high, low_part = split(jnp.concatenate([f, s], 1))
        both = dot(high, d_ref[...])
        grad = both[:, :LANES] + both[:, LANES:] + dot(low_part, d_ref[:, :LANES])
        force = v * grad + w * g
        if t is None:
            return jnp.where(wide_real[:rows], force, 0.0)
        return force + wide_sign[:rows] * roll(force, 64)

    def full_product(t, alone=False):
        vw = vw_ref[t]
        v = pair_left(wide_even, vw, vw)
        w = pair_right(wide_even, vw, vw)
        k_ref[t] = force_of(None if alone else t, NB, v, w, f_ref[t], s_ref[t], g_ref[t])

    def products(product):
        product(0, True)
        product(HALF, True)
        loop(HALF - 1, 3, lambda i: product(i + 1))

    def omegas(tiles):
        def body(i):
            rows = pl.ds(pl.multiple_of(i * 8, 8), 8)
            inputs = [k_ref[t, rows, :] for t in range(TIMES)]
            for a, value in enumerate(cosine_sine(inputs, NW, table, sign, real)):
                r_ref[a, rows, :] = value

        loop(tiles, 2, body)

    def beta(columns):
        high, low_part = split(jnp.concatenate(columns, 1) if len(columns) > 1 else columns[0])
        both = dot(w_ref[...], high)
        out = both[: 2 * NB] + both[2 * NB :] + dot(w_ref[pl.ds(0, 2 * NB), :], low_part)
        result = []
        for j in range(len(columns)):
            cosine = out[:NB, j * LANES : (j + 1) * LANES]
            sine = roll(out[NB:, j * LANES : (j + 1) * LANES], 64)
            result.append((cosine + wide_sign * sine, wide_sign * cosine - sine))
        return result

    def store(a, plus, minus):
        mirror = (NW - a) % NW
        n_ref[pl.ds(pl.multiple_of(mirror * NB, NB), NB), :] = minus
        n_ref[pl.ds(pl.multiple_of(a * NB, NB), NB), :] = plus

    products(full_product)
    omegas(NB // 8)

    def full_beta(i):
        for j, (plus, minus) in enumerate(beta([r_ref[2 * i], r_ref[2 * i + 1]])):
            store(2 * i + j, plus, minus)

    loop(HALF // 2, 2, full_beta)
    store(HALF, *beta([r_ref[HALF]])[0])

    def both_halves(i):
        group = i // (modes // ROWS)
        start = pl.multiple_of(i % (modes // ROWS) * ROWS, ROWS)
        gather(group, start, o_ref, start)

    loop(groups * (modes // ROWS), 1, both_halves)
    if not with_last:
        for group in range(groups):
            o_ref[group, pl.ds(modes, 8), :] = mean_ref[...]
        return

    def half_product(t, alone=False):
        vw = vw_ref[t]
        near = vw[:half_rows]
        far = vw[half_rows:]
        v = pair_left(wide_even[:half_rows], near, far)
        w = pair_right(wide_even[:half_rows], near, far)
        k_ref[t, pl.ds(0, half_rows), :] = force_of(
            None if alone else t, half_rows, v, w, f_last_ref[t], s_last_ref[t], g_last_ref[t]
        )

    products(half_product)
    omegas(NB // 16)

    def half_columns(a):
        even = wide_even[:half_rows]
        pieces = (even, r_ref[a, pl.ds(0, half_rows), :], r_ref[a + 1, pl.ds(0, half_rows), :])
        return jnp.concatenate([pair_left(*pieces), pair_right(*pieces)], 0)

    def half_beta(i):
        for j, (plus, minus) in enumerate(beta([half_columns(4 * i), half_columns(4 * i + 2)])):
            a = 4 * i + 2 * j
            store(a, plus, minus)
            store(a + 1, roll(plus, 96), roll(minus, 96))

    loop(HALF // 4, 1, half_beta)
    last = r_ref[HALF, pl.ds(0, half_rows), :]
    store(HALF, *beta([jnp.concatenate([last, roll(last, 96)], 0)])[0])

    def turn(group):
        for block in range(modes // 2 // ROWS):
            gather(group, block * ROWS, o_ref, modes + block * ROWS)
            gather(group, modes // 2 + block * ROWS, turned_ref, block * ROWS)
        here = pl.ds(modes, modes // 2)
        near = o_ref[group, here, :]
        o_ref[group, here, :] = pair_left((lane_index(near.shape) & 32) == 0, near, turned_ref[group])

    loop(groups, 1, turn)


def find_rims(x_of, parts, zh_ref, zl_ref):
    lane = lane_index((TILE, LANES))
    edges = []
    for stripe in range(STRIPES):
        place = (lane - 2 * stripe) & (SLAB - 1)
        edges.append((place == 0) | (place == SLAB - 1))
    for part in range(PARTS):
        rows = pl.ds(part * TILE, TILE)
        if part not in parts:
            zh_ref[rows, :] = zl_ref[rows, :] = jnp.zeros((TILE, LANES), jnp.bfloat16)
            continue
        rims = x_of(0, part)
        for stripe in range(1, STRIPES):
            rims = jnp.where(edges[stripe], roll(x_of(stripe, part), 2 * stripe), rims)
        zh_ref[rows, :], zl_ref[rows, :] = split(rims)


def three_pass(high, low_part, weights):
    both = dot(high, weights)
    return both[:, :LANES] + both[:, LANES:] + dot(low_part, weights[:, :LANES])


def relax(stripe, x_of, parts, cross, kz_ref, om_ref, coup_ref, sw_ref, rh_ref, rl_ref, zh_ref, zl_ref):
    values = {part: x_of(stripe, part) for part in parts}
    rotation = kz_ref[...] * cross - om_ref[...]
    for k in range(5):
        out_re = jnp.zeros((TILE, LANES), jnp.float32)
        out_im = out_re
        if 2 * k in values:
            out_re = rotation * values[2 * k + 1]
            out_im = -(rotation * values[2 * k])
        for j in range(5):
            if 2 * j not in values:
                continue
            weight = coup_ref[pl.ds((k * 5 + j) * STRIPES + stripe, 1), :]
            out_re = out_re - weight * values[2 * j]
            out_im = out_im - weight * values[2 * j + 1]
        for part, out in ((2 * k, out_re), (2 * k + 1, out_im)):
            rows = pl.ds(part * TILE, TILE)
            rh_ref[stripe, rows, :], rl_ref[stripe, rows, :] = split(out)
    high = jnp.concatenate([rh_ref[stripe], zh_ref[...]], 1)
    low_rows = jnp.concatenate([rl_ref[stripe], zl_ref[...]], 1)
    return three_pass(high, low_rows, sw_ref[stripe]).reshape(PARTS, TILE, LANES)


def relax_first(a_ref, b_ref, mean_ref, base_ref, coup_ref, kz_ref, om_ref, sw_ref, out_ref, right_ref, x_ref, cf_ref, *halves):
    rh_ref, rl_ref, zh_ref, zl_ref = halves
    low, even = lane_masks((TILE, LANES))
    block_of = lane_index((1, LANES)) // SHARE
    for stripe in range(STRIPES):
        total = base_ref[pl.ds(stripe, 1), :]
        for block in range(BLOCKS):
            row = mean_ref[stripe * BLOCKS + block, pl.ds(0, 1), :]
            total = total + jnp.where(block_of == block, roll(row, SHARE * (block - 1)), 0.0)
        cf_ref[pl.ds(stripe, 1), :] = total
    out_ref[0, STRIPES * PARTS, pl.ds(0, 8), :] = cf_ref[...]

    for stripe in range(STRIPES):
        groups = [stripe * BLOCKS + block for block in range(BLOCKS)]
        velocity = block_transpose([b_ref[group] for group in groups], low, even)
        gained = {4: velocity[0], 6: velocity[1], 5: velocity[2], 7: velocity[3]}
        for part in range(PARTS):
            value = spread(a_ref, part // 2 * 2 * STRIPES + stripe * 2 + part % 2)
            x_ref[stripe * PARTS + part] = value
            if part in gained:
                value = value + march_step * gained[part]
            rows = pl.ds(part * TILE, TILE)
            rh_ref[stripe, rows, :], rl_ref[stripe, rows, :] = split(value)
        solved = three_pass(rh_ref[stripe], rl_ref[stripe], sw_ref[stripe, pl.ds(0, LANES), :])
        right_ref[pl.ds(stripe * PARTS, PARTS)] = solved.reshape(PARTS, TILE, LANES)

    def x_of(stripe, part):
        return x_ref[stripe * PARTS + part]

    for sweep in range(SWEEPS):
        find_rims(x_of, range(PARTS), zh_ref, zl_ref)
        for stripe in range(STRIPES):
            here = pl.ds(stripe * PARTS, PARTS)
            cross = cf_ref[pl.ds(stripe, 1), :]
            new = relax(stripe, x_of, range(PARTS), cross, kz_ref, om_ref, coup_ref, sw_ref, *halves)
            if sweep < SWEEPS - 1:
                x_ref[here] = right_ref[here] + new
            else:
                out_ref[0, here] = right_ref[here] + new


LATE = (0, 1, 2, 3, 8, 9)


def relax_last(first_hbm, b_any, *refs):
    shared_hbm, o_hbm, (first_buf, b_buf, t_buf, o_buf), shared = refs[:4], refs[4], refs[5:9], refs[9:13]
    (in_sem, out_sem, shared_sem), scratch = refs[13:16], refs[16:]
    coup_ref, kz_ref, om_ref, sw_ref = shared
    tiles = first_buf.shape[0]
    modes = tiles * TILE

    def loads(i):
        pair = b_any.at[:, pl.ds(i * TILE, TILE), :]
        last = b_any.at[:, pl.ds(modes + i % (tiles // 2) * TILE, TILE), :]
        return (
            pltpu.make_async_copy(pair, b_buf.at[i], in_sem.at[0, i]),
            pltpu.make_async_copy(last, t_buf.at[i], in_sem.at[1, i]),
            pltpu.make_async_copy(first_hbm.at[i], first_buf.at[i], in_sem.at[2, i]),
        )

    def store(i):
        target = o_hbm.at[pl.ds(i * TILE, TILE), :, :]
        return pltpu.make_async_copy(o_buf.at[i], target, out_sem.at[i])

    ahead = 2
    fixed_loads = [
        pltpu.make_async_copy(source, target, shared_sem.at[place])
        for place, (source, target) in enumerate(zip(shared_hbm, shared))
    ]
    for load in fixed_loads:
        load.start()
    for i in range(ahead):
        for load in loads(i):
            load.start()
    for load in fixed_loads:
        load.wait()

    def body(i, carry):
        for load in loads(i):
            load.wait()

        @pl.when(i + ahead < tiles)
        def _():
            for load in loads(i + ahead):
                load.start()

        modes_here = pl.ds(pl.multiple_of(i * TILE, TILE), TILE)
        relax_tile(
            i >= tiles // 2,
            first_buf.at[i],
            b_buf.at[i],
            t_buf.at[i],
            first_buf.at[i, STRIPES * PARTS],
            coup_ref,
            kz_ref.at[modes_here, :],
            om_ref.at[modes_here, :],
            sw_ref,
            o_buf.at[i],
            *scratch,
        )
        store(i).start()
        return carry

    lax.fori_loop(0, tiles, body, 0)
    for i in range(tiles):
        store(i).wait()


def relax_tile(far, first_ref, b_ref, t_ref, cf_ref, coup_ref, kz_ref, om_ref, sw_ref, o_ref, right_ref, x_ref, *halves):
    rh_ref, rl_ref, zh_ref, zl_ref = halves
    low, even = lane_masks((TILE, LANES))
    count = len(LATE)
    for stripe in range(STRIPES):
        groups = [stripe * BLOCKS + block for block in range(BLOCKS)]
        pair = block_transpose([b_ref[group] for group in groups], low, even)
        last = block_transpose([t_ref[group] for group in groups], low, even)
        last = (jnp.where(far, last[1], last[0]), jnp.where(far, last[3], last[2]))
        for place, value in enumerate((pair[0], pair[2], pair[1], pair[3]) + last):
            rows = pl.ds(place * TILE, TILE)
            rh_ref[stripe, rows, :], rl_ref[stripe, rows, :] = split(march_step * value)
        rows = pl.ds(0, count * TILE)
        weights = sw_ref[stripe, pl.ds(0, LANES), :]
        added = three_pass(rh_ref[stripe, rows, :], rl_ref[stripe, rows, :], weights)
        right_ref[stripe] = added.reshape(count, TILE, LANES)

    def right_of(stripe, part):
        return right_ref[stripe, LATE.index(part)]

    def x_of(stripe, part):
        return x_ref[stripe * PARTS + part]

    flat = o_ref.reshape(TILE * PARTS * STRIPES, LANES)
    for sweep in range(1, SWEEPS):
        source, parts = (right_of, LATE) if sweep == 1 else (x_of, range(PARTS))
        find_rims(source, parts, zh_ref, zl_ref)
        for stripe in range(STRIPES):
            cross = cf_ref[pl.ds(stripe, 1), :]
            new = relax(stripe, source, parts, cross, kz_ref, om_ref, coup_ref, sw_ref, *halves)
            for part in range(PARTS):
                value = new[part] + right_of(stripe, part) if part in LATE else new[part]
                if sweep < SWEEPS - 1:
                    x_ref[stripe * PARTS + part] = value
                    continue
                offset = part // 2 * 2 * STRIPES + stripe * 2 + part % 2
                value = value + first_ref[stripe * PARTS + part]
                flat[pl.ds(offset, TILE, stride=PARTS * STRIPES), :] = value


def split_host(x):
    high = x.astype(jnp.bfloat16)
    low_part = (x - high.astype(np.float64)).astype(jnp.bfloat16)
    return high, low_part


def beta_matrices():
    index = np.arange(NB)
    angles = (index[:, None] * index[None, :] % NB) * (2.0 * math.pi / NB)
    cosine = np.cos(angles)
    sine = np.sin(angles)
    wave = 2.0 * np.where(index >= NB // 2, index - NB, index) / NB
    factor = 1.0 / math.sqrt(M)
    forward = factor * np.block([[cosine, sine], [-sine * wave, cosine * wave]])
    backward = -factor * np.concatenate([cosine, sine], 0)
    return tuple(np.concatenate(split_host(matrix), 0) for matrix in (forward, backward))


def omega_table():
    angles = np.arange(NW) * (2.0 * math.pi / NW)
    rows = np.concatenate([np.repeat(np.cos(angles)[:, None], 64, 1), np.repeat(np.sin(angles)[:, None], 64, 1)], 1)
    return np.repeat(rows[:, None, :], 8, 1).astype(np.float32)


def split_device(x):
    high = lax.reduce_precision(x, 8, 7)
    return high.astype(jnp.bfloat16), (x - high).astype(jnp.bfloat16)


def derivative_matrix(wall_operator, half):
    own = lax.dynamic_slice(wall_operator, (half * SHARE, 0), (SHARE, SLAB)).T
    mine = lax.dynamic_slice(own, (half * SHARE, 0), (SHARE, SHARE))
    other = lax.dynamic_slice(own, ((1 - half) * SHARE, 0), (SHARE, SHARE))
    same = jnp.eye(BLOCKS, dtype=jnp.float32)
    stacked = jnp.stack([mine, other], 0)
    full = same[None, :, None, :, None] * stacked[:, None, :, None, :]
    full = full.reshape(2 * LANES, LANES)
    return jnp.concatenate(split_device(full), 1)


def solve_matrices(slab_map, slab_inverse):
    count = slab_inverse.shape[0]
    slots = jnp.arange(count, dtype=jnp.int32)
    holds = slab_map[:, None] == slots[None, :]
    below_of = jnp.concatenate([slab_map[:1] * 0 - 1, slab_map[:-1]])
    above_of = jnp.concatenate([slab_map[1:], slab_map[:1] * 0 - 1])
    below = jnp.sum(jnp.where(holds, below_of[:, None], 0), 0)
    above = jnp.sum(jnp.where(holds, above_of[:, None], 0), 0)
    lane = jnp.arange(LANES, dtype=jnp.int32)

    def one_hot(slot, position):
        where = (slot % 2 * SLAB + position + 2 * (slot // 2)) % LANES
        return ((slot >= 0)[:, None] & (where[:, None] == lane[None, :])).astype(jnp.float32)

    low_rim = one_hot(below, SLAB - 1)
    high_rim = one_hot(above, 0)
    rims = coupling * (
        low_rim[:, :, None] * slab_inverse[:, None, :, 0] + high_rim[:, :, None] * slab_inverse[:, None, :, SLAB - 1]
    )
    rims = rims.reshape(STRIPES, 2, LANES, SLAB).transpose(0, 2, 1, 3).reshape(STRIPES, LANES, LANES)
    same = jnp.eye(2, dtype=jnp.float32)
    turned = slab_inverse.transpose(0, 2, 1).reshape(STRIPES, 2, SLAB, SLAB)
    blocks = same[None, :, None, :, None] * turned[:, :, :, None, :]
    blocks = blocks.reshape(STRIPES, LANES, LANES)
    return jnp.concatenate(split_device(jnp.concatenate([blocks, rims], 1)), 2)


def call(kernel, inputs, outputs, scratch, scalars=0, cost=0, limit=VMEM_LIMIT, grid=None, in_specs=None, out_specs=None):
    whole = pl.BlockSpec(memory_space=pltpu.VMEM)
    if in_specs is None:
        in_specs = [pl.BlockSpec(memory_space=pltpu.SMEM)] * scalars + [whole] * (len(inputs) - scalars)
    if out_specs is None:
        out_specs = [whole] * len(outputs)
    extra = {} if grid is None else {"grid": grid}
    return pl.pallas_call(
        kernel,
        out_shape=[jax.ShapeDtypeStruct(shape, jnp.float32) for shape in outputs],
        in_specs=in_specs,
        out_specs=out_specs,
        scratch_shapes=scratch,
        compiler_params=pltpu.CompilerParams(vmem_limit_bytes=limit * MIB),
        cost_estimate=pl.CostEstimate(flops=cost, bytes_accessed=8 << 20, transcendentals=0),
        **extra,
    )(*inputs)


def vmem(*shape, dtype=jnp.float32):
    return pltpu.VMEM(shape, dtype)


def fixed(*shape):
    return pl.BlockSpec(shape, lambda i: (0,) * len(shape))


def local_halves(amplitudes, mode_table, slab_map, base_flow, base_coupling, slab_inverse, wall_operator):
    modes = amplitudes.shape[0]
    points = amplitudes.shape[3]
    groups = lax.axis_size("modes")
    index = lax.axis_index("modes")
    exchange = functools.partial(lax.all_to_all, axis_name="modes", split_axis=0, concat_axis=0, tiled=True)
    neighbours = [(j, j ^ 1) for j in range(groups)]
    stride = PARTS * STRIPES
    tiles = modes // TILE
    first_rows = modes // 2 * 3

    rows = amplitudes.transpose(0, 2, 1, 3).reshape(modes, 5, 2, STRIPES, LANES)
    rows = rows.transpose(0, 1, 3, 2, 4).reshape(modes, stride, LANES)
    positions = mode_table[:, 0] * NB + mode_table[:, 1]
    forward, backward = (jnp.asarray(matrix) for matrix in beta_matrices())
    table = jnp.asarray(omega_table())
    derivative = derivative_matrix(wall_operator, index % 2)
    solve = solve_matrices(slab_map, slab_inverse)
    beta_index = lax.dynamic_slice_in_dim(mode_table[:, 1], index * modes, modes)
    omega_index = lax.dynamic_slice_in_dim(mode_table[:, 0], index * modes, modes)
    signed = jnp.where(beta_index >= NB // 2, beta_index - NB, beta_index)
    wave = phase_gain * (2.0 * signed.astype(jnp.float32) / NB)
    frequency = omega_step * omega_index.astype(jnp.float32)
    wave = jnp.broadcast_to(wave[:, None], (modes, LANES))
    frequency = jnp.broadcast_to(frequency[:, None], (modes, LANES))
    couple = base_coupling.reshape(25 * STRIPES, LANES)

    in_hbm = pl.BlockSpec(memory_space=pltpu.HBM)
    anywhere = pl.BlockSpec(memory_space=pl.ANY)

    packs = modes // PACK_TILE

    def packed(first, with_last):
        places = 3 if with_last else 2
        (sent,) = call(
            functools.partial(pack, first, with_last),
            [rows],
            [(groups, places * modes // 2, LANES)],
            [
                vmem(packs, PACK_TILE, (5 if with_last else 2) * 2 * STRIPES, LANES),
                vmem(packs // 2, places, groups, PACK_TILE, LANES),
                pltpu.SemaphoreType.DMA((packs,)),
                pltpu.SemaphoreType.DMA((packs // 2, places)),
            ],
            cost=10**8,
            in_specs=[in_hbm],
            out_specs=[in_hbm],
        )
        return sent

    first = exchange(packed(2, False))
    sent_second = packed(0, True)
    sent_second, derivative, solve, wave, frequency, couple, positions = lax.optimization_barrier(
        (sent_second, derivative, solve, wave, frequency, couple, positions)
    )
    second = exchange(sent_second)

    grid = vmem(M, LANES)
    spectrum = vmem(NW, 2 * NB, LANES)
    folded = vmem(TIMES, NB, LANES)
    turned = vmem(groups, modes // 2, LANES)
    physical = (TIMES, NB, LANES)
    half_physical = (TIMES, NB // 2, LANES)
    scalars = pl.BlockSpec(memory_space=pltpu.SMEM)

    def spectral(kernel, received, count, place, outputs, scratch, cost):
        block = pl.BlockSpec((groups, count, LANES), lambda i: (0, place, 0))
        return call(
            kernel,
            [positions, received, forward, table],
            outputs,
            scratch,
            cost=cost,
            grid=(1,),
            in_specs=[scalars, block, fixed(*forward.shape), fixed(*table.shape)],
            out_specs=[fixed(*shape) for shape in outputs],
        )

    f1, g1, mean = spectral(
        functools.partial(synthesis, True), first, modes, 0, [physical, physical, (8, LANES)], [grid, spectrum], 2 * 10**9
    )
    s1 = lax.ppermute(f1, "modes", neighbours)
    (back_first,) = call(
        functools.partial(force_analysis, False),
        [positions, f1, f1, s1, g1, derivative, backward, table, mean],
        [(groups, modes + 8, LANES)],
        [folded, folded, grid],
        scalars=1,
        cost=2 * 10**9,
    )
    got_first = exchange(back_first)
    f2, g2 = spectral(
        functools.partial(synthesis, False), second, modes, 0, [physical, physical], [grid, spectrum], 2 * 10**9
    )
    s2 = lax.ppermute(f2, "modes", neighbours)
    f_last, g_last = spectral(
        synthesis_half, second, modes // 2, 2, [half_physical] * 2, [grid, spectrum, turned], 10**9
    )
    s2, f_last, g_last = lax.optimization_barrier((s2, f_last, g_last))
    s_last = lax.ppermute(f_last, "modes", neighbours)
    (back_second,) = call(
        functools.partial(force_analysis, True),
        [positions, f1, f2, s2, g2, derivative, backward, table, f_last, s_last, g_last],
        [(groups, first_rows, LANES)],
        [folded, folded, grid, turned],
        scalars=1,
        cost=3 * 10**9,
    )
    got_second = exchange(back_second)

    stacked = TILE * PARTS
    state = (tiles, STRIPES * PARTS + 1, TILE, LANES)
    state_spec = pl.BlockSpec((1,) + state[1:], lambda i: (i, 0, 0, 0))
    returned_spec = pl.BlockSpec((groups, TILE, LANES), lambda i: (0, i, 0))
    mean_spec = pl.BlockSpec((groups, 8, LANES), lambda i: (0, modes // 8, 0))
    mode_spec = pl.BlockSpec((TILE, LANES), lambda i: (i, 0))
    all_spec = pl.BlockSpec((TILE, stride, LANES), lambda i: (i, 0, 0))
    halves = [vmem(STRIPES, stacked, LANES, dtype=jnp.bfloat16)] * 2 + [vmem(stacked, LANES, dtype=jnp.bfloat16)] * 2
    shared_specs = [fixed(*couple.shape), mode_spec, mode_spec, fixed(*solve.shape)]
    shared = [couple, wave, frequency, solve]
    (iterate,) = call(
        relax_first,
        [rows, got_first, got_first, base_flow.reshape(STRIPES, LANES)] + shared,
        [state],
        [vmem(STRIPES * PARTS, TILE, LANES)] * 2 + [vmem(8, LANES)] + halves,
        cost=3 * 10**9,
        grid=(tiles,),
        in_specs=[all_spec, returned_spec, mean_spec, fixed(STRIPES, LANES)] + shared_specs,
        out_specs=[state_spec],
    )
    (out,) = call(
        relax_last,
        [iterate, got_second] + shared,
        [(modes, stride, LANES)],
        [
            vmem(*state),
            vmem(tiles, groups, TILE, LANES),
            vmem(tiles, groups, TILE, LANES),
            vmem(tiles, TILE, stride, LANES),
            vmem(*couple.shape),
            vmem(*wave.shape),
            vmem(*frequency.shape),
            vmem(*solve.shape, dtype=jnp.bfloat16),
            pltpu.SemaphoreType.DMA((3, tiles)),
            pltpu.SemaphoreType.DMA((tiles,)),
            pltpu.SemaphoreType.DMA((4,)),
            vmem(STRIPES, len(LATE), TILE, LANES),
            vmem(STRIPES * PARTS, TILE, LANES),
        ]
        + halves,
        cost=2 * 10**9,
        in_specs=[in_hbm, anywhere] + [in_hbm] * 4,
        out_specs=[in_hbm],
    )
    out = out.reshape(modes, 5, STRIPES, 2, LANES).transpose(0, 1, 3, 2, 4).reshape(modes, 5, 2, points)
    return out.transpose(0, 2, 1, 3)


def local_any(amplitudes, mode_table, slab_map, base_flow, base_coupling, slab_inverse, wall_operator):
    points = amplitudes.shape[3]
    fits = points == STRIPES * LANES and points // lax.axis_size("modes") == SHARE
    fits = fits and slab_inverse.shape == (2 * STRIPES, SLAB, SLAB) and amplitudes.shape[0] % (2 * ROWS) == 0
    chosen = local_halves if fits else local
    return chosen(amplitudes, mode_table, slab_map, base_flow, base_coupling, slab_inverse, wall_operator)


def solution(mesh):
    return jax.shard_map(
        local_any,
        mesh=mesh,
        in_specs=(
            P(("runs", "modes"), None, None, None),
            P(),
            P(),
            P("runs"),
            P("runs", None),
            P(),
            P(),
        ),
        out_specs=P(("runs", "modes"), None, None, None),
        check_vma=False,
    )
```

```python
import functools
import math

import jax
import jax.numpy as jnp
import numpy as np
from jax import lax
from jax.experimental import pallas as pl
from jax.experimental.pallas import tpu as pltpu
from jax.sharding import PartitionSpec as P

M = 4096
NB = 128
SWEEPS = 3
NW = 32


precise = lax.Precision.HIGHEST
omega_step = 0.01
phase_gain = 0.2
march_step = 0.2
coupling = 0.3


def twiddle(length):
    counter = jnp.arange(length, dtype=jnp.int32)
    product = counter[:, None] * counter[None, :] % length
    angles = product.astype(jnp.float32) * (2.0 * math.pi / length)
    return (jnp.cos(angles), jnp.sin(angles))


def mode_tables(mode_table):
    omega_index = mode_table[:, 0]
    beta_index = mode_table[:, 1]
    signed = jnp.where(beta_index >= NB // 2, beta_index - NB, beta_index)
    wavenum = 2.0 * signed.astype(jnp.float32) / NB
    frequency = omega_step * omega_index.astype(jnp.float32)
    grid_pos = omega_index * NB + beta_index
    mode_at = jnp.zeros((M,), jnp.int32).at[grid_pos].set(jnp.arange(M, dtype=jnp.int32))
    return (wavenum, frequency, grid_pos, mode_at)


def synthesize(real_part, imag_part, tables, factor):
    cos_omega, sin_omega, cos_beta, sin_beta = tables
    mixed_re = jnp.einsum("...wb,bz->...wz", real_part, cos_beta, precision=precise) - jnp.einsum(
        "...wb,bz->...wz", imag_part, sin_beta, precision=precise
    )
    mixed_im = jnp.einsum("...wb,bz->...wz", real_part, sin_beta, precision=precise) + jnp.einsum(
        "...wb,bz->...wz", imag_part, cos_beta, precision=precise
    )
    physical = jnp.einsum("...wz,wt->...tz", mixed_re, cos_omega, precision=precise) - jnp.einsum(
        "...wz,wt->...tz", mixed_im, sin_omega, precision=precise
    )
    return physical * factor


def analyze(physical, tables, factor):
    cos_omega, sin_omega, cos_beta, sin_beta = tables
    half_re = jnp.einsum("...tz,zb->...tb", physical, cos_beta, precision=precise)
    half_im = -jnp.einsum("...tz,zb->...tb", physical, sin_beta, precision=precise)
    coef_re = jnp.einsum("...tb,tw->...wb", half_re, cos_omega, precision=precise) + jnp.einsum(
        "...tb,tw->...wb", half_im, sin_omega, precision=precise
    )
    coef_im = jnp.einsum("...tb,tw->...wb", half_im, cos_omega, precision=precise) - jnp.einsum(
        "...tb,tw->...wb", half_re, sin_omega, precision=precise
    )
    return (coef_re * factor, coef_im * factor)


def forcing(normal_vel, spanwise_vel, wall_grad, span_grad, tables, factor):
    vel_v = synthesize(normal_vel[0], normal_vel[1], tables, factor)
    vel_w = synthesize(spanwise_vel[0], spanwise_vel[1], tables, factor)
    grad_y = synthesize(wall_grad[0], wall_grad[1], tables, factor)
    grad_z = synthesize(span_grad[0], span_grad[1], tables, factor)
    product = -(vel_v[None] * grad_y + vel_w[None] * grad_z)
    return analyze(product, tables, factor)


def wall_derivative(values, wall_operator):
    slab_width = wall_operator.shape[0]
    slab_count = values.shape[3] // slab_width
    blocks = values.reshape(values.shape[:3] + (slab_count, slab_width))
    return jnp.einsum("ij,abcsj->abcsi", wall_operator, blocks, precision=precise).reshape(
        values.shape
    )


def interface_table(slab_map, slab_count, slab_width):
    inverse = (
        jnp.zeros((slab_count,), jnp.int32)
        .at[slab_map]
        .set(jnp.arange(slab_count, dtype=jnp.int32))
    )
    position = jnp.arange(slab_count * slab_width, dtype=jnp.int32)
    slot_of = position // slab_width
    within = position % slab_width
    domain = inverse[slot_of]
    below = slab_map[jnp.maximum(domain - 1, 0)] * slab_width + (slab_width - 1)
    above = slab_map[jnp.minimum(domain + 1, slab_count - 1)] * slab_width
    lower_ok = (within == 0) & (domain > 0)
    upper_ok = (within == slab_width - 1) & (domain < slab_count - 1)
    source = jnp.where(lower_ok, below, jnp.where(upper_ok, above, 0))
    weight = (lower_ok | upper_ok).astype(jnp.float32)
    return (source, weight)


def relaxation(iterate, right_side, rotation, matrix, slab_inverse, source, weight):
    slab_count = slab_inverse.shape[0]
    slab_width = slab_inverse.shape[1]
    coupled = jnp.einsum("kjy,acjy->acky", matrix, iterate, precision=precise)
    applied = jnp.stack(
        [
            coupled[:, 0] - rotation[:, None, :] * iterate[:, 1],
            coupled[:, 1] + rotation[:, None, :] * iterate[:, 0],
        ],
        1,
    )
    rims = jnp.take(iterate, source, axis=3) * weight
    residual_in = right_side - applied + coupling * rims
    blocks = residual_in.reshape(iterate.shape[:3] + (slab_count, slab_width))
    return jnp.einsum("sij,acvsj->acvsi", slab_inverse, blocks, precision=precise).reshape(
        iterate.shape
    )


def local(amplitudes, mode_table, slab_map, base_flow, base_coupling, slab_inverse, wall_operator):
    local_modes = amplitudes.shape[0]
    wall_points = amplitudes.shape[3]
    groups = lax.axis_size("modes")
    point_share = wall_points // groups
    wavenum, frequency, grid_pos, mode_at = mode_tables(mode_table)
    first_mode = lax.axis_index("modes") * local_modes
    wave_local = lax.dynamic_slice_in_dim(wavenum, first_mode, local_modes)
    freq_local = lax.dynamic_slice_in_dim(frequency, first_mode, local_modes)
    tables = twiddle(NW) + twiddle(NB)
    factor = 1.0 / math.sqrt(M)
    source, weight = interface_table(slab_map, slab_inverse.shape[0], slab_inverse.shape[1])
    matrix = base_coupling.reshape(5, 5, wall_points)
    gradient = wall_derivative(amplitudes, wall_operator)
    span = jnp.stack(
        [
            -wave_local[:, None, None] * amplitudes[:, 1],
            wave_local[:, None, None] * amplitudes[:, 0],
        ],
        1,
    )
    fields = jnp.concatenate([amplitudes[:, :, 2:4], gradient, span], 2)
    field_count = fields.shape[2]
    channels = 2 * field_count
    outgoing = jnp.transpose(
        fields.reshape(local_modes, channels, groups, point_share), (1, 2, 3, 0)
    ).reshape(channels, groups, point_share * local_modes)
    incoming = lax.all_to_all(outgoing, "modes", split_axis=1, concat_axis=1, tiled=True)
    by_mode = jnp.transpose(
        incoming.reshape(channels, groups, point_share, local_modes), (0, 2, 1, 3)
    ).reshape(channels, point_share, M)
    gridded = by_mode[..., mode_at].reshape(2, field_count, point_share, NW, NB)
    normal_vel = gridded[:, 0]
    spanwise_vel = gridded[:, 1]
    wall_grad = gridded[:, 2:7]
    span_grad = gridded[:, 7:12]
    mean_crossflow = lax.all_gather(spanwise_vel[0, :, 0, 0], "modes", axis=0, tiled=True)
    coef_re, coef_im = forcing(normal_vel, spanwise_vel, wall_grad, span_grad, tables, factor)
    packed = jnp.stack([coef_re, coef_im], 0).reshape(10, point_share, M)[..., grid_pos]
    sendback = jnp.transpose(
        packed.reshape(10, point_share, groups, local_modes), (0, 2, 1, 3)
    ).reshape(10, groups, point_share * local_modes)
    returned = lax.all_to_all(sendback, "modes", split_axis=1, concat_axis=1, tiled=True)
    nonlinear = jnp.transpose(
        returned.reshape(10, groups, point_share, local_modes), (3, 0, 1, 2)
    ).reshape(local_modes, 2, 5, wall_points)
    crossflow = base_flow + mean_crossflow
    rotation = phase_gain * wave_local[:, None] * crossflow[None, :] - freq_local[:, None]
    right_side = amplitudes + march_step * nonlinear
    iterate = amplitudes
    for sweep_index in range(SWEEPS):
        iterate = relaxation(iterate, right_side, rotation, matrix, slab_inverse, source, weight)
    return iterate


LANES = 128
SHARE = 32
SLAB = 64
HALF = NW // 2
TIMES = HALF + 1
BLOCKS = LANES // SHARE
STRIPES = 4
PARTS = 10
TILE = 64
PACK_TILE = 32
MIB = 1024 * 1024
VMEM_LIMIT = 53


def roll(x, shift):
    return pltpu.roll(x, shift % LANES, x.ndim - 1)


def lane_index(shape):
    return lax.broadcasted_iota(jnp.int32, shape, len(shape) - 1)


def lane_masks(shape):
    lane = lane_index(shape)
    return (lane < 64, (lane & 32) == 0)


def real_sign(shape):
    return jnp.where(lane_index(shape) < 64, 1.0, -1.0).astype(jnp.float32)


def block_transpose(rows, low, even):
    r0, r1, r2, r3 = rows
    crossed = roll(jnp.where(low, r2, r0), 64)
    t0 = jnp.where(low, r0, crossed)
    t2 = jnp.where(low, crossed, r2)
    crossed = roll(jnp.where(low, r3, r1), 64)
    t1 = jnp.where(low, r1, crossed)
    t3 = jnp.where(low, crossed, r3)
    return (
        jnp.where(even, t0, roll(t1, 32)),
        jnp.where(even, roll(t0, 96), t1),
        jnp.where(even, t2, roll(t3, 32)),
        jnp.where(even, roll(t2, 96), t3),
    )


def split(x):
    high = x.astype(jnp.bfloat16)
    return high, (x - high.astype(jnp.float32)).astype(jnp.bfloat16)


def dot(a, b):
    return jnp.dot(a, b, preferred_element_type=jnp.float32)


def cosine_sine(inputs, length, table, sign, real):
    if length == 4:
        first, middle, last = inputs
        middle_re = middle * real
        total = first + last
        return [total + middle_re, (first - last) + (middle - middle_re), total - middle_re]
    step = NW // length
    quarter = length // 4
    even = cosine_sine(inputs[0::2], length // 2, table, sign, real)
    odd_inputs = [(a, inputs[a]) for a in range(1, length // 2, 2)]
    odd = []
    for t in range(quarter + 1):
        if t == 0:
            total = odd_inputs[0][1]
            for _, value in odd_inputs[1:]:
                total = total + value
            odd.append(total * real)
        elif t == quarter:
            total = odd_inputs[0][1]
            for a, value in odd_inputs[1:]:
                total = total + value if a % 4 == 1 else total - value
            odd.append(total - total * real)
        else:
            total = None
            for a, value in odd_inputs:
                term = table(a * t * step % NW) * value
                total = term if total is None else total + term
            odd.append(total)
    out = [None] * (length // 2 + 1)
    for t in range(quarter + 1):
        out[t] = even[t] + odd[t]
        out[length // 2 - t] = sign * (even[t] - odd[t])
    out[quarter] = even[quarter] + odd[quarter]
    return out


def spread(ref, offset):
    flat = ref.reshape(ref.shape[0] * ref.shape[1], LANES)
    return flat[pl.ds(offset, ref.shape[0], stride=ref.shape[1]), :]


def pack_pair(first, first_offset, second, second_offset, low, even):
    out = []
    for stripe in range(STRIPES):
        rows = []
        for part in range(2):
            rows.append(spread(first, first_offset + stripe * 2 + part))
            rows.append(spread(second, second_offset + stripe * 2 + part))
        out.extend(block_transpose(rows, low, even))
    return out


def pack(first, with_last, rows_ref, o_ref, in_ref, out_ref, in_sem, out_sem):
    tiles = in_ref.shape[0]
    count = in_ref.shape[1]
    wanted = pl.ds(first * 2 * STRIPES, in_ref.shape[2])
    low, even = lane_masks((count, LANES))
    loads = []
    for tile in range(tiles):
        source = rows_ref.at[pl.ds(tile * count, count), wanted, :]
        loads.append(pltpu.make_async_copy(source, in_ref.at[tile], in_sem.at[tile]))
    half = tiles // 2
    for tile in range(half):
        loads[tile].start()
        loads[tile + half].start()
    stores = []
    for tile in range(half):
        loads[tile].wait()
        loads[tile + half].wait()
        near = in_ref.at[tile]
        far = in_ref.at[tile + half]
        pieces = [(near, 0, near, 2 * STRIPES), (far, 0, far, 2 * STRIPES)]
        if with_last:
            pieces.append((near, 8 * STRIPES, far, 8 * STRIPES))
        for place, piece in enumerate(pieces):
            for group, value in enumerate(pack_pair(*piece, low, even)):
                out_ref[tile, place, group] = value
            target = o_ref.at[:, pl.ds((place * half + tile) * count, count), :]
            store = pltpu.make_async_copy(out_ref.at[tile, place], target, out_sem.at[tile, place])
            store.start()
            stores.append(store)
    for store in stores:
        store.wait()


ROWS = 128


def loop(count, unroll, body):
    def step(i, carry):
        for j in range(unroll):
            body(i * unroll + j)
        return carry

    lax.fori_loop(0, count // unroll, step, 0)
    for i in range(count // unroll * unroll, count):
        body(i)


def lanes_constants():
    sign = real_sign((8, LANES))
    real = jnp.where(lane_index((8, LANES)) < 64, 1.0, 0.0).astype(jnp.float32)
    even = (lane_index((8, LANES)) & 32) == 0
    return sign, real, even


def pair_left(even, near, far):
    return jnp.where(even, near, roll(far, 32))


def pair_right(even, near, far):
    return jnp.where(even, roll(near, 96), far)


def scatter(pos_ref, grid_ref, cell, source, group, row):
    for j in range(ROWS):
        grid_ref[pl.ds(pos_ref[cell + j], 1), :] = source[group, pl.ds(row + j, 1), :]


def synthesis_beta(w_ref, first, second):
    wide_sign = real_sign((NB, LANES))
    columns = [jnp.concatenate([x, -wide_sign * roll(x, 64)], 0) for x in (first, second)]
    high, low_part = split(jnp.concatenate(columns, 1))
    product = dot(w_ref[...], high)
    out = product[: 2 * NB] + product[2 * NB :] + dot(w_ref[pl.ds(0, 2 * NB), :], low_part)
    return out[:, :LANES], out[:, LANES:]


def synthesis(with_mean, pos_ref, r_ref, w_ref, tab_ref, *refs):
    if with_mean:
        f_ref, g_ref, mean_ref, grid_ref, spec_ref = refs
    else:
        f_ref, g_ref, grid_ref, spec_ref = refs
    groups = r_ref.shape[0]
    modes = M // groups
    sign, real, _ = lanes_constants()

    def table(j):
        return tab_ref[j]

    def grid(a):
        return grid_ref[pl.ds(pl.multiple_of(a * NB, NB), NB), :]

    def both_halves(i):
        group = i // (modes // ROWS)
        start = pl.multiple_of(i % (modes // ROWS) * ROWS, ROWS)
        scatter(pos_ref, grid_ref, i * ROWS, r_ref, group, start)

    loop(groups * (modes // ROWS), 1, both_halves)
    if with_mean:
        mean_ref[...] = grid_ref[pl.ds(0, 8), :]

    def beta(i):
        spec_ref[2 * i], spec_ref[2 * i + 1] = synthesis_beta(w_ref, grid(2 * i), grid(2 * i + 1))

    loop(NW // 2, 2, beta)

    def omega(out_ref, shift):
        def body(i):
            rows = pl.ds(pl.multiple_of(i * 8, 8), 8)
            source = pl.ds(pl.multiple_of(shift + i * 8, 8), 8)
            inputs = [spec_ref[0, source, :] * real]
            for a in range(1, HALF):
                inputs.append(spec_ref[a, source, :] + sign * spec_ref[NW - a, source, :])
            inputs.append(spec_ref[HALF, source, :] * real)
            for t, value in enumerate(cosine_sine(inputs, NW, table, sign, real)):
                out_ref[t, rows, :] = value - sign * roll(value, 64)

        loop(NB // 8, 2, body)

    omega(f_ref, 0)
    omega(g_ref, NB)


def synthesis_half(pos_ref, r_ref, w_ref, tab_ref, f_ref, g_ref, grid_ref, spec_ref, turned_ref):
    groups = r_ref.shape[0]
    modes = M // groups
    sign, real, even = lanes_constants()
    wide_even = (lane_index((NB, LANES)) & 32) == 0

    def table(j):
        return tab_ref[j]

    def grid(a):
        return grid_ref[pl.ds(pl.multiple_of(a * NB, NB), NB), :]

    def turn(group):
        turned_ref[group] = roll(r_ref[group], 96)
        for block in range(modes // 2 // ROWS):
            cell = group * modes + block * ROWS
            scatter(pos_ref, grid_ref, cell, r_ref, group, block * ROWS)
            scatter(pos_ref, grid_ref, cell + modes // 2, turned_ref, group, block * ROWS)

    loop(groups, 1, turn)

    def beta(i):
        columns = [pair_left(wide_even, grid(a), grid(a + HALF)) for a in (2 * i, 2 * i + 1)]
        spec_ref[2 * i], spec_ref[2 * i + 1] = synthesis_beta(w_ref, *columns)

    loop(HALF // 2, 2, beta)

    def omega(out_ref, shift):
        def body(i):
            rows = pl.ds(pl.multiple_of(i * 8, 8), 8)
            near = pl.ds(pl.multiple_of(shift + i * 8, 8), 8)
            far = pl.ds(pl.multiple_of(shift + NB // 2 + i * 8, 8), 8)
            firsts = []
            seconds = []
            for a in range(HALF):
                pieces = (even, spec_ref[a, near, :], spec_ref[a, far, :])
                firsts.append(pair_left(*pieces))
                seconds.append(pair_right(*pieces))
            inputs = [firsts[0] * real]
            for a in range(1, HALF):
                inputs.append(firsts[a] + sign * seconds[HALF - a])
            inputs.append(seconds[0] * real)
            for t, value in enumerate(cosine_sine(inputs, NW, table, sign, real)):
                out_ref[t, rows, :] = value - sign * roll(value, 64)

        loop(NB // 16, 2, body)

    omega(f_ref, 0)
    omega(g_ref, NB)


def force_analysis(with_last, pos_ref, vw_ref, f_ref, s_ref, g_ref, d_ref, w_ref, tab_ref, *refs):
    if with_last:
        f_last_ref, s_last_ref, g_last_ref, o_ref, k_ref, r_ref, n_ref, turned_ref = refs
    else:
        mean_ref, o_ref, k_ref, r_ref, n_ref = refs
    groups = o_ref.shape[0]
    modes = M // groups
    sign, real, _ = lanes_constants()
    wide_sign = real_sign((NB, LANES))
    wide_real, wide_even = lane_masks((NB, LANES))
    half_rows = NB // 2

    def table(j):
        return tab_ref[j]

    def gather(group, mode, target, row):
        for j in range(ROWS):
            cell = pos_ref[group * modes + mode + j]
            target[group, pl.ds(row + j, 1), :] = n_ref[pl.ds(cell, 1), :]

    def force_of(t, rows, v, w, f, s, g):
        high, low_part = split(jnp.concatenate([f, s], 1))
        both = dot(high, d_ref[...])
        grad = both[:, :LANES] + both[:, LANES:] + dot(low_part, d_ref[:, :LANES])
        force = v * grad + w * g
        if t is None:
            return jnp.where(wide_real[:rows], force, 0.0)
        return force + wide_sign[:rows] * roll(force, 64)

    def full_product(t, alone=False):
        vw = vw_ref[t]
        v = pair_left(wide_even, vw, vw)
        w = pair_right(wide_even, vw, vw)
        k_ref[t] = force_of(None if alone else t, NB, v, w, f_ref[t], s_ref[t], g_ref[t])

    def products(product):
        product(0, True)
        product(HALF, True)
        loop(HALF - 1, 3, lambda i: product(i + 1))

    def omegas(tiles):
        def body(i):
            rows = pl.ds(pl.multiple_of(i * 8, 8), 8)
            inputs = [k_ref[t, rows, :] for t in range(TIMES)]
            for a, value in enumerate(cosine_sine(inputs, NW, table, sign, real)):
                r_ref[a, rows, :] = value

        loop(tiles, 2, body)

    def beta(columns):
        high, low_part = split(jnp.concatenate(columns, 1) if len(columns) > 1 else columns[0])
        both = dot(w_ref[...], high)
        out = both[: 2 * NB] + both[2 * NB :] + dot(w_ref[pl.ds(0, 2 * NB), :], low_part)
        result = []
        for j in range(len(columns)):
            cosine = out[:NB, j * LANES : (j + 1) * LANES]
            sine = roll(out[NB:, j * LANES : (j + 1) * LANES], 64)
            result.append((cosine + wide_sign * sine, wide_sign * cosine - sine))
        return result

    def store(a, plus, minus):
        mirror = (NW - a) % NW
        n_ref[pl.ds(pl.multiple_of(mirror * NB, NB), NB), :] = minus
        n_ref[pl.ds(pl.multiple_of(a * NB, NB), NB), :] = plus

    products(full_product)
    omegas(NB // 8)

    def full_beta(i):
        for j, (plus, minus) in enumerate(beta([r_ref[2 * i], r_ref[2 * i + 1]])):
            store(2 * i + j, plus, minus)

    loop(HALF // 2, 2, full_beta)
    store(HALF, *beta([r_ref[HALF]])[0])

    def both_halves(i):
        group = i // (modes // ROWS)
        start = pl.multiple_of(i % (modes // ROWS) * ROWS, ROWS)
        gather(group, start, o_ref, start)

    loop(groups * (modes // ROWS), 1, both_halves)
    if not with_last:
        for group in range(groups):
            o_ref[group, pl.ds(modes, 8), :] = mean_ref[...]
        return

    def half_product(t, alone=False):
        vw = vw_ref[t]
        near = vw[:half_rows]
        far = vw[half_rows:]
        v = pair_left(wide_even[:half_rows], near, far)
        w = pair_right(wide_even[:half_rows], near, far)
        k_ref[t, pl.ds(0, half_rows), :] = force_of(
            None if alone else t, half_rows, v, w, f_last_ref[t], s_last_ref[t], g_last_ref[t]
        )

    products(half_product)
    omegas(NB // 16)

    def half_columns(a):
        even = wide_even[:half_rows]
        pieces = (even, r_ref[a, pl.ds(0, half_rows), :], r_ref[a + 1, pl.ds(0, half_rows), :])
        return jnp.concatenate([pair_left(*pieces), pair_right(*pieces)], 0)

    def half_beta(i):
        for j, (plus, minus) in enumerate(beta([half_columns(4 * i), half_columns(4 * i + 2)])):
            a = 4 * i + 2 * j
            store(a, plus, minus)
            store(a + 1, roll(plus, 96), roll(minus, 96))

    loop(HALF // 4, 1, half_beta)
    last = r_ref[HALF, pl.ds(0, half_rows), :]
    store(HALF, *beta([jnp.concatenate([last, roll(last, 96)], 0)])[0])

    def turn(group):
        for block in range(modes // 2 // ROWS):
            gather(group, block * ROWS, o_ref, modes + block * ROWS)
            gather(group, modes // 2 + block * ROWS, turned_ref, block * ROWS)
        here = pl.ds(modes, modes // 2)
        near = o_ref[group, here, :]
        o_ref[group, here, :] = pair_left((lane_index(near.shape) & 32) == 0, near, turned_ref[group])

    loop(groups, 1, turn)


def find_rims(x_of, parts, zh_ref, zl_ref):
    lane = lane_index((TILE, LANES))
    edges = []
    for stripe in range(STRIPES):
        place = (lane - 2 * stripe) & (SLAB - 1)
        edges.append((place == 0) | (place == SLAB - 1))
    for part in range(PARTS):
        rows = pl.ds(part * TILE, TILE)
        if part not in parts:
            zh_ref[rows, :] = zl_ref[rows, :] = jnp.zeros((TILE, LANES), jnp.bfloat16)
            continue
        rims = x_of(0, part)
        for stripe in range(1, STRIPES):
            rims = jnp.where(edges[stripe], roll(x_of(stripe, part), 2 * stripe), rims)
        zh_ref[rows, :], zl_ref[rows, :] = split(rims)


def three_pass(high, low_part, weights):
    both = dot(high, weights)
    return both[:, :LANES] + both[:, LANES:] + dot(low_part, weights[:, :LANES])


def relax(stripe, x_of, parts, cross, kz_ref, om_ref, coup_ref, sw_ref, rh_ref, rl_ref, zh_ref, zl_ref):
    values = {part: x_of(stripe, part) for part in parts}
    rotation = kz_ref[...] * cross - om_ref[...]
    outs = []
    for k in range(5):
        out_re = jnp.zeros((TILE, LANES), jnp.float32)
        out_im = out_re
        if 2 * k in values:
            out_re = rotation * values[2 * k + 1]
            out_im = -(rotation * values[2 * k])
        for j in range(5):
            if 2 * j not in values:
                continue
            weight = coup_ref[pl.ds((k * 5 + j) * STRIPES + stripe, 1), :]
            out_re = out_re - weight * values[2 * j]
            out_im = out_im - weight * values[2 * j + 1]
        outs += [split(out_re), split(out_im)]
    high = jnp.concatenate([jnp.concatenate([out[0] for out in outs], 0), zh_ref[...]], 1)
    low_rows = jnp.concatenate([jnp.concatenate([out[1] for out in outs], 0), zl_ref[...]], 1)
    return three_pass(high, low_rows, sw_ref[stripe]).reshape(PARTS, TILE, LANES)


def relax_first(a_ref, b_ref, mean_ref, base_ref, coup_ref, kz_ref, om_ref, sw_ref, out_ref, right_ref, x_ref, cf_ref, *halves):
    rh_ref, rl_ref, zh_ref, zl_ref = halves
    low, even = lane_masks((TILE, LANES))
    block_of = lane_index((1, LANES)) // SHARE
    for stripe in range(STRIPES):
        total = base_ref[pl.ds(stripe, 1), :]
        for block in range(BLOCKS):
            row = mean_ref[stripe * BLOCKS + block, pl.ds(0, 1), :]
            total = total + jnp.where(block_of == block, roll(row, SHARE * (block - 1)), 0.0)
        cf_ref[pl.ds(stripe, 1), :] = total
    out_ref[0, STRIPES * PARTS, pl.ds(0, 8), :] = cf_ref[...]

    for stripe in range(STRIPES):
        groups = [stripe * BLOCKS + block for block in range(BLOCKS)]
        velocity = block_transpose([b_ref[group] for group in groups], low, even)
        gained = {4: velocity[0], 6: velocity[1], 5: velocity[2], 7: velocity[3]}
        for part in range(PARTS):
            value = spread(a_ref, part // 2 * 2 * STRIPES + stripe * 2 + part % 2)
            x_ref[stripe * PARTS + part] = value
            if part in gained:
                value = value + march_step * gained[part]
            rows = pl.ds(part * TILE, TILE)
            rh_ref[stripe, rows, :], rl_ref[stripe, rows, :] = split(value)
        solved = three_pass(rh_ref[stripe], rl_ref[stripe], sw_ref[stripe, pl.ds(0, LANES), :])
        right_ref[pl.ds(stripe * PARTS, PARTS)] = solved.reshape(PARTS, TILE, LANES)

    def x_of(stripe, part):
        return x_ref[stripe * PARTS + part]

    for sweep in range(SWEEPS):
        find_rims(x_of, range(PARTS), zh_ref, zl_ref)
        for stripe in range(STRIPES):
            here = pl.ds(stripe * PARTS, PARTS)
            cross = cf_ref[pl.ds(stripe, 1), :]
            new = relax(stripe, x_of, range(PARTS), cross, kz_ref, om_ref, coup_ref, sw_ref, *halves)
            if sweep < SWEEPS - 1:
                x_ref[here] = right_ref[here] + new
            else:
                out_ref[0, here] = right_ref[here] + new


LATE = (0, 1, 2, 3, 8, 9)


def relax_last(first_hbm, b_any, *refs):
    shared_hbm, o_hbm, (first_buf, b_buf, t_buf, o_buf), shared = refs[:4], refs[4], refs[5:9], refs[9:13]
    (in_sem, out_sem, shared_sem), scratch = refs[13:16], refs[16:]
    coup_ref, kz_ref, om_ref, sw_ref = shared
    tiles = first_buf.shape[0]
    modes = tiles * TILE

    def loads(i):
        pair = b_any.at[:, pl.ds(i * TILE, TILE), :]
        last = b_any.at[:, pl.ds(modes + i % (tiles // 2) * TILE, TILE), :]
        return (
            pltpu.make_async_copy(pair, b_buf.at[i], in_sem.at[0, i]),
            pltpu.make_async_copy(last, t_buf.at[i], in_sem.at[1, i]),
            pltpu.make_async_copy(first_hbm.at[i], first_buf.at[i], in_sem.at[2, i]),
        )

    def store(i):
        target = o_hbm.at[pl.ds(i * TILE, TILE), :, :]
        return pltpu.make_async_copy(o_buf.at[i], target, out_sem.at[i])

    ahead = 2
    fixed_loads = [
        pltpu.make_async_copy(source, target, shared_sem.at[place])
        for place, (source, target) in enumerate(zip(shared_hbm, shared))
    ]
    for load in fixed_loads:
        load.start()
    for i in range(ahead):
        for load in loads(i):
            load.start()
    for load in fixed_loads:
        load.wait()

    def body(i, carry):
        for load in loads(i):
            load.wait()

        @pl.when(i + ahead < tiles)
        def _():
            for load in loads(i + ahead):
                load.start()

        modes_here = pl.ds(pl.multiple_of(i * TILE, TILE), TILE)
        relax_tile(
            i >= tiles // 2,
            first_buf.at[i],
            b_buf.at[i],
            t_buf.at[i],
            first_buf.at[i, STRIPES * PARTS],
            coup_ref,
            kz_ref.at[modes_here, :],
            om_ref.at[modes_here, :],
            sw_ref,
            o_buf.at[i],
            *scratch,
        )
        store(i).start()
        return carry

    lax.fori_loop(0, tiles, body, 0)
    for i in range(tiles):
        store(i).wait()


def relax_tile(far, first_ref, b_ref, t_ref, cf_ref, coup_ref, kz_ref, om_ref, sw_ref, o_ref, right_ref, x_ref, *halves):
    rh_ref, rl_ref, zh_ref, zl_ref = halves
    low, even = lane_masks((TILE, LANES))
    count = len(LATE)
    for stripe in range(STRIPES):
        groups = [stripe * BLOCKS + block for block in range(BLOCKS)]
        pair = block_transpose([b_ref[group] for group in groups], low, even)
        last = block_transpose([t_ref[group] for group in groups], low, even)
        last = (jnp.where(far, last[1], last[0]), jnp.where(far, last[3], last[2]))
        late = jnp.concatenate((pair[0], pair[2], pair[1], pair[3]) + last, 0)
        weights = sw_ref[stripe, pl.ds(0, LANES), :]
        added = three_pass(*split(march_step * late), weights)
        right_ref[stripe] = added.reshape(count, TILE, LANES)

    def right_of(stripe, part):
        return right_ref[stripe, LATE.index(part)]

    def x_of(stripe, part):
        return x_ref[stripe * PARTS + part]

    flat = o_ref.reshape(TILE * PARTS * STRIPES, LANES)
    for sweep in range(1, SWEEPS):
        source, parts = (right_of, LATE) if sweep == 1 else (x_of, range(PARTS))
        find_rims(source, parts, zh_ref, zl_ref)
        for stripe in range(STRIPES):
            cross = cf_ref[pl.ds(stripe, 1), :]
            new = relax(stripe, source, parts, cross, kz_ref, om_ref, coup_ref, sw_ref, *halves)
            for part in range(PARTS):
                value = new[part] + right_of(stripe, part) if part in LATE else new[part]
                if sweep < SWEEPS - 1:
                    x_ref[stripe * PARTS + part] = value
                    continue
                offset = part // 2 * 2 * STRIPES + stripe * 2 + part % 2
                value = value + first_ref[stripe * PARTS + part]
                flat[pl.ds(offset, TILE, stride=PARTS * STRIPES), :] = value


def split_host(x):
    high = x.astype(jnp.bfloat16)
    low_part = (x - high.astype(np.float64)).astype(jnp.bfloat16)
    return high, low_part


def beta_matrices():
    index = np.arange(NB)
    angles = (index[:, None] * index[None, :] % NB) * (2.0 * math.pi / NB)
    cosine = np.cos(angles)
    sine = np.sin(angles)
    wave = 2.0 * np.where(index >= NB // 2, index - NB, index) / NB
    factor = 1.0 / math.sqrt(M)
    forward = factor * np.block([[cosine, sine], [-sine * wave, cosine * wave]])
    backward = -factor * np.concatenate([cosine, sine], 0)
    return tuple(np.concatenate(split_host(matrix), 0) for matrix in (forward, backward))


def omega_table():
    angles = np.arange(NW) * (2.0 * math.pi / NW)
    rows = np.concatenate([np.repeat(np.cos(angles)[:, None], 64, 1), np.repeat(np.sin(angles)[:, None], 64, 1)], 1)
    return np.repeat(rows[:, None, :], 8, 1).astype(np.float32)


def split_device(x):
    high = lax.reduce_precision(x, 8, 7)
    return high.astype(jnp.bfloat16), (x - high).astype(jnp.bfloat16)


def derivative_matrix(wall_operator, half):
    own = lax.dynamic_slice(wall_operator, (half * SHARE, 0), (SHARE, SLAB)).T
    mine = lax.dynamic_slice(own, (half * SHARE, 0), (SHARE, SHARE))
    other = lax.dynamic_slice(own, ((1 - half) * SHARE, 0), (SHARE, SHARE))
    same = jnp.eye(BLOCKS, dtype=jnp.float32)
    stacked = jnp.stack([mine, other], 0)
    full = same[None, :, None, :, None] * stacked[:, None, :, None, :]
    full = full.reshape(2 * LANES, LANES)
    return jnp.concatenate(split_device(full), 1)


def solve_matrices(slab_map, slab_inverse):
    count = slab_inverse.shape[0]
    slots = jnp.arange(count, dtype=jnp.int32)
    holds = slab_map[:, None] == slots[None, :]
    below_of = jnp.concatenate([slab_map[:1] * 0 - 1, slab_map[:-1]])
    above_of = jnp.concatenate([slab_map[1:], slab_map[:1] * 0 - 1])
    below = jnp.sum(jnp.where(holds, below_of[:, None], 0), 0)
    above = jnp.sum(jnp.where(holds, above_of[:, None], 0), 0)
    lane = jnp.arange(LANES, dtype=jnp.int32)

    def one_hot(slot, position):
        where = (slot % 2 * SLAB + position + 2 * (slot // 2)) % LANES
        return ((slot >= 0)[:, None] & (where[:, None] == lane[None, :])).astype(jnp.float32)

    low_rim = one_hot(below, SLAB - 1)
    high_rim = one_hot(above, 0)
    rims = coupling * (
        low_rim[:, :, None] * slab_inverse[:, None, :, 0] + high_rim[:, :, None] * slab_inverse[:, None, :, SLAB - 1]
    )
    rims = rims.reshape(STRIPES, 2, LANES, SLAB).transpose(0, 2, 1, 3).reshape(STRIPES, LANES, LANES)
    same = jnp.eye(2, dtype=jnp.float32)
    turned = slab_inverse.transpose(0, 2, 1).reshape(STRIPES, 2, SLAB, SLAB)
    blocks = same[None, :, None, :, None] * turned[:, :, :, None, :]
    blocks = blocks.reshape(STRIPES, LANES, LANES)
    return jnp.concatenate(split_device(jnp.concatenate([blocks, rims], 1)), 2)


def call(kernel, inputs, outputs, scratch, scalars=0, cost=0, limit=VMEM_LIMIT, grid=None, in_specs=None, out_specs=None):
    whole = pl.BlockSpec(memory_space=pltpu.VMEM)
    if in_specs is None:
        in_specs = [pl.BlockSpec(memory_space=pltpu.SMEM)] * scalars + [whole] * (len(inputs) - scalars)
    if out_specs is None:
        out_specs = [whole] * len(outputs)
    extra = {} if grid is None else {"grid": grid}
    return pl.pallas_call(
        kernel,
        out_shape=[jax.ShapeDtypeStruct(shape, jnp.float32) for shape in outputs],
        in_specs=in_specs,
        out_specs=out_specs,
        scratch_shapes=scratch,
        compiler_params=pltpu.CompilerParams(vmem_limit_bytes=limit * MIB),
        cost_estimate=pl.CostEstimate(flops=cost, bytes_accessed=8 << 20, transcendentals=0),
        **extra,
    )(*inputs)


def vmem(*shape, dtype=jnp.float32):
    return pltpu.VMEM(shape, dtype)


def fixed(*shape):
    return pl.BlockSpec(shape, lambda i: (0,) * len(shape))


def local_halves(amplitudes, mode_table, slab_map, base_flow, base_coupling, slab_inverse, wall_operator):
    modes = amplitudes.shape[0]
    points = amplitudes.shape[3]
    groups = lax.axis_size("modes")
    index = lax.axis_index("modes")
    exchange = functools.partial(lax.all_to_all, axis_name="modes", split_axis=0, concat_axis=0, tiled=True)
    neighbours = [(j, j ^ 1) for j in range(groups)]
    stride = PARTS * STRIPES
    tiles = modes // TILE
    first_rows = modes // 2 * 3

    rows = amplitudes.transpose(0, 2, 1, 3).reshape(modes, 5, 2, STRIPES, LANES)
    rows = rows.transpose(0, 1, 3, 2, 4).reshape(modes, stride, LANES)
    positions = mode_table[:, 0] * NB + mode_table[:, 1]
    forward, backward = (jnp.asarray(matrix) for matrix in beta_matrices())
    table = jnp.asarray(omega_table())
    derivative = derivative_matrix(wall_operator, index % 2)
    solve = solve_matrices(slab_map, slab_inverse)
    beta_index = lax.dynamic_slice_in_dim(mode_table[:, 1], index * modes, modes)
    omega_index = lax.dynamic_slice_in_dim(mode_table[:, 0], index * modes, modes)
    signed = jnp.where(beta_index >= NB // 2, beta_index - NB, beta_index)
    wave = phase_gain * (2.0 * signed.astype(jnp.float32) / NB)
    frequency = omega_step * omega_index.astype(jnp.float32)
    wave = jnp.broadcast_to(wave[:, None], (modes, LANES))
    frequency = jnp.broadcast_to(frequency[:, None], (modes, LANES))
    couple = base_coupling.reshape(25 * STRIPES, LANES)

    in_hbm = pl.BlockSpec(memory_space=pltpu.HBM)
    anywhere = pl.BlockSpec(memory_space=pl.ANY)

    packs = modes // PACK_TILE

    def packed(first, with_last):
        places = 3 if with_last else 2
        (sent,) = call(
            functools.partial(pack, first, with_last),
            [rows],
            [(groups, places * modes // 2, LANES)],
            [
                vmem(packs, PACK_TILE, (5 if with_last else 2) * 2 * STRIPES, LANES),
                vmem(packs // 2, places, groups, PACK_TILE, LANES),
                pltpu.SemaphoreType.DMA((packs,)),
                pltpu.SemaphoreType.DMA((packs // 2, places)),
            ],
            cost=10**8,
            in_specs=[in_hbm],
            out_specs=[in_hbm],
        )
        return sent

    first = exchange(packed(2, False))
    sent_second = packed(0, True)
    sent_second, derivative, solve, wave, frequency, couple, positions = lax.optimization_barrier(
        (sent_second, derivative, solve, wave, frequency, couple, positions)
    )
    second = exchange(sent_second)

    grid = vmem(M, LANES)
    spectrum = vmem(NW, 2 * NB, LANES)
    folded = vmem(TIMES, NB, LANES)
    turned = vmem(groups, modes // 2, LANES)
    physical = (TIMES, NB, LANES)
    half_physical = (TIMES, NB // 2, LANES)
    scalars = pl.BlockSpec(memory_space=pltpu.SMEM)

    def spectral(kernel, received, count, place, outputs, scratch, cost):
        block = pl.BlockSpec((groups, count, LANES), lambda i: (0, place, 0))
        return call(
            kernel,
            [positions, received, forward, table],
            outputs,
            scratch,
            cost=cost,
            grid=(1,),
            in_specs=[scalars, block, fixed(*forward.shape), fixed(*table.shape)],
            out_specs=[fixed(*shape) for shape in outputs],
        )

    f1, g1, mean = spectral(
        functools.partial(synthesis, True), first, modes, 0, [physical, physical, (8, LANES)], [grid, spectrum], 2 * 10**9
    )
    s1 = lax.ppermute(f1, "modes", neighbours)
    (back_first,) = call(
        functools.partial(force_analysis, False),
        [positions, f1, f1, s1, g1, derivative, backward, table, mean],
        [(groups, modes + 8, LANES)],
        [folded, folded, grid],
        scalars=1,
        cost=2 * 10**9,
    )
    got_first = exchange(back_first)
    f2, g2 = spectral(
        functools.partial(synthesis, False), second, modes, 0, [physical, physical], [grid, spectrum], 2 * 10**9
    )
    s2 = lax.ppermute(f2, "modes", neighbours)
    f_last, g_last = spectral(
        synthesis_half, second, modes // 2, 2, [half_physical] * 2, [grid, spectrum, turned], 10**9
    )
    s2, f_last, g_last = lax.optimization_barrier((s2, f_last, g_last))
    s_last = lax.ppermute(f_last, "modes", neighbours)
    (back_second,) = call(
        functools.partial(force_analysis, True),
        [positions, f1, f2, s2, g2, derivative, backward, table, f_last, s_last, g_last],
        [(groups, first_rows, LANES)],
        [folded, folded, grid, turned],
        scalars=1,
        cost=3 * 10**9,
    )
    got_second = exchange(back_second)

    stacked = TILE * PARTS
    state = (tiles, STRIPES * PARTS + 1, TILE, LANES)
    state_spec = pl.BlockSpec((1,) + state[1:], lambda i: (i, 0, 0, 0))
    returned_spec = pl.BlockSpec((groups, TILE, LANES), lambda i: (0, i, 0))
    mean_spec = pl.BlockSpec((groups, 8, LANES), lambda i: (0, modes // 8, 0))
    mode_spec = pl.BlockSpec((TILE, LANES), lambda i: (i, 0))
    all_spec = pl.BlockSpec((TILE, stride, LANES), lambda i: (i, 0, 0))
    halves = [vmem(STRIPES, stacked, LANES, dtype=jnp.bfloat16)] * 2 + [vmem(stacked, LANES, dtype=jnp.bfloat16)] * 2
    shared_specs = [fixed(*couple.shape), mode_spec, mode_spec, fixed(*solve.shape)]
    shared = [couple, wave, frequency, solve]
    (iterate,) = call(
        relax_first,
        [rows, got_first, got_first, base_flow.reshape(STRIPES, LANES)] + shared,
        [state],
        [vmem(STRIPES * PARTS, TILE, LANES)] * 2 + [vmem(8, LANES)] + halves,
        cost=3 * 10**9,
        grid=(tiles,),
        in_specs=[all_spec, returned_spec, mean_spec, fixed(STRIPES, LANES)] + shared_specs,
        out_specs=[state_spec],
    )
    (out,) = call(
        relax_last,
        [iterate, got_second] + shared,
        [(modes, stride, LANES)],
        [
            vmem(*state),
            vmem(tiles, groups, TILE, LANES),
            vmem(tiles, groups, TILE, LANES),
            vmem(tiles, TILE, stride, LANES),
            vmem(*couple.shape),
            vmem(*wave.shape),
            vmem(*frequency.shape),
            vmem(*solve.shape, dtype=jnp.bfloat16),
            pltpu.SemaphoreType.DMA((3, tiles)),
            pltpu.SemaphoreType.DMA((tiles,)),
            pltpu.SemaphoreType.DMA((4,)),
            vmem(STRIPES, len(LATE), TILE, LANES),
            vmem(STRIPES * PARTS, TILE, LANES),
        ]
        + halves,
        cost=2 * 10**9,
        in_specs=[in_hbm, anywhere] + [in_hbm] * 4,
        out_specs=[in_hbm],
    )
    out = out.reshape(modes, 5, STRIPES, 2, LANES).transpose(0, 1, 3, 2, 4).reshape(modes, 5, 2, points)
    return out.transpose(0, 2, 1, 3)


def local_any(amplitudes, mode_table, slab_map, base_flow, base_coupling, slab_inverse, wall_operator):
    points = amplitudes.shape[3]
    fits = points == STRIPES * LANES and points // lax.axis_size("modes") == SHARE
    fits = fits and slab_inverse.shape == (2 * STRIPES, SLAB, SLAB) and amplitudes.shape[0] % (2 * ROWS) == 0
    chosen = local_halves if fits else local
    return chosen(amplitudes, mode_table, slab_map, base_flow, base_coupling, slab_inverse, wall_operator)


def solution(mesh):
    return jax.shard_map(
        local_any,
        mesh=mesh,
        in_specs=(
            P(("runs", "modes"), None, None, None),
            P(),
            P(),
            P("runs"),
            P("runs", None),
            P(),
            P(),
        ),
        out_specs=P(("runs", "modes"), None, None, None),
        check_vma=False,
    )
```
